32 devices in a mesh: mem: 4 (over y, core), gy: 4 (over z), gx: 2 (over x).
Axes of the slice: x: 2, y: 2, z: 4, core: 2. Of those that a mesh axis runs over, the one named last changes fastest.
Arguments:
- fields: float32 [20, 2, 256, 256], P('mem', None, 'gy', 'gx'), parts along dimension 0, may hold values from -6.5 to 6.5
- wind_x: float32 [8], P('mem'), parts along dimension 0, may hold values from -0.71 to 0.71
- wind_y: float32 [8], P('mem'), parts along dimension 0, may hold values from -0.71 to 0.71
- coupling: float32 [2, 5, 5], replicated, may hold values from -0.15 to 0.035
- north: bfloat16 [20, 2, 8, 256], P('mem'), parts along dimension 0, may hold values from -6 to 6
- south: bfloat16 [20, 2, 8, 256], P('mem'), parts along dimension 0, may hold values from -6 to 6
- west: bfloat16 [20, 2, 256, 8], P('mem'), parts along dimension 0, may hold values from -6 to 6
- east: bfloat16 [20, 2, 256, 8], P('mem'), parts along dimension 0, may hold values from -6 to 6
- strip_scale: float32 [16, 5, 2], P('mem'), parts along dimension 0, may hold values from 0.5 to 2
- widths: int32 [4], replicated, may hold values from 2 to 8, as said below
Outputs:
- advanced: float32 [20, 2, 256, 256], P('mem', None, 'gy', 'gx'), parts along dimension 0
The draws below stay inside these ranges and needn't reach their ends.
There are 4 independent parts, one for each index of `mem`. The reference program is written for one: setup_inputs(seed, part) draws one part's arguments, and reference() takes and returns one part's arrays. A program takes and returns all parts, laid end to end along the dimension named above; an argument that names none is the same for every part. Nothing has to cross between parts.
Inputs may be any that keep to these rules, and one draw needn't show every extreme that they name: One of the four widths equals 8 in every draw.
All inputs are finite; a program needn't handle non-finite values.
Results may differ from the reference program's by a relative error of at most 0.0003.
Values sent between devices are 32-bit elements; how exact they have to be, the bound alone decides.
No kernel may reach another device: no remote copies, remote signals or barrier semaphores. Data moves between devices by JAX's collectives and lax.ppermute only.
A program may use at most 64 MiB of HBM per device.

```python
import math
import jax
import jax.numpy as jnp
from jax import lax

NFIELD = 5
LEV = 2
BW = 8
NY = 256
NX = 256


def draw_widths(key, part):
    first_key, second_key = jax.random.split(jax.random.fold_in(key, 17))
    drawn = jax.random.randint(first_key, (4,), 2, BW + 1)
    chosen = jax.random.randint(second_key, (), 0, 4)
    return jnp.where(jnp.arange(4) == chosen, BW, drawn).astype(jnp.int32)


def draw_fields(key, part):
    amp_key, noise_key = jax.random.split(jax.random.fold_in(key, 31))
    amplitude = jnp.exp(jax.random.uniform(amp_key, (NFIELD, LEV), jnp.float32, jnp.log(4.0), jnp.log(6.0)))
    noise = jnp.clip(0.12 * jax.random.normal(noise_key, (NFIELD, LEV, NY, NX), jnp.float32), -0.5, 0.5)
    rows_index = jnp.arange(NY, dtype=jnp.int32)
    cols_index = jnp.arange(NX, dtype=jnp.int32)
    parity = (rows_index[:, None] + cols_index[None, :]) % 2
    checker = 1.0 - 2.0 * parity.astype(jnp.float32)
    return (amplitude[:, :, None, None] * checker[None, None, :, :] + noise).astype(jnp.float32)


def wind_levels(key, salt):
    size_key, sign_key = jax.random.split(jax.random.fold_in(key, salt))
    uniform_part = jax.random.uniform(size_key, (LEV,), jnp.float32)
    magnitude = 0.67 + 0.04 * uniform_part
    signs = 2.0 * jax.random.randint(sign_key, (LEV,), 0, 2).astype(jnp.float32) - 1.0
    return (signs * magnitude).astype(jnp.float32)


def draw_wind_x(key, part):
    return wind_levels(key, 41)


def draw_wind_y(key, part):
    return wind_levels(key, 43)


def draw_coupling(key, part):
    diag_key, off_key = jax.random.split(jax.random.fold_in(key, 53))
    uniform_part = jax.random.uniform(diag_key, (LEV, NFIELD), jnp.float32)
    diagonal = -(0.09 + 0.06 * uniform_part)
    off_part = jnp.clip(0.01 * jax.random.normal(off_key, (LEV, NFIELD, NFIELD), jnp.float32), -0.035, 0.035)
    identity = jnp.eye(NFIELD, dtype=jnp.float32)
    return (off_part * (1.0 - identity)[None, :, :] + identity[None, :, :] * diagonal[:, :, None]).astype(jnp.float32)


def gaussian(stream_key, dims, scale, most, kind=jnp.bfloat16):
    values = scale * jax.random.normal(stream_key, dims, jnp.float32)
    return jnp.clip(values, min=-most, max=most).astype(kind)


def setup_inputs(seed: int = 0, part: int = 0) -> dict:
    splits = jax.random.split(jax.random.key(seed), 11)
    part_splits = jax.random.split(jax.random.fold_in(splits[10], part), 11)
    return {
        "fields": draw_fields(jax.random.fold_in(jax.random.fold_in(splits[10], part), 71), part),
        "wind_x": draw_wind_x(jax.random.fold_in(jax.random.fold_in(splits[10], part), 71), part),
        "wind_y": draw_wind_y(jax.random.fold_in(jax.random.fold_in(splits[10], part), 71), part),
        "coupling": draw_coupling(jax.random.fold_in(splits[10], 71), part),
        "north": gaussian(part_splits[4], (NFIELD, LEV, BW, NX), 1.0, 6.0),
        "south": gaussian(part_splits[5], (NFIELD, LEV, BW, NX), 1.0, 6.0),
        "west": gaussian(part_splits[6], (NFIELD, LEV, NY, BW), 1.0, 6.0),
        "east": gaussian(part_splits[7], (NFIELD, LEV, NY, BW), 1.0, 6.0),
        "strip_scale": jnp.clip(jnp.exp(jax.random.uniform(part_splits[8], (4, NFIELD, LEV), jnp.float32, math.log(0.5), math.log(2.0))), 0.5, 2.0),
        "widths": draw_widths(jax.random.fold_in(splits[10], 71), part),
    }


RELAX = 0.25


def profile(distance, width):
    dist_float = distance.astype(jnp.float32)
    return jnp.where((dist_float >= 0.0) & (dist_float < width), jnp.square((width - dist_float) / width), 0.0)


def strip_values(strip, rows, cols, scale_side):
    picked = jnp.take(jnp.take(strip, rows, axis=2), cols, axis=3)
    return picked.astype(jnp.float32) * scale_side[:, :, None, None]


def relax_terms(north, south, west, east, strip_scale, widths, rows_global, cols_global):
    strip_width = north.shape[2]
    total_cols = north.shape[3]
    total_rows = west.shape[2]
    width_float = widths.astype(jnp.float32)
    cols_clip = jnp.clip(cols_global, 0, total_cols - 1).astype(jnp.int32)
    rows_clip = jnp.clip(rows_global, 0, total_rows - 1).astype(jnp.int32)
    north_weight = profile(rows_global, width_float[0])
    south_weight = profile(total_rows - 1 - rows_global, width_float[1])
    west_weight = profile(cols_global, width_float[2])
    east_weight = profile(total_cols - 1 - cols_global, width_float[3])
    north_rows = jnp.clip(rows_global, 0, strip_width - 1).astype(jnp.int32)
    south_rows = jnp.clip(rows_global - (total_rows - strip_width), 0, strip_width - 1).astype(jnp.int32)
    west_cols = jnp.clip(cols_global, 0, strip_width - 1).astype(jnp.int32)
    east_cols = jnp.clip(cols_global - (total_cols - strip_width), 0, strip_width - 1).astype(jnp.int32)
    weight_sum = north_weight[:, None] + south_weight[:, None] + west_weight[None, :] + east_weight[None, :]
    driver_sum = north_weight[:, None] * strip_values(north, north_rows, cols_clip, strip_scale[0])
    driver_sum = driver_sum + south_weight[:, None] * strip_values(south, south_rows, cols_clip, strip_scale[1])
    driver_sum = driver_sum + west_weight[None, :] * strip_values(west, rows_clip, west_cols, strip_scale[2])
    driver_sum = driver_sum + east_weight[None, :] * strip_values(east, rows_clip, east_cols, strip_scale[3])
    return weight_sum, driver_sum


def divergence(values, wind, axis):
    count = values.shape[axis] - 5

    def shifted(offset):
        return lax.slice_in_dim(values, offset, offset + count, axis=axis)

    centered = 37.0 * (shifted(3) + shifted(2)) - 8.0 * (shifted(4) + shifted(1)) + (shifted(5) + shifted(0))
    damping = 10.0 * (shifted(3) - shifted(2)) - 5.0 * (shifted(4) - shifted(1)) + (shifted(5) - shifted(0))
    flux = (wind * centered - jnp.abs(wind) * damping) / 60.0
    return lax.slice_in_dim(flux, 1, count, axis=axis) - lax.slice_in_dim(flux, 0, count - 1, axis=axis)


def tendency(padded_x, padded_y, wind_x, wind_y, coupling, weight_sum, driver_sum):
    center = padded_x[:, :, :, 3:-3]
    advection = divergence(padded_x, wind_x[None, :, None, None], 3) + divergence(padded_y, wind_y[None, :, None, None], 2)
    mixing = jnp.einsum("lfg,glyx->flyx", coupling, center, precision=lax.Precision.HIGHEST)
    return mixing - advection - RELAX * (weight_sum * center - driver_sum)


def reference(fields, wind_x, wind_y, coupling, north, south, west, east, strip_scale, widths):
    rows_global = jnp.arange(fields.shape[2], dtype=jnp.int32)
    cols_global = jnp.arange(fields.shape[3], dtype=jnp.int32)
    weight_sum, driver_sum = relax_terms(north, south, west, east, strip_scale, widths, rows_global, cols_global)

    def full_tendency(state):
        padded = jnp.pad(state, ((0, 0), (0, 0), (3, 3), (3, 3)))
        return tendency(padded[:, :, 3:-3, :], padded[:, :, :, 3:-3], wind_x, wind_y, coupling, weight_sum, driver_sum)

    section_one = fields + full_tendency(fields) / 3.0
    section_two = fields + full_tendency(section_one) / 2.0
    return fields + full_tendency(section_two)
```

```python
import functools

import jax
import jax.numpy as jnp
import numpy as np
from jax import lax
from jax.experimental import pallas as pl
from jax.experimental.pallas import tpu as pltpu
from jax.sharding import PartitionSpec as P

RELAX = 0.25
REACH = 3
HALO = 3 * REACH
PAD = 16
LANES = 128

UPWIND = (-2.0, 15.0, -60.0, 20.0, 30.0, -3.0, 0.0)
CENTRAL = (-1.0, 9.0, -45.0, 0.0, 45.0, -9.0, 1.0)
DAMPING = (1.0, -6.0, 15.0, -20.0, 15.0, -6.0, 1.0)


def band_matrices(width):
    bands = np.zeros((2, width, width), np.float32)
    for offset in range(-REACH, REACH + 1):
        for col in range(width):
            row = (col + offset) % width
            bands[0, row, col] = UPWIND[offset + REACH]
            bands[1, row, col] = -UPWIND[REACH - offset]
    return bands


def iota(shape, dim):
    return lax.broadcasted_iota(jnp.int32, shape, dim)


def edge_weight(distance, width):
    dist = distance.astype(jnp.float32)
    inside = (dist >= 0.0) & (dist < width)
    return jnp.where(inside, jnp.square((width - dist) / width), 0.0)


def pack_y_kernel(fields, to_north, to_south):
    count_f, count_l, rows, _ = fields.shape
    for f in range(count_f):
        for l in range(count_l):
            base = HALO * (f * count_l + l)
            to_north[base : base + HALO, :] = fields[f, l, 0:HALO, :]
            to_south[base : base + HALO, :] = fields[f, l, rows - HALO : rows, :]


def pack_x_kernel(gx_count, fields, from_north, from_south, *rest):
    outs, ext = rest[:-1], rest[-1]
    count_f, count_l, rows, cols = fields.shape
    ext_rows = ext.shape[0]
    lane = iota((ext_rows, LANES), 1)
    col_east, col_west = cols - HALO, 0
    if gx_count == 2:
        starts = [jnp.where(lax.axis_index("gx") == 0, col_east, col_west)]
    else:
        starts = [col_east, col_west]
    packed = [jnp.zeros((ext_rows, LANES), jnp.float32) for _ in starts]
    ext[...] = jnp.zeros_like(ext)
    for f in range(count_f):
        for l in range(count_l):
            slot = HALO * (f * count_l + l)
            ext[PAD - HALO : PAD, 0:cols] = from_north[slot : slot + HALO, :]
            ext[PAD : PAD + rows, 0:cols] = fields[f, l]
            ext[PAD + rows : PAD + rows + HALO, 0:cols] = from_south[slot : slot + HALO, :]
            whole = ext[...]
            for n, start in enumerate(starts):
                shift = lax.rem(slot + LANES - start, LANES)
                moved = pltpu.roll(whole, shift, 1)
                packed[n] = jnp.where((lane >= slot) & (lane < slot + HALO), moved, packed[n])
    for out, value in zip(outs, packed):
        out[...] = value


def step_kernel(
    grid_sizes,
    gx_recv,
    fields,
    from_north,
    from_south,
    *rest,
):
    gy_count, gx_count = grid_sizes
    side = rest[:gx_recv]
    (
        wind_x,
        wind_y,
        coupling,
        north,
        south,
        west,
        east,
        scale,
        widths,
        bands,
        out,
        q0,
        q1,
        q2,
        drive,
        relax,
        inside,
        xdiv,
    ) = rest[gx_recv:]
    count_f, count_l, rows, cols = fields.shape
    tiles, _, _, ext_rows, _ = q0.shape
    span = tiles * LANES
    last = tiles - 1
    strip = north.shape[2]
    total_rows, total_cols = rows * gy_count, cols * gx_count
    gy, gx = lax.axis_index("gy"), lax.axis_index("gx")
    row_start, col_start = gy * rows, gx * cols

    q0[...] = jnp.zeros_like(q0)
    lane = iota((ext_rows, LANES), 1)
    for f in range(count_f):
        for l in range(count_l):
            slot = HALO * (f * count_l + l)
            q0[0, f, l, PAD - HALO : PAD, 0:cols] = from_north[slot : slot + HALO, :]
            q0[0, f, l, PAD : PAD + rows, 0:cols] = fields[f, l]
            q0[0, f, l, PAD + rows : PAD + rows + HALO, 0:cols] = from_south[slot : slot + HALO, :]
            east_lane, west_lane = cols % LANES, LANES - HALO
            if gx_recv == 1:
                target = jnp.where(gx == 0, east_lane, west_lane)
                placed = [(side[0], target)]
            else:
                placed = [(side[0], west_lane), (side[1], east_lane)]
            merged = q0[last, f, l]
            for source, target in placed:
                moved = pltpu.roll(source[...], lax.rem(target + LANES - slot, LANES), 1)
                merged = jnp.where((lane >= target) & (lane < target + HALO), moved, merged)
            q0[last, f, l] = merged

    width = [widths[s].astype(jnp.float32) for s in range(4)]
    row_global = iota((ext_rows, LANES), 0) + (row_start - PAD)
    row_weight = edge_weight(row_global, width[0]) + edge_weight(
        total_rows - 1 - row_global, width[1]
    )
    row_inside = (row_global >= 0) & (row_global < total_rows)
    for t in range(tiles):
        pos = lane + t * LANES
        col_global = jnp.where(pos >= span - HALO, pos - span, pos) + col_start
        col_weight = edge_weight(col_global, width[2]) + edge_weight(
            total_cols - 1 - col_global, width[3]
        )
        relax[t] = RELAX * (row_weight + col_weight)
        inside[t] = jnp.where(
            row_inside & (col_global >= 0) & (col_global < total_cols), 1.0, 0.0
        )

    drive[...] = jnp.zeros_like(drive)
    pos = iota((strip, LANES), 1)
    depth = iota((strip, LANES), 0)
    pick = jnp.concatenate([pos == depth, pos == depth + (cols - strip)], axis=0).astype(
        jnp.float32
    ).astype(jnp.bfloat16)
    lane8 = iota((8, LANES), 1)
    west_weight = RELAX * edge_weight(lane8 + col_start, width[2])
    east_weight = RELAX * edge_weight(total_cols - 1 - (lane8 + col_start), width[3])
    west_weight = jnp.where(lane8 < strip, west_weight, 0.0)
    east_weight = jnp.where((lane8 >= cols - strip) & (lane8 < cols), east_weight, 0.0)
    shift = lax.rem(PAD + total_rows - row_start, total_rows)
    for f in range(count_f):
        for l in range(count_l):
            both = jnp.concatenate([west[f, l], east[f, l]], axis=0).astype(jnp.float32)
            both = pltpu.roll(both, shift, 1)[:, 0:LANES].astype(jnp.bfloat16)
            raw = lax.dot_general(
                both, pick, (((0,), (0,)), ((), ())), preferred_element_type=jnp.float32
            )
            factor = west_weight * scale[2, l, f] + east_weight * scale[3, l, f]
            drive[0, f, l] = raw[0:ext_rows] * factor[0:1, :]

    shift = lax.rem(total_cols - col_start, total_cols)
    strip_lane = iota((strip, LANES), 1)
    strip_row = iota((strip, LANES), 0)
    for source, side_id, at, here in (
        (north, 0, PAD, gy == 0),
        (south, 1, PAD + rows - strip, gy == gy_count - 1),
    ):

        @pl.when(here)
        def _(source=source, side_id=side_id, at=at):
            distance = strip_row if side_id == 0 else strip - 1 - strip_row
            weight = RELAX * edge_weight(distance, width[side_id])
            for f in range(count_f):
                for l in range(count_l):
                    values = pltpu.roll(source[f, l].astype(jnp.float32), shift, 1)
                    factor = weight * scale[side_id, l, f]
                    for t in range(tiles):
                        part = values[:, t * LANES : (t + 1) * LANES]
                        if t == last:
                            wrapped = values[:, total_cols - LANES : total_cols]
                            part = jnp.where(strip_lane >= LANES - HALO, wrapped, part)
                        old = drive[t, f, l, at : at + strip, :]
                        drive[t, f, l, at : at + strip, :] = old + factor * part

    def section(src, base, dst, fac, first, groups, out_tiles):
        for l in range(count_l):
            c_x, c_y = wind_x[l], wind_y[l]
            band = bands[jnp.where(c_x < 0.0, 1, 0)]
            height = groups * 8
            flat = [
                src[t, :, l, first : first + height, :].reshape(count_f * height, LANES)
                for t in range(tiles)
            ]
            state = jnp.concatenate(flat, axis=1) if tiles > 1 else flat[0]
            high = state.astype(jnp.bfloat16)
            low = (state - high.astype(jnp.float32)).astype(jnp.bfloat16)
            band = band[:, 0 : out_tiles * LANES]
            moved = jnp.dot(high, band, preferred_element_type=jnp.float32) + jnp.dot(
                low, band, preferred_element_type=jnp.float32
            )
            for t in range(out_tiles):
                xdiv[t, :, 0:height, :] = moved[:, t * LANES : (t + 1) * LANES].reshape(
                    count_f, height, LANES
                )
            scaled_y, scaled_abs = fac / 60.0 * c_y, fac / 60.0 * jnp.abs(c_y)
            scaled_x = fac / 60.0 * c_x
            taps = [
                scaled_abs * DAMPING[k] - scaled_y * CENTRAL[k] for k in range(2 * REACH + 1)
            ]
            mix = [
                [
                    fac * coupling[f, l, g] + (taps[REACH] if f == g else 0.0)
                    for g in range(count_f)
                ]
                for f in range(count_f)
            ]

            def group(n, _):
                at = pl.multiple_of(first + n * 8, 8)
                local = pl.multiple_of(n * 8, 8)
                for t in range(out_tiles):
                    center = [src[t, g, l, pl.ds(at, 8), :] for g in range(count_f)]
                    weight = relax[t, pl.ds(at, 8), :]
                    for f in range(count_f):
                        rate = drive[t, f, l, pl.ds(at, 8), :] - weight * center[f]
                        total = fac * rate - scaled_x * xdiv[t, f, pl.ds(local, 8), :]
                        for g in range(count_f):
                            total = total + mix[f][g] * center[g]
                        for k in range(2 * REACH + 1):
                            if k != REACH:
                                total = total + taps[k] * src[
                                    t, f, l, pl.ds(at + (k - REACH), 8), :
                                ]
                        value = base[t, f, l, pl.ds(at, 8), :] + total
                        if dst is out:
                            out[f, l, pl.ds(local, 8), :] = value[:, 0:cols]
                        else:
                            dst[t, f, l, pl.ds(at, 8), :] = value * inside[t, pl.ds(at, 8), :]
                return 0

            lax.fori_loop(0, groups, group, 0)

    wide = (rows + 16) // 8
    q1[...] = jnp.zeros_like(q1)
    q2[...] = jnp.zeros_like(q2)
    section(q0, q0, q1, 1.0 / 3.0, PAD - 8, wide, tiles)
    section(q1, q0, q2, 0.5, PAD - 8, wide, tiles)
    section(q2, q0, out, 1.0, PAD, rows // 8, 1)


def swap_rounds(count):
    forward = [(i, i + 1) for i in range(count - 1)]
    return forward, [(b, a) for a, b in forward]


def local(gy_count, gx_count, fields, wind_x, wind_y, coupling, north, south, west, east, strip_scale, widths):
    count_f, count_l, rows, cols = fields.shape
    ext_rows = rows + 2 * PAD
    tiles = 1 if cols + 2 * HALO <= LANES else 2
    packed_rows = -(-HALO * count_f * count_l // 8) * 8
    vmem = pl.BlockSpec(memory_space=pltpu.VMEM)
    smem = pl.BlockSpec(memory_space=pltpu.SMEM)

    strip_shape = jax.ShapeDtypeStruct((packed_rows, cols), jnp.float32)
    to_north, to_south = pl.pallas_call(
        pack_y_kernel,
        out_shape=(strip_shape, strip_shape),
        in_specs=[vmem],
        out_specs=(vmem, vmem),
        name="pack_y",
    )(fields)
    forward, backward = swap_rounds(gy_count)
    from_north = lax.ppermute(to_south, "gy", forward)
    from_south = lax.ppermute(to_north, "gy", backward)

    recv_count = 1 if gx_count == 2 else 2
    side_shape = jax.ShapeDtypeStruct((ext_rows, LANES), jnp.float32)
    sent = pl.pallas_call(
        functools.partial(pack_x_kernel, gx_count),
        out_shape=(side_shape,) * recv_count,
        in_specs=[vmem] * 3,
        out_specs=(vmem,) * recv_count,
        scratch_shapes=[pltpu.VMEM((ext_rows, LANES), jnp.float32)],
        name="pack_x",
    )(fields, from_north, from_south)
    forward, backward = swap_rounds(gx_count)
    if recv_count == 1:
        side = [lax.ppermute(sent[0], "gx", forward + backward)]
    else:
        side = [lax.ppermute(sent[0], "gx", forward), lax.ppermute(sent[1], "gx", backward)]

    state = pltpu.VMEM((tiles, count_f, count_l, ext_rows, LANES), jnp.float32)
    plane = pltpu.VMEM((tiles, ext_rows, LANES), jnp.float32)
    bands = jnp.asarray(band_matrices(tiles * LANES), jnp.bfloat16)
    return pl.pallas_call(
        functools.partial(step_kernel, (gy_count, gx_count), recv_count),
        out_shape=jax.ShapeDtypeStruct(fields.shape, jnp.float32),
        in_specs=[vmem] * (3 + recv_count) + [smem] * 3 + [vmem] * 4 + [smem] * 2 + [vmem],
        out_specs=vmem,
        scratch_shapes=[
            state,
            state,
            state,
            state,
            plane,
            plane,
            pltpu.VMEM((tiles, count_f, rows + 16, LANES), jnp.float32),
        ],
        name="three_sections",
    )(
        fields,
        from_north,
        from_south,
        *side,
        wind_x,
        wind_y,
        jnp.transpose(coupling, (1, 0, 2)),
        north,
        south,
        jnp.swapaxes(west, 2, 3),
        jnp.swapaxes(east, 2, 3),
        jnp.transpose(strip_scale, (0, 2, 1)),
        widths,
        bands,
    )


def solution(mesh):
    return jax.shard_map(
        functools.partial(local, mesh.shape["gy"], mesh.shape["gx"]),
        mesh=mesh,
        in_specs=(
            P("mem", None, "gy", "gx"),
            P("mem"),
            P("mem"),
            P(),
            P("mem", None, None, None),
            P("mem", None, None, None),
            P("mem", None, None, None),
            P("mem", None, None, None),
            P("mem", None, None),
            P(),
        ),
        out_specs=P("mem", None, "gy", "gx"),
        check_vma=False,
    )
```

```python
import functools

import jax
import jax.numpy as jnp
import numpy as np
from jax import lax
from jax.experimental import pallas as pl
from jax.experimental.pallas import tpu as pltpu
from jax.sharding import PartitionSpec as P

RELAX = 0.25
REACH = 3
HALO = 3 * REACH
PAD = 16
LANES = 128

UPWIND = (-2.0, 15.0, -60.0, 20.0, 30.0, -3.0, 0.0)
CENTRAL = (-1.0, 9.0, -45.0, 0.0, 45.0, -9.0, 1.0)
DAMPING = (1.0, -6.0, 15.0, -20.0, 15.0, -6.0, 1.0)


def band_matrices(width):
    bands = np.zeros((2, width, width), np.float32)
    for offset in range(-REACH, REACH + 1):
        for col in range(width):
            row = (col + offset) % width
            bands[0, row, col] = UPWIND[offset + REACH]
            bands[1, row, col] = -UPWIND[REACH - offset]
    return bands


def iota(shape, dim):
    return lax.broadcasted_iota(jnp.int32, shape, dim)


def edge_weight(distance, width):
    dist = distance.astype(jnp.float32)
    inside = (dist >= 0.0) & (dist < width)
    return jnp.where(inside, jnp.square((width - dist) / width), 0.0)


def pack_y_kernel(fields, to_north, to_south):
    count_f, count_l, rows, _ = fields.shape
    for f in range(count_f):
        for l in range(count_l):
            base = HALO * (f * count_l + l)
            to_north[base : base + HALO, :] = fields[f, l, 0:HALO, :]
            to_south[base : base + HALO, :] = fields[f, l, rows - HALO : rows, :]


def pack_x_kernel(gx_count, fields, from_north, from_south, *rest):
    outs, ext = rest[:-1], rest[-1]
    count_f, count_l, rows, cols = fields.shape
    ext_rows = ext.shape[0]
    lane = iota((ext_rows, LANES), 1)
    col_east, col_west = cols - HALO, 0
    if gx_count == 2:
        starts = [jnp.where(lax.axis_index("gx") == 0, col_east, col_west)]
    else:
        starts = [col_east, col_west]
    packed = [jnp.zeros((ext_rows, LANES), jnp.float32) for _ in starts]
    ext[...] = jnp.zeros_like(ext)
    for f in range(count_f):
        for l in range(count_l):
            slot = HALO * (f * count_l + l)
            ext[PAD - HALO : PAD, 0:cols] = from_north[slot : slot + HALO, :]
            ext[PAD : PAD + rows, 0:cols] = fields[f, l]
            ext[PAD + rows : PAD + rows + HALO, 0:cols] = from_south[slot : slot + HALO, :]
            whole = ext[...]
            for n, start in enumerate(starts):
                shift = lax.rem(slot + LANES - start, LANES)
                moved = pltpu.roll(whole, shift, 1)
                packed[n] = jnp.where((lane >= slot) & (lane < slot + HALO), moved, packed[n])
    for out, value in zip(outs, packed):
        out[...] = value


def step_kernel(
    grid_sizes,
    gx_recv,
    fields,
    from_north,
    from_south,
    *rest,
):
    gy_count, gx_count = grid_sizes
    side = rest[:gx_recv]
    (
        wind_x,
        wind_y,
        coupling,
        north,
        south,
        west,
        east,
        scale,
        widths,
        bands,
        out,
        q0,
        q1,
        q2,
        drive,
        relax,
        inside,
        xdiv,
    ) = rest[gx_recv:]
    count_f, count_l, rows, cols = fields.shape
    tiles, _, _, ext_rows, _ = q0.shape
    span = tiles * LANES
    last = tiles - 1
    strip = north.shape[2]
    total_rows, total_cols = rows * gy_count, cols * gx_count
    gy, gx = lax.axis_index("gy"), lax.axis_index("gx")
    row_start, col_start = gy * rows, gx * cols

    q0[...] = jnp.zeros_like(q0)
    lane = iota((ext_rows, LANES), 1)
    for f in range(count_f):
        for l in range(count_l):
            slot = HALO * (f * count_l + l)
            q0[0, f, l, PAD - HALO : PAD, 0:cols] = from_north[slot : slot + HALO, :]
            q0[0, f, l, PAD : PAD + rows, 0:cols] = fields[f, l]
            q0[0, f, l, PAD + rows : PAD + rows + HALO, 0:cols] = from_south[slot : slot + HALO, :]
            east_lane, west_lane = cols % LANES, LANES - HALO
            if gx_recv == 1:
                target = jnp.where(gx == 0, east_lane, west_lane)
                placed = [(side[0], target)]
            else:
                placed = [(side[0], west_lane), (side[1], east_lane)]
            merged = q0[last, f, l]
            for source, target in placed:
                moved = pltpu.roll(source[...], lax.rem(target + LANES - slot, LANES), 1)
                merged = jnp.where((lane >= target) & (lane < target + HALO), moved, merged)
            q0[last, f, l] = merged

    width = [widths[s].astype(jnp.float32) for s in range(4)]
    row_global = iota((ext_rows, LANES), 0) + (row_start - PAD)
    row_weight = edge_weight(row_global, width[0]) + edge_weight(
        total_rows - 1 - row_global, width[1]
    )
    row_inside = (row_global >= 0) & (row_global < total_rows)
    for t in range(tiles):
        pos = lane + t * LANES
        col_global = jnp.where(pos >= span - HALO, pos - span, pos) + col_start
        col_weight = edge_weight(col_global, width[2]) + edge_weight(
            total_cols - 1 - col_global, width[3]
        )
        relax[t] = RELAX * (row_weight + col_weight)
        inside[t] = jnp.where(
            row_inside & (col_global >= 0) & (col_global < total_cols), 1.0, 0.0
        )

    drive[...] = jnp.zeros_like(drive)
    pos = iota((strip, LANES), 1)
    depth = iota((strip, LANES), 0)
    pick = jnp.concatenate([pos == depth, pos == depth + (cols - strip)], axis=0).astype(
        jnp.float32
    ).astype(jnp.bfloat16)
    lane8 = iota((8, LANES), 1)
    west_weight = RELAX * edge_weight(lane8 + col_start, width[2])
    east_weight = RELAX * edge_weight(total_cols - 1 - (lane8 + col_start), width[3])
    west_weight = jnp.where(lane8 < strip, west_weight, 0.0)
    east_weight = jnp.where((lane8 >= cols - strip) & (lane8 < cols), east_weight, 0.0)
    shift = lax.rem(PAD + total_rows - row_start, total_rows)
    for f in range(count_f):
        for l in range(count_l):
            both = jnp.concatenate([west[f, l], east[f, l]], axis=0).astype(jnp.float32)
            both = pltpu.roll(both, shift, 1)[:, 0:LANES].astype(jnp.bfloat16)
            raw = lax.dot_general(
                both, pick, (((0,), (0,)), ((), ())), preferred_element_type=jnp.float32
            )
            factor = west_weight * scale[2, l, f] + east_weight * scale[3, l, f]
            drive[0, f, l] = raw[0:ext_rows] * factor[0:1, :]

    shift = lax.rem(total_cols - col_start, total_cols)
    strip_lane = iota((strip, LANES), 1)
    strip_row = iota((strip, LANES), 0)
    for source, side_id, at, here in (
        (north, 0, PAD, gy == 0),
        (south, 1, PAD + rows - strip, gy == gy_count - 1),
    ):

        @pl.when(here)
        def _(source=source, side_id=side_id, at=at):
            distance = strip_row if side_id == 0 else strip - 1 - strip_row
            weight = RELAX * edge_weight(distance, width[side_id])
            for f in range(count_f):
                for l in range(count_l):
                    values = pltpu.roll(source[f, l].astype(jnp.float32), shift, 1)
                    factor = weight * scale[side_id, l, f]
                    for t in range(tiles):
                        part = values[:, t * LANES : (t + 1) * LANES]
                        if t == last:
                            wrapped = values[:, total_cols - LANES : total_cols]
                            part = jnp.where(strip_lane >= LANES - HALO, wrapped, part)
                        old = drive[t, f, l, at : at + strip, :]
                        drive[t, f, l, at : at + strip, :] = old + factor * part

    def section(src, base, dst, fac, first, groups, out_tiles):
        for l in range(count_l):
            c_x, c_y = wind_x[l], wind_y[l]
            band = bands[jnp.where(c_x < 0.0, 1, 0)]
            height = groups * 8
            flat = [
                src[t, :, l, first : first + height, :].reshape(count_f * height, LANES)
                for t in range(tiles)
            ]
            state = jnp.concatenate(flat, axis=1) if tiles > 1 else flat[0]
            high = state.astype(jnp.bfloat16)
            low = (state - high.astype(jnp.float32)).astype(jnp.bfloat16)
            band = band[:, 0 : out_tiles * LANES]
            moved = jnp.dot(high, band, preferred_element_type=jnp.float32) + jnp.dot(
                low, band, preferred_element_type=jnp.float32
            )
            for t in range(out_tiles):
                xdiv[t, :, 0:height, :] = moved[:, t * LANES : (t + 1) * LANES].reshape(
                    count_f, height, LANES
                )
            scaled_y, scaled_abs = fac / 60.0 * c_y, fac / 60.0 * jnp.abs(c_y)
            scaled_x = fac / 60.0 * c_x
            taps = [
                scaled_abs * DAMPING[k] - scaled_y * CENTRAL[k] for k in range(2 * REACH + 1)
            ]
            mix = [
                [
                    fac * coupling[f, l, g] + (taps[REACH] if f == g else 0.0)
                    for g in range(count_f)
                ]
                for f in range(count_f)
            ]

            def group(n, _):
                at = pl.multiple_of(first + n * 8, 8)
                local = pl.multiple_of(n * 8, 8)
                for t in range(out_tiles):
                    center = [src[t, g, l, pl.ds(at, 8), :] for g in range(count_f)]
                    weight = relax[t, pl.ds(at, 8), :]
                    for f in range(count_f):
                        rate = drive[t, f, l, pl.ds(at, 8), :] - weight * center[f]
                        total = fac * rate - scaled_x * xdiv[t, f, pl.ds(local, 8), :]
                        for g in range(count_f):
                            total = total + mix[f][g] * center[g]
                        for k in range(2 * REACH + 1):
                            if k != REACH:
                                total = total + taps[k] * src[
                                    t, f, l, pl.ds(at + (k - REACH), 8), :
                                ]
                        value = base[t, f, l, pl.ds(at, 8), :] + total
                        if dst is out:
                            out[f, l, pl.ds(local, 8), :] = value[:, 0:cols]
                        else:
                            dst[t, f, l, pl.ds(at, 8), :] = value * inside[t, pl.ds(at, 8), :]
                return 0

            lax.fori_loop(0, groups, group, 0)

    wide = (rows + 16) // 8
    q1[...] = jnp.zeros_like(q1)
    q2[...] = jnp.zeros_like(q2)
    section(q0, q0, q1, 1.0 / 3.0, PAD - 8, wide, tiles)
    section(q1, q0, q2, 0.5, PAD - 8, wide, tiles)
    section(q2, q0, out, 1.0, PAD, rows // 8, 1)


def swap_rounds(count):
    forward = [(i, i + 1) for i in range(count - 1)]
    return forward, [(b, a) for a, b in forward]


def local(gy_count, gx_count, fields, wind_x, wind_y, coupling, north, south, west, east, strip_scale, widths):
    count_f, count_l, rows, cols = fields.shape
    ext_rows = rows + 2 * PAD
    tiles = 1 if cols + 2 * HALO <= LANES else 2
    packed_rows = -(-HALO * count_f * count_l // 8) * 8
    vmem = pl.BlockSpec(memory_space=pltpu.VMEM)
    smem = pl.BlockSpec(memory_space=pltpu.SMEM)

    strip_shape = jax.ShapeDtypeStruct((packed_rows, cols), jnp.float32)
    to_north, to_south = pl.pallas_call(
        pack_y_kernel,
        out_shape=(strip_shape, strip_shape),
        in_specs=[vmem],
        out_specs=(vmem, vmem),
        compiler_params=pltpu.CompilerParams(vmem_limit_bytes=4 << 20),
        name="pack_y",
    )(fields)
    forward, backward = swap_rounds(gy_count)
    from_north = lax.ppermute(to_south, "gy", forward)
    from_south = lax.ppermute(to_north, "gy", backward)

    recv_count = 1 if gx_count == 2 else 2
    side_shape = jax.ShapeDtypeStruct((ext_rows, LANES), jnp.float32)
    sent = pl.pallas_call(
        functools.partial(pack_x_kernel, gx_count),
        out_shape=(side_shape,) * recv_count,
        in_specs=[vmem] * 3,
        out_specs=(vmem,) * recv_count,
        scratch_shapes=[pltpu.VMEM((ext_rows, LANES), jnp.float32)],
        compiler_params=pltpu.CompilerParams(vmem_limit_bytes=4 << 20),
        name="pack_x",
    )(fields, from_north, from_south)
    forward, backward = swap_rounds(gx_count)
    if recv_count == 1:
        side = [lax.ppermute(sent[0], "gx", forward + backward)]
    else:
        side = [lax.ppermute(sent[0], "gx", forward), lax.ppermute(sent[1], "gx", backward)]

    state = pltpu.VMEM((tiles, count_f, count_l, ext_rows, LANES), jnp.float32)
    plane = pltpu.VMEM((tiles, ext_rows, LANES), jnp.float32)
    bands = jnp.asarray(band_matrices(tiles * LANES), jnp.bfloat16)
    return pl.pallas_call(
        functools.partial(step_kernel, (gy_count, gx_count), recv_count),
        out_shape=jax.ShapeDtypeStruct(fields.shape, jnp.float32),
        in_specs=[vmem] * (3 + recv_count) + [smem] * 3 + [vmem] * 4 + [smem] * 2 + [vmem],
        out_specs=vmem,
        scratch_shapes=[
            state,
            state,
            state,
            state,
            plane,
            plane,
            pltpu.VMEM((tiles, count_f, rows + 16, LANES), jnp.float32),
        ],
        compiler_params=pltpu.CompilerParams(vmem_limit_bytes=16 << 20),
        name="three_sections",
    )(
        fields,
        from_north,
        from_south,
        *side,
        wind_x,
        wind_y,
        jnp.transpose(coupling, (1, 0, 2)),
        north,
        south,
        jnp.swapaxes(west, 2, 3),
        jnp.swapaxes(east, 2, 3),
        jnp.transpose(strip_scale, (0, 2, 1)),
        widths,
        bands,
    )


def solution(mesh):
    return jax.shard_map(
        functools.partial(local, mesh.shape["gy"], mesh.shape["gx"]),
        mesh=mesh,
        in_specs=(
            P("mem", None, "gy", "gx"),
            P("mem"),
            P("mem"),
            P(),
            P("mem", None, None, None),
            P("mem", None, None, None),
            P("mem", None, None, None),
            P("mem", None, None, None),
            P("mem", None, None),
            P(),
        ),
        out_specs=P("mem", None, "gy", "gx"),
        check_vma=False,
    )
```

```python
import functools

import jax
import jax.numpy as jnp
import numpy as np
from jax import lax
from jax.experimental import pallas as pl
from jax.experimental.pallas import tpu as pltpu
from jax.sharding import PartitionSpec as P

RELAX = 0.25
REACH = 3
HALO = 3 * REACH
PAD = 16
LANES = 128
FIRST = PAD - 8
THIRD, HALF = 1.0 / 3.0, 0.5

UPWIND = (-2.0, 15.0, -60.0, 20.0, 30.0, -3.0, 0.0)
CENTRAL = (-1.0, 9.0, -45.0, 0.0, 45.0, -9.0, 1.0)
DAMPING = (1.0, -6.0, 15.0, -20.0, 15.0, -6.0, 1.0)


def lane_of(col, cols):
    if col < 0:
        return 2 * LANES + col
    return col if col < cols else LANES + col - cols


def band_matrices(cols):
    bands = np.zeros((2, 2 * LANES, 2 * LANES), np.float32)
    for col in range(-HALO, cols + HALO):
        for offset in range(-REACH, REACH + 1):
            if -HALO <= col + offset < cols + HALO:
                at = lane_of(col + offset, cols), lane_of(col, cols)
                bands[0][at] = UPWIND[offset + REACH]
                bands[1][at] = -UPWIND[REACH - offset]
    return bands


def iota(shape, dim):
    return lax.broadcasted_iota(jnp.int32, shape, dim)


def edge_weight(distance, width):
    dist = distance.astype(jnp.float32)
    inside = (dist >= 0.0) & (dist < width)
    return jnp.where(inside, jnp.square((width - dist) / width), 0.0)


def slots(count_f, count_l):
    return [(f, l, HALO * (f * count_l + l)) for f in range(count_f) for l in range(count_l)]


def pack_y_kernel(fields, first_round, second_round):
    count_f, count_l, rows, _ = fields.shape
    even = lax.rem(lax.axis_index("gy"), 2) == 0
    for f, l, slot in slots(count_f, count_l):
        top = fields[f, l, 0:HALO, :]
        bottom = fields[f, l, rows - HALO : rows, :]
        first_round[slot : slot + HALO, :] = jnp.where(even, bottom, top)
        second_round[slot : slot + HALO, :] = jnp.where(even, top, bottom)


def halo_rows(gy_count, first_round, second_round, slot):
    gy = lax.axis_index("gy")
    even = lax.rem(gy, 2) == 0
    first = first_round[slot : slot + HALO, :]
    second = second_round[slot : slot + HALO, :]
    north = jnp.where(gy == 0, 0.0, jnp.where(even, second, first))
    south = jnp.where(gy == gy_count - 1, 0.0, jnp.where(even, first, second))
    return north, south


def sent_starts(gx_count, cols):
    if gx_count == 2:
        return [jnp.where(lax.axis_index("gx") == 0, cols - HALO, 0)]
    return [cols - HALO, 0]


def prepare_kernel(
    grid_sizes, fields, north, south, west, east, scale, widths, drive, relax, inside, *rest
):
    gy_count, gx_count = grid_sizes
    payloads, wide = rest[:-1], rest[-1]
    count_f, count_l, rows, cols = fields.shape
    ext_rows = relax.shape[1]
    strip = north.shape[2]
    total_rows, total_cols = rows * gy_count, cols * gx_count
    gy, gx = lax.axis_index("gy"), lax.axis_index("gx")
    row_start, col_start = gy * rows, gx * cols
    width = [widths[s].astype(jnp.float32) for s in range(4)]

    lane_rows = iota((rows, LANES), 1)
    starts = sent_starts(gx_count, cols)
    packed = [jnp.zeros((rows, LANES), jnp.float32) for _ in starts]
    if cols < LANES:
        wide[...] = jnp.zeros_like(wide)
    for f, l, slot in slots(count_f, count_l):
        if cols < LANES:
            wide[:, 0:cols] = fields[f, l]
            own = wide[...]
        else:
            own = fields[f, l]
        for n, start in enumerate(starts):
            moved = pltpu.roll(own, lax.rem(slot + LANES - start, LANES), 1)
            here = (lane_rows >= slot) & (lane_rows < slot + HALO)
            packed[n] = jnp.where(here, moved, packed[n])
    for payload, value in zip(payloads, packed):
        payload[...] = value

    lane = iota((ext_rows, LANES), 1)
    row_global = iota((ext_rows, LANES), 0) + (row_start - PAD)
    row_weight = edge_weight(row_global, width[0]) + edge_weight(
        total_rows - 1 - row_global, width[1]
    )
    lane_one = iota((8, LANES), 1)
    outer_lane = jnp.where(lane_one >= LANES - HALO, lane_one - LANES, lane_one + cols)
    for t, col in enumerate((lane_one, outer_lane)):
        col_weight = edge_weight(col + col_start, width[2]) + edge_weight(
            total_cols - 1 - (col + col_start), width[3]
        )
        relax[t] = RELAX * (row_weight + col_weight[0:1, :])
    outer_col = jnp.where(lane >= LANES - HALO, lane - LANES, lane + cols) + col_start
    inside[...] = jnp.where(
        (row_global >= 0)
        & (row_global < total_rows)
        & (outer_col >= 0)
        & (outer_col < total_cols),
        1.0,
        0.0,
    )

    pos = iota((strip, LANES), 1)
    depth = iota((strip, LANES), 0)
    pick = jnp.concatenate([pos == depth, pos == depth + (cols - strip)], axis=0)
    pick = pick.astype(jnp.float32).astype(jnp.bfloat16)
    west_weight = RELAX * edge_weight(lane_one + col_start, width[2])
    east_weight = RELAX * edge_weight(total_cols - 1 - (lane_one + col_start), width[3])
    west_weight = jnp.where(lane_one < strip, west_weight, 0.0)
    east_weight = jnp.where((lane_one >= cols - strip) & (lane_one < cols), east_weight, 0.0)
    shift = lax.rem(PAD + total_rows - row_start, total_rows)
    for f in range(count_f):
        for l in range(count_l):
            both = jnp.concatenate([west[f, l], east[f, l]], axis=0).astype(jnp.float32)
            both = pltpu.roll(both, shift, 1)[:, 0:LANES].astype(jnp.bfloat16)
            raw = lax.dot_general(
                both, pick, (((0,), (0,)), ((), ())), preferred_element_type=jnp.float32
            )
            factor = west_weight * scale[2, l, f] + east_weight * scale[3, l, f]
            drive[0, f, l] = raw[0:ext_rows] * factor[0:1, :]
    drive[1] = jnp.zeros(drive.shape[1:], jnp.float32)

    own_shift = lax.rem(total_cols - col_start, total_cols)
    outer_shift = lax.rem(2 * total_cols - cols - col_start, total_cols)
    for source, side, at, here in (
        (north, 0, PAD, gy == 0),
        (south, 1, PAD + rows - strip, gy == gy_count - 1),
    ):

        @pl.when(here)
        def _(source=source, side=side, at=at):
            distance = depth if side == 0 else strip - 1 - depth
            weight = RELAX * edge_weight(distance, width[side])
            for f in range(count_f):
                for l in range(count_l):
                    values = source[f, l].astype(jnp.float32)
                    own = pltpu.roll(values, own_shift, 1)
                    outer = pltpu.roll(values, outer_shift, 1)[:, 0:LANES]
                    outer = jnp.where(
                        pos >= LANES - HALO, own[:, total_cols - LANES : total_cols], outer
                    )
                    factor = weight * scale[side, l, f]
                    old = drive[0, f, l, at : at + strip, :]
                    drive[0, f, l, at : at + strip, :] = old + factor * own[:, 0:LANES]
                    drive[1, f, l, at : at + strip, :] = factor * outer


def pack_x_kernel(grid_sizes, first_round, second_round, *rest):
    gy_count, gx_count = grid_sizes
    sides = (len(rest) - 1) // 2
    payloads, outs, ext = rest[:sides], rest[sides:-1], rest[-1]
    cols = first_round.shape[1]
    rows = payloads[0].shape[0]
    lane = iota((2 * PAD, LANES), 1)
    starts = sent_starts(gx_count, cols)
    packed = [jnp.zeros((2 * PAD, LANES), jnp.float32) for _ in starts]
    ext[...] = jnp.zeros_like(ext)
    for index in range(ext.shape[0]):
        slot = index * HALO
        north, south = halo_rows(gy_count, first_round, second_round, slot)
        ext[index, PAD - HALO : PAD, 0:cols] = north
        ext[index, PAD : PAD + HALO, 0:cols] = south
        for n, start in enumerate(starts):
            moved = pltpu.roll(ext[index], lax.rem(slot + LANES - start, LANES), 1)
            packed[n] = jnp.where((lane >= slot) & (lane < slot + HALO), moved, packed[n])
    for out, payload, value in zip(outs, payloads, packed):
        out[0:PAD, :] = value[0:PAD]
        out[PAD : PAD + rows, :] = payload[...]
        out[PAD + rows : 2 * PAD + rows, :] = value[PAD : 2 * PAD]


def level_weights(coupling, wind_y, l, fac, count_f):
    scaled, scaled_abs = fac / 60.0 * wind_y[l], fac / 60.0 * jnp.abs(wind_y[l])
    taps = [scaled_abs * DAMPING[k] - scaled * CENTRAL[k] for k in range(2 * REACH + 1)]
    mix = [
        [fac * coupling[f, l, g] + (taps[REACH] if f == g else 0.0) for g in range(count_f)]
        for f in range(count_f)
    ]
    return taps, mix


def cell_terms(src, l, f, at, centers, weight, taps, mix, total):
    for g, center in enumerate(centers):
        total = total + (mix[f][g] - weight if g == f else mix[f][g]) * center
    for k in range(2 * REACH + 1):
        if k != REACH:
            total = total + taps[k] * src[f, l, pl.ds(at + (k - REACH), 8), :]
    return total


def begin_kernel(
    gy_count,
    fields,
    first_round,
    second_round,
    drive,
    relax,
    wind_y,
    coupling,
    state,
    part_one,
    base_two,
    base_three,
):
    count_f, count_l, rows, cols = fields.shape
    ext_rows = state.shape[2]
    state[...] = jnp.zeros_like(state)
    for f, l, slot in slots(count_f, count_l):
        north, south = halo_rows(gy_count, first_round, second_round, slot)
        state[f, l, PAD - HALO : PAD, 0:cols] = north
        state[f, l, PAD : PAD + rows, 0:cols] = fields[f, l]
        state[f, l, PAD + rows : PAD + rows + HALO, 0:cols] = south
    for l in range(count_l):
        taps, mix = level_weights(coupling, wind_y, l, THIRD, count_f)

        def group(n, _):
            at = pl.multiple_of(FIRST + n * 8, 8)
            to = pl.multiple_of(n * 8, 8)
            centers = [state[g, l, pl.ds(at, 8), :] for g in range(count_f)]
            weight = THIRD * relax[0, pl.ds(at, 8), :]
            for f in range(count_f):
                forced = drive[0, f, l, pl.ds(at, 8), :]
                base_two[f, l, pl.ds(to, 8), :] = centers[f] + HALF * forced
                base_three[f, l, pl.ds(to, 8), :] = centers[f] + forced
                total = centers[f] + THIRD * forced
                total = cell_terms(state, l, f, at, centers, weight, taps, mix, total)
                part_one[f, l, pl.ds(to, 8), :] = total
            return 0

        lax.fori_loop(0, (rows + 16) // 8, group, 0)


def finish_kernel(grid_sizes, sides, *refs):
    gy_count, gx_count = grid_sizes
    side = refs[:sides]
    (
        state,
        part_one,
        base_two,
        base_three,
        drive,
        relax,
        inside,
        wind_x,
        wind_y,
        coupling,
        bands,
        out,
        outer,
        own_one,
        outer_one,
        own_two,
        outer_two,
        xdiv,
    ) = refs[sides:]
    count_f, count_l, rows, cols = out.shape
    ext_rows = state.shape[2]
    gy, gx = lax.axis_index("gy"), lax.axis_index("gx")

    lane = iota((ext_rows, LANES), 1)
    for f, l, slot in slots(count_f, count_l):
        if sides == 1:
            placed = [(side[0], jnp.where(gx == 0, 0, LANES - HALO))]
        else:
            placed = [(side[0], LANES - HALO), (side[1], 0)]
        merged = jnp.zeros((ext_rows, LANES), jnp.float32)
        for source, target in placed:
            moved = pltpu.roll(source[...], lax.rem(target + LANES - slot, LANES), 1)
            merged = jnp.where((lane >= target) & (lane < target + HALO), moved, merged)
        outer[f, l] = merged

    def x_divergence(own, outer_cols, l, first, height, tiles):
        flat = [
            source[:, l, first : first + height, :].reshape(count_f * height, LANES)
            for source in (own, outer_cols)
        ]
        whole = jnp.concatenate(flat, axis=1)
        high = whole.astype(jnp.bfloat16)
        low = (whole - high.astype(jnp.float32)).astype(jnp.bfloat16)
        band = bands[jnp.where(wind_x[l] < 0.0, 1, 0)][:, 0 : tiles * LANES]
        moved = jnp.dot(high, band, preferred_element_type=jnp.float32) + jnp.dot(
            low, band, preferred_element_type=jnp.float32
        )
        for t in range(tiles):
            xdiv[t, :, 0:height, :] = moved[:, t * LANES : (t + 1) * LANES].reshape(
                count_f, height, LANES
            )

    def outside_rows(dst):
        @pl.when(gy == 0)
        def _():
            dst[:, :, FIRST : FIRST + 8, :] = jnp.zeros((count_f, count_l, 8, LANES), jnp.float32)

        @pl.when(gy == gy_count - 1)
        def _():
            dst[:, :, PAD + rows : PAD + rows + 8, :] = jnp.zeros(
                (count_f, count_l, 8, LANES), jnp.float32
            )

    groups = (rows + 16) // 8
    for own, outer_cols, own_next, outer_next, fac in (
        (state, outer, own_one, outer_one, THIRD),
        (own_one, outer_one, own_two, outer_two, HALF),
    ):
        for l in range(count_l):
            x_divergence(own, outer_cols, l, FIRST, groups * 8, 2)
            taps, mix = level_weights(coupling, wind_y, l, fac, count_f)
            scaled_x = fac / 60.0 * wind_x[l]

            def group(n, _):
                at = pl.multiple_of(FIRST + n * 8, 8)
                to = pl.multiple_of(n * 8, 8)
                centers = [outer_cols[g, l, pl.ds(at, 8), :] for g in range(count_f)]
                weight = fac * relax[1, pl.ds(at, 8), :]
                kept = inside[pl.ds(at, 8), :]
                for f in range(count_f):
                    total = outer[f, l, pl.ds(at, 8), :] + fac * drive[1, f, l, pl.ds(at, 8), :]
                    total = total - scaled_x * xdiv[1, f, pl.ds(to, 8), :]
                    total = cell_terms(outer_cols, l, f, at, centers, weight, taps, mix, total)
                    outer_next[f, l, pl.ds(at, 8), :] = total * kept
                if own is state:
                    for f in range(count_f):
                        total = part_one[f, l, pl.ds(to, 8), :]
                        own_next[f, l, pl.ds(at, 8), :] = (
                            total - scaled_x * xdiv[0, f, pl.ds(to, 8), :]
                        )
                else:
                    centers = [own[g, l, pl.ds(at, 8), :] for g in range(count_f)]
                    weight = fac * relax[0, pl.ds(at, 8), :]
                    for f in range(count_f):
                        total = base_two[f, l, pl.ds(to, 8), :]
                        total = total - scaled_x * xdiv[0, f, pl.ds(to, 8), :]
                        own_next[f, l, pl.ds(at, 8), :] = cell_terms(
                            own, l, f, at, centers, weight, taps, mix, total
                        )
                return 0

            lax.fori_loop(0, groups, group, 0)
        outside_rows(own_next)

    for l in range(count_l):
        x_divergence(own_two, outer_two, l, PAD, rows, 1)
        taps, mix = level_weights(coupling, wind_y, l, 1.0, count_f)
        scaled_x = wind_x[l] / 60.0

        def group(n, _):
            at = pl.multiple_of(PAD + n * 8, 8)
            to = pl.multiple_of(n * 8, 8)
            centers = [own_two[g, l, pl.ds(at, 8), :] for g in range(count_f)]
            weight = relax[0, pl.ds(at, 8), :]
            for f in range(count_f):
                total = base_three[f, l, pl.ds(to + 8, 8), :]
                total = total - scaled_x * xdiv[0, f, pl.ds(to, 8), :]
                total = cell_terms(own_two, l, f, at, centers, weight, taps, mix, total)
                out[f, l, pl.ds(to, 8), :] = total[:, 0:cols]
            return 0

        lax.fori_loop(0, rows // 8, group, 0)


def pair_rounds(gy_count, gx_count):
    rounds = []
    for start in (0, 1):
        partner = {}
        for low in range(start, gy_count - 1, 2):
            partner[low], partner[low + 1] = low + 1, low
        pairs = []
        for y in range(gy_count):
            for x in range(gx_count):
                if y in partner:
                    pairs.append((y * gx_count + x, partner[y] * gx_count + x))
                elif gx_count % 2 == 0:
                    pairs.append((y * gx_count + x, y * gx_count + (x ^ 1)))
        rounds.append(pairs)
    return rounds


def local(
    gy_count, gx_count, fields, wind_x, wind_y, coupling, north, south, west, east, strip_scale, widths
):
    count_f, count_l, rows, cols = fields.shape
    ext_rows = rows + 2 * PAD
    grid_sizes = (gy_count, gx_count)
    packed_rows = -(-HALO * count_f * count_l // 8) * 8
    vmem = pl.BlockSpec(memory_space=pltpu.VMEM)
    smem = pl.BlockSpec(memory_space=pltpu.SMEM)
    f32 = functools.partial(jax.ShapeDtypeStruct, dtype=jnp.float32)

    def call(body, name, out_shape, inputs, scratch=(), limit=4):
        several = isinstance(out_shape, tuple)
        return pl.pallas_call(
            body,
            out_shape=out_shape,
            in_specs=[space for _, space in inputs],
            out_specs=(vmem,) * len(out_shape) if several else vmem,
            scratch_shapes=list(scratch),
            compiler_params=pltpu.CompilerParams(vmem_limit_bytes=limit << 20),
            name=name,
        )(*[value for value, _ in inputs])

    def inputs(space, *values):
        return [(value, space) for value in values]

    strip_shape = f32((packed_rows, cols))
    sent_first, sent_second = call(
        pack_y_kernel, "pack_y", (strip_shape, strip_shape), inputs(vmem, fields)
    )
    first_pairs, second_pairs = pair_rounds(gy_count, gx_count)
    first_round = lax.ppermute(sent_first, ("gy", "gx"), first_pairs)
    second_round = lax.ppermute(sent_second, ("gy", "gx"), second_pairs)

    mixing = jnp.transpose(coupling, (1, 0, 2))
    scales = jnp.transpose(strip_scale, (0, 2, 1))
    sides = 1 if gx_count == 2 else 2
    state_shape = (count_f, count_l, ext_rows, LANES)
    prepared = call(
        functools.partial(prepare_kernel, grid_sizes),
        "prepare",
        (f32((2,) + state_shape), f32((2, ext_rows, LANES)), f32((ext_rows, LANES)))
        + (f32((rows, LANES)),) * sides,
        inputs(vmem, fields, north, south, jnp.swapaxes(west, 2, 3), jnp.swapaxes(east, 2, 3))
        + inputs(smem, scales, widths),
        scratch=[pltpu.VMEM((rows, LANES), jnp.float32)],
    )
    drive, relax, inside = prepared[:3]

    sent = call(
        functools.partial(pack_x_kernel, grid_sizes),
        "pack_x",
        (f32((ext_rows, LANES)),) * sides,
        inputs(vmem, first_round, second_round, *prepared[3:]),
        scratch=[pltpu.VMEM((count_f * count_l, 2 * PAD, LANES), jnp.float32)],
    )
    forward = [(i, i + 1) for i in range(gx_count - 1)]
    backward = [(b, a) for a, b in forward]
    if sides == 1:
        side = [lax.ppermute(sent[0], "gx", forward + backward)]
    else:
        side = [lax.ppermute(sent[0], "gx", forward), lax.ppermute(sent[1], "gx", backward)]

    wide_shape = (count_f, count_l, rows + 16, LANES)
    begun = call(
        functools.partial(begin_kernel, gy_count),
        "begin",
        (f32(state_shape), f32(wide_shape), f32(wide_shape), f32(wide_shape)),
        inputs(vmem, fields, first_round, second_round, drive, relax)
        + inputs(smem, wind_y, mixing),
    )
    bands = jnp.asarray(band_matrices(cols), jnp.bfloat16)
    return call(
        functools.partial(finish_kernel, grid_sizes, sides),
        "finish",
        f32(fields.shape),
        inputs(vmem, *side, *begun, drive, relax, inside)
        + inputs(smem, wind_x, wind_y, mixing)
        + inputs(vmem, bands),
        scratch=[pltpu.VMEM(state_shape, jnp.float32)] * 5
        + [pltpu.VMEM((2, count_f, rows + 16, LANES), jnp.float32)],
        limit=12,
    )


def solution(mesh):
    return jax.shard_map(
        functools.partial(local, mesh.shape["gy"], mesh.shape["gx"]),
        mesh=mesh,
        in_specs=(
            P("mem", None, "gy", "gx"),
            P("mem"),
            P("mem"),
            P(),
            P("mem", None, None, None),
            P("mem", None, None, None),
            P("mem", None, None, None),
            P("mem", None, None, None),
            P("mem", None, None),
            P(),
        ),
        out_specs=P("mem", None, "gy", "gx"),
        check_vma=False,
    )
```

```python
import functools

import jax
import jax.numpy as jnp
import numpy as np
from jax import lax
from jax.experimental import pallas as pl
from jax.experimental.pallas import tpu as pltpu
from jax.sharding import PartitionSpec as P

RELAX = 0.25
REACH = 3
HALO = 3 * REACH
PAD = 16
LANES = 128
FIRST = PAD - 8
THIRD, HALF = 1.0 / 3.0, 0.5

UPWIND = (-2.0, 15.0, -60.0, 20.0, 30.0, -3.0, 0.0)
CENTRAL = (-1.0, 9.0, -45.0, 0.0, 45.0, -9.0, 1.0)
DAMPING = (1.0, -6.0, 15.0, -20.0, 15.0, -6.0, 1.0)


def own_bands(cols):
    bands = np.zeros((2, LANES, LANES), np.float32)
    for col in range(cols):
        for offset in range(-REACH, REACH + 1):
            if 0 <= col + offset < cols:
                bands[0, col + offset, col] = UPWIND[offset + REACH]
                bands[1, col + offset, col] = -UPWIND[REACH - offset]
    return bands


def side_bands(count):
    bands = np.zeros((2, 2, 2 * LANES, 2 * LANES), np.float32)
    for side, (halo_at, edge_at) in enumerate(((0, -REACH), (-HALO, 0))):
        cells = [(halo_at + k, 0, k) for k in range(HALO)]
        cells += [(edge_at + k, LANES, k) for k in range(REACH)]
        for index in range(count):
            slot = index * HALO
            for source, source_half, source_lane in cells:
                for target, target_half, target_lane in cells:
                    offset = source - target
                    if abs(offset) > REACH or source_half == target_half == LANES:
                        continue
                    at = source_half + slot + source_lane, target_half + slot + target_lane
                    bands[side, 0][at] = UPWIND[offset + REACH]
                    bands[side, 1][at] = -UPWIND[REACH - offset]
    return bands


def iota(shape, dim):
    return lax.broadcasted_iota(jnp.int32, shape, dim)


def edge_weight(distance, width):
    dist = distance.astype(jnp.float32)
    inside = (dist >= 0.0) & (dist < width)
    return jnp.where(inside, jnp.square((width - dist) / width), 0.0)


def slots(count_f, count_l):
    return [(f, l, HALO * (f * count_l + l)) for f in range(count_f) for l in range(count_l)]


def pack_y_kernel(fields, first_round, second_round):
    count_f, count_l, rows, _ = fields.shape
    even = lax.rem(lax.axis_index("gy"), 2) == 0
    for f, l, slot in slots(count_f, count_l):
        top = fields[f, l, 0:HALO, :]
        bottom = fields[f, l, rows - HALO : rows, :]
        first_round[slot : slot + HALO, :] = jnp.where(even, bottom, top)
        second_round[slot : slot + HALO, :] = jnp.where(even, top, bottom)


def halo_rows(gy_count, first_round, second_round, slot):
    gy = lax.axis_index("gy")
    even = lax.rem(gy, 2) == 0
    first = first_round[slot : slot + HALO, :]
    second = second_round[slot : slot + HALO, :]
    north = jnp.where(gy == 0, 0.0, jnp.where(even, second, first))
    south = jnp.where(gy == gy_count - 1, 0.0, jnp.where(even, first, second))
    return north, south


def sent_starts(gx_count, cols):
    if gx_count == 2:
        return [jnp.where(lax.axis_index("gx") == 0, cols - HALO, 0)]
    return [cols - HALO, 0]


def side_ids(gx_count):
    if gx_count == 2:
        return [jnp.where(lax.axis_index("gx") == 0, 0, 1)]
    return [1, 0]


def edge_starts(gx_count, cols):
    return [jnp.where(side == 0, cols - REACH, 0) for side in side_ids(gx_count)]


def level_weights(coupling, wind_x, wind_y, l, count_f):
    speed, size = wind_y[l] / 60.0, jnp.abs(wind_y[l]) / 60.0
    taps = [size * DAMPING[k] - speed * CENTRAL[k] for k in range(2 * REACH + 1)]
    mix = [
        [coupling[f, l, g] + (taps[REACH] if f == g else 0.0) for g in range(count_f)]
        for f in range(count_f)
    ]
    return [tap for k, tap in enumerate(taps) if k != REACH], mix, -wind_x[l] / 60.0


def prepare_kernel(
    grid_sizes,
    fields,
    north,
    south,
    west,
    east,
    own_band,
    side_band,
    scale,
    widths,
    wind_x,
    wind_y,
    coupling,
    drive,
    relax,
    row_relax,
    inside,
    weights,
    lane_weights,
    own_matrix,
    *rest,
):
    gy_count, gx_count = grid_sizes
    sides = (len(rest) - 1) // 3
    payloads, side_drive, side_matrix = rest[:sides], rest[sides : 2 * sides], rest[2 * sides : -1]
    wide = rest[-1]
    count_f, count_l, rows, cols = fields.shape
    wide_rows = relax.shape[0]
    strip = north.shape[2]
    total_rows, total_cols = rows * gy_count, cols * gx_count
    gy, gx = lax.axis_index("gy"), lax.axis_index("gx")
    row_start, col_start = gy * rows, gx * cols
    width = [widths[s].astype(jnp.float32) for s in range(4)]
    lane = iota((8, LANES), 1)

    lane_rows = iota((rows, LANES), 1)
    starts = sent_starts(gx_count, cols)
    packed = [jnp.zeros((rows, LANES), jnp.float32) for _ in starts]
    if cols < LANES:
        wide[...] = jnp.zeros_like(wide)
    for f, l, slot in slots(count_f, count_l):
        if cols < LANES:
            wide[:, 0:cols] = fields[f, l]
            own = wide[...]
        else:
            own = fields[f, l]
        for n, start in enumerate(starts):
            moved = pltpu.roll(own, lax.rem(slot + LANES - start, LANES), 1)
            here = (lane_rows >= slot) & (lane_rows < slot + HALO)
            packed[n] = jnp.where(here, moved, packed[n])
    for payload, value in zip(payloads, packed):
        payload[...] = value

    def full(value):
        return jnp.full((8, LANES), value, jnp.float32)

    negative = jnp.zeros((1, 2 * LANES), jnp.bool_)
    double = lax.rem(iota((1, 2 * LANES), 1), LANES)
    lane_taps = [full(0.0) for _ in range(2 * REACH)]
    lane_mix = [full(0.0) for _ in range(2 * count_f - 1)]
    lane_speed = full(0.0)
    for l in range(count_l):
        taps, mix, speed = level_weights(coupling, wind_x, wind_y, l, count_f)
        flat = taps + [entry for line in mix for entry in line] + [speed]
        for n, entry in enumerate(flat):
            weights[l, n] = full(entry)
        own_matrix[l] = own_band[jnp.where(wind_x[l] < 0.0, 1, 0)]
        for f in range(count_f):
            slot = HALO * (f * count_l + l)
            here = (lane >= slot) & (lane < slot + HALO)
            lane_taps = [jnp.where(here, tap, old) for tap, old in zip(taps, lane_taps)]
            lane_speed = jnp.where(here, speed, lane_speed)
            for g in range(count_f):
                at = g - f + count_f - 1
                lane_mix[at] = jnp.where(here, mix[f][g], lane_mix[at])
            here = (double >= slot) & (double < slot + HALO)
            negative = negative | (here & (wind_x[l] < 0.0))
    for n, entry in enumerate(lane_taps + lane_mix + [lane_speed]):
        lane_weights[n] = entry
    for side, matrix in zip(side_ids(gx_count), side_matrix):
        matrix[...] = jnp.where(
            negative, side_band[side, 1].astype(jnp.float32), side_band[side, 0].astype(jnp.float32)
        ).astype(jnp.bfloat16)

    row_global = iota((wide_rows, LANES), 0) + (row_start - 8)
    row_weight = RELAX * (
        edge_weight(row_global, width[0]) + edge_weight(total_rows - 1 - row_global, width[1])
    )
    col_weight = RELAX * (
        edge_weight(lane + col_start, width[2])
        + edge_weight(total_cols - 1 - (lane + col_start), width[3])
    )
    row_relax[...] = row_weight
    relax[...] = row_weight + col_weight[0:1, :]
    inside[...] = jnp.where((row_global >= 0) & (row_global < total_rows), 1.0, 0.0)

    pos = iota((strip, LANES), 1)
    depth = iota((strip, LANES), 0)
    pick = jnp.concatenate([pos == depth, pos == depth + (cols - strip)], axis=0)
    pick = pick.astype(jnp.float32).astype(jnp.bfloat16)
    west_weight = RELAX * edge_weight(lane + col_start, width[2])
    east_weight = RELAX * edge_weight(total_cols - 1 - (lane + col_start), width[3])
    west_weight = jnp.where(lane < strip, west_weight, 0.0)
    east_weight = jnp.where((lane >= cols - strip) & (lane < cols), east_weight, 0.0)
    shift = lax.rem(8 + total_rows - row_start, total_rows)
    for f in range(count_f):
        for l in range(count_l):
            both = jnp.concatenate([west[f, l], east[f, l]], axis=0).astype(jnp.float32)
            both = pltpu.roll(both, shift, 1)[:, 0:LANES].astype(jnp.bfloat16)
            raw = lax.dot_general(
                both, pick, (((0,), (0,)), ((), ())), preferred_element_type=jnp.float32
            )
            factor = west_weight * scale[2, l, f] + east_weight * scale[3, l, f]
            drive[f, l] = raw[0:wide_rows] * factor[0:1, :]
    for ref in side_drive:
        ref[...] = jnp.zeros_like(ref)

    own_shift = lax.rem(total_cols - col_start, total_cols)
    for source, side, at, here in (
        (north, 0, 8, gy == 0),
        (south, 1, 8 + rows - strip, gy == gy_count - 1),
    ):

        @pl.when(here)
        def _(source=source, side=side, at=at):
            distance = depth if side == 0 else strip - 1 - depth
            weight = RELAX * edge_weight(distance, width[side])
            packed = [jnp.zeros((strip, LANES), jnp.float32) for _ in side_drive]
            for f, l, slot in slots(count_f, count_l):
                values = source[f, l].astype(jnp.float32)
                factor = weight * scale[side, l, f]
                own = pltpu.roll(values, own_shift, 1)[:, 0:LANES]
                drive[f, l, at : at + strip, :] = drive[f, l, at : at + strip, :] + factor * own
                for n, which in enumerate(side_ids(gx_count)):
                    begin = jnp.where(which == 0, cols, -HALO) + col_start
                    outer = pltpu.roll(
                        values, lax.rem(slot + 2 * total_cols - begin, total_cols), 1
                    )[:, 0:LANES]
                    packed[n] = jnp.where(
                        (pos >= slot) & (pos < slot + HALO), factor * outer, packed[n]
                    )
            for ref, value in zip(side_drive, packed):
                ref[at : at + strip, :] = value


def pack_x_kernel(grid_sizes, first_round, second_round, *rest):
    gy_count, gx_count = grid_sizes
    sides = (len(rest) - 1) // 2
    payloads, outs, ext = rest[:sides], rest[sides:-1], rest[-1]
    cols = first_round.shape[1]
    rows = payloads[0].shape[0]
    lane = iota((2 * PAD, LANES), 1)
    starts = sent_starts(gx_count, cols)
    packed = [jnp.zeros((2 * PAD, LANES), jnp.float32) for _ in starts]
    ext[...] = jnp.zeros_like(ext)
    for index in range(ext.shape[0]):
        slot = index * HALO
        north, south = halo_rows(gy_count, first_round, second_round, slot)
        ext[index, PAD - HALO : PAD, 0:cols] = north
        ext[index, PAD : PAD + HALO, 0:cols] = south
        for n, start in enumerate(starts):
            moved = pltpu.roll(ext[index], lax.rem(slot + LANES - start, LANES), 1)
            packed[n] = jnp.where((lane >= slot) & (lane < slot + HALO), moved, packed[n])
    for out, payload, value in zip(outs, payloads, packed):
        out[0:PAD, :] = value[0:PAD]
        out[PAD : PAD + rows, :] = payload[...]
        out[PAD + rows : 2 * PAD + rows, :] = value[PAD : 2 * PAD]


def loaded(weights, l, fac, count_f):
    flat = [fac * weights[l, n] for n in range(weights.shape[1])]
    taps, flat, speed = flat[: 2 * REACH], flat[2 * REACH : -1], flat[-1]
    return taps, [flat[f * count_f : (f + 1) * count_f] for f in range(count_f)], speed


def y_terms(rows_at, at, taps, total):
    offsets = [k for k in range(-REACH, REACH + 1) if k != 0]
    for tap, offset in zip(taps, offsets):
        total = total + tap * rows_at(at + offset)
    return total


def cell_terms(src, l, f, at, centers, weight, taps, mix, total):
    for g, center in enumerate(centers):
        total = total + (mix[f][g] - weight if g == f else mix[f][g]) * center
    return y_terms(lambda row: src[f, l, pl.ds(row, 8), :], at, taps, total)


def split(value):
    high = value.astype(jnp.bfloat16)
    return high, (value - high.astype(jnp.float32)).astype(jnp.bfloat16)


def x_divergence(src, l, first, height, matrix, xdiv):
    count_f = src.shape[0]
    whole = src[:, l, first : first + height, :].reshape(count_f * height, LANES)
    both = jnp.concatenate(split(whole), axis=1)
    twice = jnp.concatenate([matrix[l], matrix[l]], axis=0)
    moved = jnp.dot(both, twice, preferred_element_type=jnp.float32)
    xdiv[:, 0:height, :] = moved.reshape(count_f, height, LANES)


def begin_kernel(
    grid_sizes,
    fields,
    first_round,
    second_round,
    drive,
    relax,
    weights,
    own_matrix,
    part_one,
    base_two,
    base_three,
    *rest,
):
    gy_count, gx_count = grid_sizes
    edges, state, xdiv = rest[:-2], rest[-2], rest[-1]
    count_f, count_l, rows, cols = fields.shape
    wide_rows = relax.shape[0]
    pad_rows = jnp.zeros((PAD, LANES), jnp.float32)
    for f, l, slot in slots(count_f, count_l):
        north, south = halo_rows(gy_count, first_round, second_round, slot)
        if cols < LANES:
            state[f, l] = jnp.zeros(state.shape[2:], jnp.float32)
        else:
            state[f, l, 0:PAD, :] = pad_rows
            state[f, l, PAD + rows : 2 * PAD + rows, :] = pad_rows
        state[f, l, PAD - HALO : PAD, 0:cols] = north
        state[f, l, PAD : PAD + rows, 0:cols] = fields[f, l]
        state[f, l, PAD + rows : PAD + rows + HALO, 0:cols] = south
    lane = iota((wide_rows, LANES), 1)
    for edge, start in zip(edges, edge_starts(gx_count, cols)):
        packed = jnp.zeros((wide_rows, LANES), jnp.float32)
        near = (lane >= start) & (lane < start + REACH)
        for f, l, slot in slots(count_f, count_l):
            kept = jnp.where(near, state[f, l, FIRST : FIRST + wide_rows, :], 0.0)
            packed = packed + pltpu.roll(kept, lax.rem(slot + LANES - start, LANES), 1)
        edge[...] = packed
    for l in range(count_l):
        x_divergence(state, l, FIRST, wide_rows, own_matrix, xdiv)
        taps, mix, speed = loaded(weights, l, THIRD, count_f)

        def group(n, _):
            at = pl.multiple_of(FIRST + n * 8, 8)
            to = pl.multiple_of(n * 8, 8)
            centers = [state[g, l, pl.ds(at, 8), :] for g in range(count_f)]
            weight = THIRD * relax[pl.ds(to, 8), :]
            for f in range(count_f):
                forced = drive[f, l, pl.ds(to, 8), :]
                base_two[f, l, pl.ds(to, 8), :] = centers[f] + HALF * forced
                base_three[f, l, pl.ds(to, 8), :] = centers[f] + forced
                total = centers[f] + THIRD * forced + speed * xdiv[f, pl.ds(to, 8), :]
                total = cell_terms(state, l, f, at, centers, weight, taps, mix, total)
                part_one[f, l, pl.ds(to, 8), :] = total
            return 0

        lax.fori_loop(0, wide_rows // 8, group, 0)


def finish_kernel(grid_sizes, sides, *refs):
    gy_count, gx_count = grid_sizes
    halos, edges, side_drive, side_matrix = (
        refs[n * sides : (n + 1) * sides] for n in range(4)
    )
    (
        part_one,
        base_two,
        base_three,
        relax,
        row_relax,
        inside,
        weights,
        lane_weights,
        own_matrix,
        out,
        own_one,
        own_two,
        halo_one,
        halo_two,
        edge_next,
        halo_div,
        edge_add,
        xdiv,
    ) = refs[4 * sides :]
    count_f, count_l, rows, cols = out.shape
    wide_rows = relax.shape[0]
    groups = wide_rows // 8
    gy, gx = lax.axis_index("gy"), lax.axis_index("gx")
    starts = edge_starts(gx_count, cols)
    exists = [None] if sides == 1 else [gx > 0, gx < gx_count - 1]
    lane = iota((8, LANES), 1)
    near = [(lane >= start) & (lane < start + REACH) for start in starts]
    zeros = jnp.zeros((8, LANES), jnp.float32)

    def halo_products(halo, edge, matrix, s, fac, first, height):
        speed = lane_weights[lane_weights.shape[0] - 1][0:1, :]
        rows_in = halo[pl.ds(first, height), :]
        if edge is None:
            both = jnp.concatenate(split(rows_in), axis=0)
            moved = jnp.dot(
                both, matrix[0:LANES, LANES:], preferred_element_type=jnp.float32
            )
            add = moved[0:height] + moved[height:]
        else:
            rows_in = jnp.concatenate([rows_in, edge], axis=1)
            both = jnp.concatenate(split(rows_in), axis=0)
            moved = jnp.dot(both, matrix[...], preferred_element_type=jnp.float32)
            moved = moved[0:height] + moved[height:]
            halo_div[s] = speed * moved[:, 0:LANES]
            add = moved[:, LANES:]
        edge_add[s, 0:height, :] = (fac * speed) * add

    def halo_section(halo, halo_next, s, fac):
        count = 2 * count_f - 1
        for n in range(groups):
            at, to = FIRST + n * 8, n * 8
            center = halo[at : at + 8, :]
            rate = side_drive[s][to : to + 8, :] + halo_div[s, to : to + 8, :]
            rate = rate - row_relax[to : to + 8, :] * center
            for d in range(count):
                moved = center
                if d != count_f - 1:
                    step = (d - (count_f - 1)) * HALO * count_l
                    moved = pltpu.roll(center, -step % LANES, 1)
                rate = rate + lane_weights[2 * REACH + d] * moved
            taps = [lane_weights[k] for k in range(2 * REACH)]
            rate = y_terms(lambda row: halo[row : row + 8, :], at, taps, rate)
            value = halos[s][at : at + 8, :] + fac * rate
            kept = inside[to : to + 8, :]
            if exists[s] is not None:
                kept = jnp.where(exists[s], kept, 0.0)
            halo_next[s, at : at + 8, :] = value * kept

    def from_halo(total, slot, to):
        for s, start in enumerate(starts):
            shift = lax.rem(start + LANES - slot, LANES)
            moved = pltpu.roll(edge_add[s, pl.ds(to, 8), :], shift, 1)
            total = total + jnp.where(near[s], moved, 0.0)
        return total

    def keep_edges(packed, value, slot):
        for s, start in enumerate(starts):
            moved = pltpu.roll(
                jnp.where(near[s], value, 0.0), lax.rem(slot + LANES - start, LANES), 1
            )
            packed[s] = packed[s] + moved

    def outside_rows(own, section):
        for row, here in ((0, gy == 0), (rows + 8, gy == gy_count - 1)):

            @pl.when(here)
            def _(row=row):
                own[:, :, FIRST + row : FIRST + row + 8, :] = jnp.zeros(
                    (count_f, count_l, 8, LANES), jnp.float32
                )
                for s in range(sides):
                    for l in range(count_l):
                        edge_next[section, s, l, row : row + 8, :] = zeros

    for s in range(sides):
        halo_products(halos[s], edges[s][...], side_matrix[s], s, THIRD, FIRST, wide_rows)
        halo_section(halos[s], halo_one, s, THIRD)
    for l in range(count_l):

        def group(n, _):
            at = pl.multiple_of(FIRST + n * 8, 8)
            to = pl.multiple_of(n * 8, 8)
            packed = [zeros] * sides
            for f in range(count_f):
                slot = HALO * (f * count_l + l)
                value = from_halo(part_one[f, l, pl.ds(to, 8), :], slot, to)
                own_one[f, l, pl.ds(at, 8), :] = value
                keep_edges(packed, value, slot)
            for s in range(sides):
                edge_next[0, s, l, pl.ds(to, 8), :] = packed[s]
            return 0

        lax.fori_loop(0, groups, group, 0)
    outside_rows(own_one, 0)

    def edges_of(section, s):
        return sum(edge_next[section, s, l] for l in range(count_l))

    for s in range(sides):
        halo_products(
            halo_one.at[s], edges_of(0, s), side_matrix[s], s, HALF, FIRST, wide_rows
        )
        halo_section(halo_one.at[s], halo_two, s, HALF)
    for l in range(count_l):
        x_divergence(own_one, l, FIRST, wide_rows, own_matrix, xdiv)
        taps, mix, speed = loaded(weights, l, HALF, count_f)

        def group(n, _):
            at = pl.multiple_of(FIRST + n * 8, 8)
            to = pl.multiple_of(n * 8, 8)
            centers = [own_one[g, l, pl.ds(at, 8), :] for g in range(count_f)]
            weight = HALF * relax[pl.ds(to, 8), :]
            for f in range(count_f):
                total = base_two[f, l, pl.ds(to, 8), :] + speed * xdiv[f, pl.ds(to, 8), :]
                total = from_halo(total, HALO * (f * count_l + l), to)
                own_two[f, l, pl.ds(at, 8), :] = cell_terms(
                    own_one, l, f, at, centers, weight, taps, mix, total
                )
            return 0

        lax.fori_loop(0, groups, group, 0)
    for row, here in ((0, gy == 0), (rows + 8, gy == gy_count - 1)):

        @pl.when(here)
        def _(row=row):
            own_two[:, :, FIRST + row : FIRST + row + 8, :] = jnp.zeros(
                (count_f, count_l, 8, LANES), jnp.float32
            )

    for s in range(sides):
        halo_products(halo_two.at[s], None, side_matrix[s], s, 1.0, PAD, rows)
    for l in range(count_l):
        x_divergence(own_two, l, PAD, rows, own_matrix, xdiv)
        taps, mix, speed = loaded(weights, l, 1.0, count_f)

        def group(n, _):
            at = pl.multiple_of(PAD + n * 8, 8)
            to = pl.multiple_of(n * 8, 8)
            centers = [own_two[g, l, pl.ds(at, 8), :] for g in range(count_f)]
            weight = relax[pl.ds(to + 8, 8), :]
            for f in range(count_f):
                total = base_three[f, l, pl.ds(to + 8, 8), :] + speed * xdiv[f, pl.ds(to, 8), :]
                total = from_halo(total, HALO * (f * count_l + l), to)
                total = cell_terms(own_two, l, f, at, centers, weight, taps, mix, total)
                out[f, l, pl.ds(to, 8), :] = total[:, 0:cols]
            return 0

        lax.fori_loop(0, rows // 8, group, 0)


def pair_rounds(gy_count, gx_count):
    rounds = []
    for start in (0, 1):
        partner = {}
        for low in range(start, gy_count - 1, 2):
            partner[low], partner[low + 1] = low + 1, low
        pairs = []
        for y in range(gy_count):
            for x in range(gx_count):
                if y in partner:
                    pairs.append((y * gx_count + x, partner[y] * gx_count + x))
                elif gx_count % 2 == 0:
                    pairs.append((y * gx_count + x, y * gx_count + (x ^ 1)))
        rounds.append(pairs)
    return rounds


def local(
    gy_count, gx_count, fields, wind_x, wind_y, coupling, north, south, west, east, strip_scale, widths
):
    count_f, count_l, rows, cols = fields.shape
    ext_rows = rows + 2 * PAD
    grid_sizes = (gy_count, gx_count)
    packed_rows = -(-HALO * count_f * count_l // 8) * 8
    vmem = pl.BlockSpec(memory_space=pltpu.VMEM)
    smem = pl.BlockSpec(memory_space=pltpu.SMEM)
    f32 = functools.partial(jax.ShapeDtypeStruct, dtype=jnp.float32)

    def call(body, name, out_shape, inputs, scratch=(), limit=4):
        several = isinstance(out_shape, tuple)
        return pl.pallas_call(
            body,
            out_shape=out_shape,
            in_specs=[space for _, space in inputs],
            out_specs=(vmem,) * len(out_shape) if several else vmem,
            scratch_shapes=list(scratch),
            compiler_params=pltpu.CompilerParams(vmem_limit_bytes=limit << 20),
            name=name,
        )(*[value for value, _ in inputs])

    def inputs(space, *values):
        return [(value, space) for value in values]

    strip_shape = f32((packed_rows, cols))
    sent_first, sent_second = call(
        pack_y_kernel, "pack_y", (strip_shape, strip_shape), inputs(vmem, fields)
    )
    first_pairs, second_pairs = pair_rounds(gy_count, gx_count)
    first_round = lax.ppermute(sent_first, ("gy", "gx"), first_pairs)
    second_round = lax.ppermute(sent_second, ("gy", "gx"), second_pairs)

    mixing = jnp.transpose(coupling, (1, 0, 2))
    scales = jnp.transpose(strip_scale, (0, 2, 1))
    sides = 1 if gx_count == 2 else 2
    wide_rows = rows + 16
    state_shape = (count_f, count_l, ext_rows, LANES)
    wide_shape = (count_f, count_l, wide_rows, LANES)
    plane = f32((wide_rows, LANES))
    matrix = functools.partial(jax.ShapeDtypeStruct, dtype=jnp.bfloat16)
    entries = 2 * REACH + count_f * count_f + 1
    lane_entries = 2 * REACH + 2 * count_f
    prepared = call(
        functools.partial(prepare_kernel, grid_sizes),
        "prepare",
        (f32(wide_shape), plane, plane, plane)
        + (f32((count_l, entries, 8, LANES)), f32((lane_entries, 8, LANES)))
        + (matrix((count_l, LANES, LANES)),)
        + (f32((rows, LANES)),) * sides
        + (plane,) * sides
        + (matrix((2 * LANES, 2 * LANES)),) * sides,
        inputs(vmem, fields, north, south, jnp.swapaxes(west, 2, 3), jnp.swapaxes(east, 2, 3))
        + inputs(
            vmem,
            jnp.asarray(own_bands(cols), jnp.bfloat16),
            jnp.asarray(side_bands(count_f * count_l), jnp.bfloat16),
        )
        + inputs(smem, scales, widths, wind_x, wind_y, mixing),
        scratch=[pltpu.VMEM((rows, LANES), jnp.float32)],
    )
    drive, relax, row_relax, inside, weights, lane_weights, own_matrix = prepared[:7]
    payloads, side_drive, side_matrix = (
        prepared[7 + n * sides : 7 + (n + 1) * sides] for n in range(3)
    )

    sent = call(
        functools.partial(pack_x_kernel, grid_sizes),
        "pack_x",
        (f32((ext_rows, LANES)),) * sides,
        inputs(vmem, first_round, second_round, *payloads),
        scratch=[pltpu.VMEM((count_f * count_l, 2 * PAD, LANES), jnp.float32)],
    )
    forward = [(i, i + 1) for i in range(gx_count - 1)]
    backward = [(b, a) for a, b in forward]
    if sides == 1:
        halos = [lax.ppermute(sent[0], "gx", forward + backward)]
    else:
        halos = [lax.ppermute(sent[0], "gx", forward), lax.ppermute(sent[1], "gx", backward)]

    begun = call(
        functools.partial(begin_kernel, grid_sizes),
        "begin",
        (f32(wide_shape),) * 3 + (plane,) * sides,
        inputs(vmem, fields, first_round, second_round, drive, relax, weights, own_matrix),
        scratch=[
            pltpu.VMEM(state_shape, jnp.float32),
            pltpu.VMEM((count_f, wide_rows, LANES), jnp.float32),
        ],
    )
    halo_state = pltpu.VMEM((sides, ext_rows, LANES), jnp.float32)
    halo_plane = pltpu.VMEM((sides, wide_rows, LANES), jnp.float32)
    return call(
        functools.partial(finish_kernel, grid_sizes, sides),
        "finish",
        f32(fields.shape),
        inputs(vmem, *halos, *begun[3:], *side_drive, *side_matrix, *begun[:3])
        + inputs(vmem, relax, row_relax, inside, weights, lane_weights, own_matrix),
        scratch=[
            pltpu.VMEM(state_shape, jnp.float32),
            pltpu.VMEM(state_shape, jnp.float32),
            halo_state,
            halo_state,
            pltpu.VMEM((1, sides, count_l, wide_rows, LANES), jnp.float32),
            halo_plane,
            halo_plane,
            pltpu.VMEM((count_f, wide_rows, LANES), jnp.float32),
        ],
        limit=8,
    )


def solution(mesh):
    return jax.shard_map(
        functools.partial(local, mesh.shape["gy"], mesh.shape["gx"]),
        mesh=mesh,
        in_specs=(
            P("mem", None, "gy", "gx"),
            P("mem"),
            P("mem"),
            P(),
            P("mem", None, None, None),
            P("mem", None, None, None),
            P("mem", None, None, None),
            P("mem", None, None, None),
            P("mem", None, None),
            P(),
        ),
        out_specs=P("mem", None, "gy", "gx"),
        check_vma=False,
    )
```

```python
import functools

import jax
import jax.numpy as jnp
import numpy as np
from jax import lax
from jax.experimental import pallas as pl
from jax.experimental.pallas import tpu as pltpu
from jax.sharding import PartitionSpec as P

RELAX = 0.25
REACH = 3
HALO = 3 * REACH
PAD = 16
LANES = 128
FIRST = PAD - 8
THIRD, HALF = 1.0 / 3.0, 0.5

UPWIND = (-2.0, 15.0, -60.0, 20.0, 30.0, -3.0, 0.0)
CENTRAL = (-1.0, 9.0, -45.0, 0.0, 45.0, -9.0, 1.0)
DAMPING = (1.0, -6.0, 15.0, -20.0, 15.0, -6.0, 1.0)


def own_bands(cols):
    bands = np.zeros((2, LANES, LANES), np.float32)
    for col in range(cols):
        for offset in range(-REACH, REACH + 1):
            if 0 <= col + offset < cols:
                bands[0, col + offset, col] = UPWIND[offset + REACH]
                bands[1, col + offset, col] = -UPWIND[REACH - offset]
    return bands


def side_bands(count):
    bands = np.zeros((2, 2, 2 * LANES, 2 * LANES), np.float32)
    for side, (halo_at, edge_at) in enumerate(((0, -REACH), (-HALO, 0))):
        cells = [(halo_at + k, 0, k) for k in range(HALO)]
        cells += [(edge_at + k, LANES, k) for k in range(REACH)]
        for index in range(count):
            slot = index * HALO
            for source, source_half, source_lane in cells:
                for target, target_half, target_lane in cells:
                    offset = source - target
                    if abs(offset) > REACH or source_half == target_half == LANES:
                        continue
                    at = source_half + slot + source_lane, target_half + slot + target_lane
                    bands[side, 0][at] = UPWIND[offset + REACH]
                    bands[side, 1][at] = -UPWIND[REACH - offset]
    return bands


def iota(shape, dim):
    return lax.broadcasted_iota(jnp.int32, shape, dim)


def edge_weight(distance, width):
    dist = distance.astype(jnp.float32)
    inside = (dist >= 0.0) & (dist < width)
    return jnp.where(inside, jnp.square((width - dist) / width), 0.0)


def slots(count_f, count_l):
    return [(f, l, HALO * (f * count_l + l)) for f in range(count_f) for l in range(count_l)]


def pack_y_kernel(fields, first_round, second_round):
    count_f, count_l, rows, _ = fields.shape
    even = lax.rem(lax.axis_index("gy"), 2) == 0
    for f, l, slot in slots(count_f, count_l):
        top = fields[f, l, 0:HALO, :]
        bottom = fields[f, l, rows - HALO : rows, :]
        first_round[slot : slot + HALO, :] = jnp.where(even, bottom, top)
        second_round[slot : slot + HALO, :] = jnp.where(even, top, bottom)


def halo_rows(gy_count, first_round, second_round, slot):
    gy = lax.axis_index("gy")
    even = lax.rem(gy, 2) == 0
    first = first_round[slot : slot + HALO, :]
    second = second_round[slot : slot + HALO, :]
    north = jnp.where(gy == 0, 0.0, jnp.where(even, second, first))
    south = jnp.where(gy == gy_count - 1, 0.0, jnp.where(even, first, second))
    return north, south


def sent_starts(gx_count, cols):
    if gx_count == 2:
        return [jnp.where(lax.axis_index("gx") == 0, cols - HALO, 0)]
    return [cols - HALO, 0]


def side_ids(gx_count):
    if gx_count == 2:
        return [jnp.where(lax.axis_index("gx") == 0, 0, 1)]
    return [1, 0]


def edge_starts(gx_count, cols):
    return [jnp.where(side == 0, cols - REACH, 0) for side in side_ids(gx_count)]


def level_weights(coupling, wind_x, wind_y, l, count_f):
    speed, size = wind_y[l] / 60.0, jnp.abs(wind_y[l]) / 60.0
    taps = [size * DAMPING[k] - speed * CENTRAL[k] for k in range(2 * REACH + 1)]
    mix = [
        [coupling[f, l, g] + (taps[REACH] if f == g else 0.0) for g in range(count_f)]
        for f in range(count_f)
    ]
    return [tap for k, tap in enumerate(taps) if k != REACH], mix, -wind_x[l] / 60.0


def prepare_kernel(
    grid_sizes,
    fields,
    north,
    south,
    west,
    east,
    own_band,
    side_band,
    scale,
    widths,
    wind_x,
    wind_y,
    coupling,
    drive,
    relax,
    row_relax,
    inside,
    weights,
    lane_weights,
    own_matrix,
    *rest,
):
    gy_count, gx_count = grid_sizes
    sides = (len(rest) - 1) // 3
    payloads, side_drive, side_matrix = rest[:sides], rest[sides : 2 * sides], rest[2 * sides : -1]
    wide = rest[-1]
    count_f, count_l, rows, cols = fields.shape
    wide_rows = relax.shape[0]
    strip = north.shape[2]
    total_rows, total_cols = rows * gy_count, cols * gx_count
    gy, gx = lax.axis_index("gy"), lax.axis_index("gx")
    row_start, col_start = gy * rows, gx * cols
    width = [widths[s].astype(jnp.float32) for s in range(4)]
    lane = iota((8, LANES), 1)

    lane_rows = iota((rows, LANES), 1)
    starts = sent_starts(gx_count, cols)
    packed = [jnp.zeros((rows, LANES), jnp.float32) for _ in starts]
    if cols < LANES:
        wide[...] = jnp.zeros_like(wide)
    for f, l, slot in slots(count_f, count_l):
        if cols < LANES:
            wide[:, 0:cols] = fields[f, l]
            own = wide[...]
        else:
            own = fields[f, l]
        for n, start in enumerate(starts):
            moved = pltpu.roll(own, lax.rem(slot + LANES - start, LANES), 1)
            here = (lane_rows >= slot) & (lane_rows < slot + HALO)
            packed[n] = jnp.where(here, moved, packed[n])
    for payload, value in zip(payloads, packed):
        payload[...] = value

    def full(value):
        return jnp.full((8, LANES), value, jnp.float32)

    negative = jnp.zeros((1, 2 * LANES), jnp.bool_)
    double = lax.rem(iota((1, 2 * LANES), 1), LANES)
    lane_taps = [full(0.0) for _ in range(2 * REACH)]
    lane_mix = [full(0.0) for _ in range(2 * count_f - 1)]
    lane_speed = full(0.0)
    for l in range(count_l):
        taps, mix, speed = level_weights(coupling, wind_x, wind_y, l, count_f)
        flat = taps + [entry for line in mix for entry in line] + [speed]
        for n, entry in enumerate(flat):
            weights[l, n] = full(entry)
        own_matrix[l] = own_band[jnp.where(wind_x[l] < 0.0, 1, 0)]
        for f in range(count_f):
            slot = HALO * (f * count_l + l)
            here = (lane >= slot) & (lane < slot + HALO)
            lane_taps = [jnp.where(here, tap, old) for tap, old in zip(taps, lane_taps)]
            lane_speed = jnp.where(here, speed, lane_speed)
            for g in range(count_f):
                at = g - f + count_f - 1
                lane_mix[at] = jnp.where(here, mix[f][g], lane_mix[at])
            here = (double >= slot) & (double < slot + HALO)
            negative = negative | (here & (wind_x[l] < 0.0))
    for n, entry in enumerate(lane_taps + lane_mix + [lane_speed]):
        lane_weights[n] = entry
    for side, matrix in zip(side_ids(gx_count), side_matrix):
        matrix[...] = jnp.where(
            negative, side_band[side, 1].astype(jnp.float32), side_band[side, 0].astype(jnp.float32)
        ).astype(jnp.bfloat16)

    row_global = iota((wide_rows, LANES), 0) + (row_start - 8)
    row_weight = RELAX * (
        edge_weight(row_global, width[0]) + edge_weight(total_rows - 1 - row_global, width[1])
    )
    col_weight = RELAX * (
        edge_weight(lane + col_start, width[2])
        + edge_weight(total_cols - 1 - (lane + col_start), width[3])
    )
    row_relax[...] = row_weight
    relax[...] = row_weight + col_weight[0:1, :]
    inside[...] = jnp.where((row_global >= 0) & (row_global < total_rows), 1.0, 0.0)

    pos = iota((strip, LANES), 1)
    depth = iota((strip, LANES), 0)
    pick = jnp.concatenate([pos == depth, pos == depth + (cols - strip)], axis=0)
    pick = pick.astype(jnp.float32).astype(jnp.bfloat16)
    west_weight = RELAX * edge_weight(lane + col_start, width[2])
    east_weight = RELAX * edge_weight(total_cols - 1 - (lane + col_start), width[3])
    west_weight = jnp.where(lane < strip, west_weight, 0.0)
    east_weight = jnp.where((lane >= cols - strip) & (lane < cols), east_weight, 0.0)
    shift = lax.rem(8 + total_rows - row_start, total_rows)
    for f in range(count_f):
        for l in range(count_l):
            both = jnp.concatenate([west[f, l], east[f, l]], axis=0).astype(jnp.float32)
            both = pltpu.roll(both, shift, 1)[:, 0:LANES].astype(jnp.bfloat16)
            raw = lax.dot_general(
                both, pick, (((0,), (0,)), ((), ())), preferred_element_type=jnp.float32
            )
            factor = west_weight * scale[2, l, f] + east_weight * scale[3, l, f]
            drive[f, l] = raw[0:wide_rows] * factor[0:1, :]
    for ref in side_drive:
        ref[...] = jnp.zeros_like(ref)

    own_shift = lax.rem(total_cols - col_start, total_cols)
    for source, side, at, here in (
        (north, 0, 8, gy == 0),
        (south, 1, 8 + rows - strip, gy == gy_count - 1),
    ):

        @pl.when(here)
        def _(source=source, side=side, at=at):
            distance = depth if side == 0 else strip - 1 - depth
            weight = RELAX * edge_weight(distance, width[side])
            packed = [jnp.zeros((strip, LANES), jnp.float32) for _ in side_drive]
            for f, l, slot in slots(count_f, count_l):
                values = source[f, l].astype(jnp.float32)
                factor = weight * scale[side, l, f]
                own = pltpu.roll(values, own_shift, 1)[:, 0:LANES]
                drive[f, l, at : at + strip, :] = drive[f, l, at : at + strip, :] + factor * own
                for n, which in enumerate(side_ids(gx_count)):
                    begin = jnp.where(which == 0, cols, -HALO) + col_start
                    outer = pltpu.roll(
                        values, lax.rem(slot + 2 * total_cols - begin, total_cols), 1
                    )[:, 0:LANES]
                    packed[n] = jnp.where(
                        (pos >= slot) & (pos < slot + HALO), factor * outer, packed[n]
                    )
            for ref, value in zip(side_drive, packed):
                ref[at : at + strip, :] = value


def pack_x_kernel(grid_sizes, first_round, second_round, *rest):
    gy_count, gx_count = grid_sizes
    sides = (len(rest) - 1) // 2
    payloads, outs, ext = rest[:sides], rest[sides:-1], rest[-1]
    cols = first_round.shape[1]
    rows = payloads[0].shape[0]
    lane = iota((2 * PAD, LANES), 1)
    starts = sent_starts(gx_count, cols)
    packed = [jnp.zeros((2 * PAD, LANES), jnp.float32) for _ in starts]
    ext[...] = jnp.zeros_like(ext)
    for index in range(ext.shape[0]):
        slot = index * HALO
        north, south = halo_rows(gy_count, first_round, second_round, slot)
        ext[index, PAD - HALO : PAD, 0:cols] = north
        ext[index, PAD : PAD + HALO, 0:cols] = south
        for n, start in enumerate(starts):
            moved = pltpu.roll(ext[index], lax.rem(slot + LANES - start, LANES), 1)
            packed[n] = jnp.where((lane >= slot) & (lane < slot + HALO), moved, packed[n])
    for out, payload, value in zip(outs, payloads, packed):
        out[0:PAD, :] = value[0:PAD]
        out[PAD : PAD + rows, :] = payload[...]
        out[PAD + rows : 2 * PAD + rows, :] = value[PAD : 2 * PAD]


def loaded(weights, l, fac, count_f):
    flat = [fac * weights[l, n] for n in range(weights.shape[1])]
    taps, flat, speed = flat[: 2 * REACH], flat[2 * REACH : -1], flat[-1]
    return taps, [flat[f * count_f : (f + 1) * count_f] for f in range(count_f)], speed


def y_terms(rows_at, at, taps, total):
    offsets = [k for k in range(-REACH, REACH + 1) if k != 0]
    for tap, offset in zip(taps, offsets):
        total = total + tap * rows_at(at + offset)
    return total


def cell_terms(src, l, f, at, centers, weight, taps, mix, total):
    for g, center in enumerate(centers):
        total = total + (mix[f][g] - weight if g == f else mix[f][g]) * center
    return y_terms(lambda row: src[f, l, pl.ds(row, 8), :], at, taps, total)


def split(value):
    high = value.astype(jnp.bfloat16)
    return high, (value - high.astype(jnp.float32)).astype(jnp.bfloat16)


def x_divergence(src, l, first, height, matrix, xdiv):
    count_f = src.shape[0]
    whole = src[:, l, first : first + height, :].reshape(count_f * height, LANES)
    both = jnp.concatenate(split(whole), axis=1)
    twice = jnp.concatenate([matrix[l], matrix[l]], axis=0)
    moved = jnp.dot(both, twice, preferred_element_type=jnp.float32)
    xdiv[:, 0:height, :] = moved.reshape(count_f, height, LANES)


def begin_kernel(
    grid_sizes,
    fields,
    first_round,
    second_round,
    drive,
    relax,
    weights,
    own_matrix,
    part_one,
    base_two,
    base_three,
    *rest,
):
    gy_count, gx_count = grid_sizes
    edges, state, xdiv = rest[:-2], rest[-2], rest[-1]
    count_f, count_l, rows, cols = fields.shape
    wide_rows = relax.shape[0]
    pad_rows = jnp.zeros((PAD, LANES), jnp.float32)
    for f, l, slot in slots(count_f, count_l):
        north, south = halo_rows(gy_count, first_round, second_round, slot)
        if cols < LANES:
            state[f, l] = jnp.zeros(state.shape[2:], jnp.float32)
        else:
            state[f, l, 0:PAD, :] = pad_rows
            state[f, l, PAD + rows : 2 * PAD + rows, :] = pad_rows
        state[f, l, PAD - HALO : PAD, 0:cols] = north
        state[f, l, PAD : PAD + rows, 0:cols] = fields[f, l]
        state[f, l, PAD + rows : PAD + rows + HALO, 0:cols] = south
    lane = iota((wide_rows, LANES), 1)
    for edge, start in zip(edges, edge_starts(gx_count, cols)):
        packed = jnp.zeros((wide_rows, LANES), jnp.float32)
        near = (lane >= start) & (lane < start + REACH)
        for f, l, slot in slots(count_f, count_l):
            kept = jnp.where(near, state[f, l, FIRST : FIRST + wide_rows, :], 0.0)
            packed = packed + pltpu.roll(kept, lax.rem(slot + LANES - start, LANES), 1)
        edge[...] = packed
    for l in range(count_l):
        x_divergence(state, l, FIRST, wide_rows, own_matrix, xdiv)
        taps, mix, speed = loaded(weights, l, THIRD, count_f)

        def group(n, _):
            at = pl.multiple_of(FIRST + n * 8, 8)
            to = pl.multiple_of(n * 8, 8)
            centers = [state[g, l, pl.ds(at, 8), :] for g in range(count_f)]
            weight = THIRD * relax[pl.ds(to, 8), :]
            for f in range(count_f):
                forced = drive[f, l, pl.ds(to, 8), :]
                base_two[f, l, pl.ds(to, 8), :] = centers[f] + HALF * forced
                base_three[f, l, pl.ds(to, 8), :] = centers[f] + forced
                total = centers[f] + THIRD * forced + speed * xdiv[f, pl.ds(to, 8), :]
                total = cell_terms(state, l, f, at, centers, weight, taps, mix, total)
                part_one[f, l, pl.ds(to, 8), :] = total
            return 0

        lax.fori_loop(0, wide_rows // 8, group, 0, unroll=True)


def finish_kernel(grid_sizes, sides, *refs):
    gy_count, gx_count = grid_sizes
    halos, edges, side_drive, side_matrix = (
        refs[n * sides : (n + 1) * sides] for n in range(4)
    )
    (
        part_one,
        base_two,
        base_three,
        relax,
        row_relax,
        inside,
        weights,
        lane_weights,
        own_matrix,
        out,
        own_one,
        own_two,
        halo_one,
        halo_two,
        edge_next,
        halo_div,
        edge_add,
        xdiv,
    ) = refs[4 * sides :]
    count_f, count_l, rows, cols = out.shape
    wide_rows = relax.shape[0]
    groups = wide_rows // 8
    gy, gx = lax.axis_index("gy"), lax.axis_index("gx")
    starts = edge_starts(gx_count, cols)
    exists = [None] if sides == 1 else [gx > 0, gx < gx_count - 1]
    lane = iota((8, LANES), 1)
    near = [(lane >= start) & (lane < start + REACH) for start in starts]
    zeros = jnp.zeros((8, LANES), jnp.float32)

    def halo_products(halo, edge, matrix, s, fac, first, height):
        speed = lane_weights[lane_weights.shape[0] - 1][0:1, :]
        rows_in = halo[pl.ds(first, height), :]
        if edge is None:
            both = jnp.concatenate(split(rows_in), axis=0)
            moved = jnp.dot(
                both, matrix[0:LANES, LANES:], preferred_element_type=jnp.float32
            )
            add = moved[0:height] + moved[height:]
        else:
            rows_in = jnp.concatenate([rows_in, edge], axis=1)
            both = jnp.concatenate(split(rows_in), axis=0)
            moved = jnp.dot(both, matrix[...], preferred_element_type=jnp.float32)
            moved = moved[0:height] + moved[height:]
            halo_div[s] = speed * moved[:, 0:LANES]
            add = moved[:, LANES:]
        edge_add[s, 0:height, :] = (fac * speed) * add

    def halo_section(halo, halo_next, s, fac):
        count = 2 * count_f - 1
        for n in range(groups):
            at, to = FIRST + n * 8, n * 8
            center = halo[at : at + 8, :]
            rate = side_drive[s][to : to + 8, :] + halo_div[s, to : to + 8, :]
            rate = rate - row_relax[to : to + 8, :] * center
            for d in range(count):
                moved = center
                if d != count_f - 1:
                    step = (d - (count_f - 1)) * HALO * count_l
                    moved = pltpu.roll(center, -step % LANES, 1)
                rate = rate + lane_weights[2 * REACH + d] * moved
            taps = [lane_weights[k] for k in range(2 * REACH)]
            rate = y_terms(lambda row: halo[row : row + 8, :], at, taps, rate)
            value = halos[s][at : at + 8, :] + fac * rate
            kept = inside[to : to + 8, :]
            if exists[s] is not None:
                kept = jnp.where(exists[s], kept, 0.0)
            halo_next[s, at : at + 8, :] = value * kept

    def from_halo(total, slot, to):
        for s, start in enumerate(starts):
            shift = lax.rem(start + LANES - slot, LANES)
            moved = pltpu.roll(edge_add[s, pl.ds(to, 8), :], shift, 1)
            total = total + jnp.where(near[s], moved, 0.0)
        return total

    def keep_edges(packed, value, slot):
        for s, start in enumerate(starts):
            moved = pltpu.roll(
                jnp.where(near[s], value, 0.0), lax.rem(slot + LANES - start, LANES), 1
            )
            packed[s] = packed[s] + moved

    def outside_rows(own, section):
        for row, here in ((0, gy == 0), (rows + 8, gy == gy_count - 1)):

            @pl.when(here)
            def _(row=row):
                own[:, :, FIRST + row : FIRST + row + 8, :] = jnp.zeros(
                    (count_f, count_l, 8, LANES), jnp.float32
                )
                for s in range(sides):
                    for l in range(count_l):
                        edge_next[section, s, l, row : row + 8, :] = zeros

    for s in range(sides):
        halo_products(halos[s], edges[s][...], side_matrix[s], s, THIRD, FIRST, wide_rows)
        halo_section(halos[s], halo_one, s, THIRD)
    for l in range(count_l):

        def group(n, _):
            at = pl.multiple_of(FIRST + n * 8, 8)
            to = pl.multiple_of(n * 8, 8)
            packed = [zeros] * sides
            for f in range(count_f):
                slot = HALO * (f * count_l + l)
                value = from_halo(part_one[f, l, pl.ds(to, 8), :], slot, to)
                own_one[f, l, pl.ds(at, 8), :] = value
                keep_edges(packed, value, slot)
            for s in range(sides):
                edge_next[0, s, l, pl.ds(to, 8), :] = packed[s]
            return 0

        lax.fori_loop(0, groups, group, 0, unroll=True)
    outside_rows(own_one, 0)

    def edges_of(section, s):
        return sum(edge_next[section, s, l] for l in range(count_l))

    for s in range(sides):
        halo_products(
            halo_one.at[s], edges_of(0, s), side_matrix[s], s, HALF, FIRST, wide_rows
        )
        halo_section(halo_one.at[s], halo_two, s, HALF)
    for l in range(count_l):
        x_divergence(own_one, l, FIRST, wide_rows, own_matrix, xdiv)
        taps, mix, speed = loaded(weights, l, HALF, count_f)

        def group(n, _):
            at = pl.multiple_of(FIRST + n * 8, 8)
            to = pl.multiple_of(n * 8, 8)
            centers = [own_one[g, l, pl.ds(at, 8), :] for g in range(count_f)]
            weight = HALF * relax[pl.ds(to, 8), :]
            for f in range(count_f):
                total = base_two[f, l, pl.ds(to, 8), :] + speed * xdiv[f, pl.ds(to, 8), :]
                total = from_halo(total, HALO * (f * count_l + l), to)
                own_two[f, l, pl.ds(at, 8), :] = cell_terms(
                    own_one, l, f, at, centers, weight, taps, mix, total
                )
            return 0

        lax.fori_loop(0, groups, group, 0, unroll=True)
    for row, here in ((0, gy == 0), (rows + 8, gy == gy_count - 1)):

        @pl.when(here)
        def _(row=row):
            own_two[:, :, FIRST + row : FIRST + row + 8, :] = jnp.zeros(
                (count_f, count_l, 8, LANES), jnp.float32
            )

    for s in range(sides):
        halo_products(halo_two.at[s], None, side_matrix[s], s, 1.0, PAD, rows)
    for l in range(count_l):
        x_divergence(own_two, l, PAD, rows, own_matrix, xdiv)
        taps, mix, speed = loaded(weights, l, 1.0, count_f)

        def group(n, _):
            at = pl.multiple_of(PAD + n * 8, 8)
            to = pl.multiple_of(n * 8, 8)
            centers = [own_two[g, l, pl.ds(at, 8), :] for g in range(count_f)]
            weight = relax[pl.ds(to + 8, 8), :]
            for f in range(count_f):
                total = base_three[f, l, pl.ds(to + 8, 8), :] + speed * xdiv[f, pl.ds(to, 8), :]
                total = from_halo(total, HALO * (f * count_l + l), to)
                total = cell_terms(own_two, l, f, at, centers, weight, taps, mix, total)
                out[f, l, pl.ds(to, 8), :] = total[:, 0:cols]
            return 0

        lax.fori_loop(0, rows // 8, group, 0, unroll=True)


def pair_rounds(gy_count, gx_count):
    rounds = []
    for start in (0, 1):
        partner = {}
        for low in range(start, gy_count - 1, 2):
            partner[low], partner[low + 1] = low + 1, low
        pairs = []
        for y in range(gy_count):
            for x in range(gx_count):
                if y in partner:
                    pairs.append((y * gx_count + x, partner[y] * gx_count + x))
                elif gx_count % 2 == 0:
                    pairs.append((y * gx_count + x, y * gx_count + (x ^ 1)))
        rounds.append(pairs)
    return rounds


def local(
    gy_count, gx_count, fields, wind_x, wind_y, coupling, north, south, west, east, strip_scale, widths
):
    count_f, count_l, rows, cols = fields.shape
    ext_rows = rows + 2 * PAD
    grid_sizes = (gy_count, gx_count)
    packed_rows = -(-HALO * count_f * count_l // 8) * 8
    vmem = pl.BlockSpec(memory_space=pltpu.VMEM)
    smem = pl.BlockSpec(memory_space=pltpu.SMEM)
    f32 = functools.partial(jax.ShapeDtypeStruct, dtype=jnp.float32)

    def call(body, name, out_shape, inputs, scratch=(), limit=4):
        several = isinstance(out_shape, tuple)
        return pl.pallas_call(
            body,
            out_shape=out_shape,
            in_specs=[space for _, space in inputs],
            out_specs=(vmem,) * len(out_shape) if several else vmem,
            scratch_shapes=list(scratch),
            compiler_params=pltpu.CompilerParams(vmem_limit_bytes=limit << 20),
            name=name,
        )(*[value for value, _ in inputs])

    def inputs(space, *values):
        return [(value, space) for value in values]

    strip_shape = f32((packed_rows, cols))
    sent_first, sent_second = call(
        pack_y_kernel, "pack_y", (strip_shape, strip_shape), inputs(vmem, fields)
    )
    first_pairs, second_pairs = pair_rounds(gy_count, gx_count)
    first_round = lax.ppermute(sent_first, ("gy", "gx"), first_pairs)
    second_round = lax.ppermute(sent_second, ("gy", "gx"), second_pairs)

    mixing = jnp.transpose(coupling, (1, 0, 2))
    scales = jnp.transpose(strip_scale, (0, 2, 1))
    sides = 1 if gx_count == 2 else 2
    wide_rows = rows + 16
    state_shape = (count_f, count_l, ext_rows, LANES)
    wide_shape = (count_f, count_l, wide_rows, LANES)
    plane = f32((wide_rows, LANES))
    matrix = functools.partial(jax.ShapeDtypeStruct, dtype=jnp.bfloat16)
    entries = 2 * REACH + count_f * count_f + 1
    lane_entries = 2 * REACH + 2 * count_f
    prepared = call(
        functools.partial(prepare_kernel, grid_sizes),
        "prepare",
        (f32(wide_shape), plane, plane, plane)
        + (f32((count_l, entries, 8, LANES)), f32((lane_entries, 8, LANES)))
        + (matrix((count_l, LANES, LANES)),)
        + (f32((rows, LANES)),) * sides
        + (plane,) * sides
        + (matrix((2 * LANES, 2 * LANES)),) * sides,
        inputs(vmem, fields, north, south, jnp.swapaxes(west, 2, 3), jnp.swapaxes(east, 2, 3))
        + inputs(
            vmem,
            jnp.asarray(own_bands(cols), jnp.bfloat16),
            jnp.asarray(side_bands(count_f * count_l), jnp.bfloat16),
        )
        + inputs(smem, scales, widths, wind_x, wind_y, mixing),
        scratch=[pltpu.VMEM((rows, LANES), jnp.float32)],
    )
    drive, relax, row_relax, inside, weights, lane_weights, own_matrix = prepared[:7]
    payloads, side_drive, side_matrix = (
        prepared[7 + n * sides : 7 + (n + 1) * sides] for n in range(3)
    )

    sent = call(
        functools.partial(pack_x_kernel, grid_sizes),
        "pack_x",
        (f32((ext_rows, LANES)),) * sides,
        inputs(vmem, first_round, second_round, *payloads),
        scratch=[pltpu.VMEM((count_f * count_l, 2 * PAD, LANES), jnp.float32)],
    )
    forward = [(i, i + 1) for i in range(gx_count - 1)]
    backward = [(b, a) for a, b in forward]
    if sides == 1:
        halos = [lax.ppermute(sent[0], "gx", forward + backward)]
    else:
        halos = [lax.ppermute(sent[0], "gx", forward), lax.ppermute(sent[1], "gx", backward)]

    begun = call(
        functools.partial(begin_kernel, grid_sizes),
        "begin",
        (f32(wide_shape),) * 3 + (plane,) * sides,
        inputs(vmem, fields, first_round, second_round, drive, relax, weights, own_matrix),
        scratch=[
            pltpu.VMEM(state_shape, jnp.float32),
            pltpu.VMEM((count_f, wide_rows, LANES), jnp.float32),
        ],
    )
    halo_state = pltpu.VMEM((sides, ext_rows, LANES), jnp.float32)
    halo_plane = pltpu.VMEM((sides, wide_rows, LANES), jnp.float32)
    return call(
        functools.partial(finish_kernel, grid_sizes, sides),
        "finish",
        f32(fields.shape),
        inputs(vmem, *halos, *begun[3:], *side_drive, *side_matrix, *begun[:3])
        + inputs(vmem, relax, row_relax, inside, weights, lane_weights, own_matrix),
        scratch=[
            pltpu.VMEM(state_shape, jnp.float32),
            pltpu.VMEM(state_shape, jnp.float32),
            halo_state,
            halo_state,
            pltpu.VMEM((1, sides, count_l, wide_rows, LANES), jnp.float32),
            halo_plane,
            halo_plane,
            pltpu.VMEM((count_f, wide_rows, LANES), jnp.float32),
        ],
        limit=8,
    )


def solution(mesh):
    return jax.shard_map(
        functools.partial(local, mesh.shape["gy"], mesh.shape["gx"]),
        mesh=mesh,
        in_specs=(
            P("mem", None, "gy", "gx"),
            P("mem"),
            P("mem"),
            P(),
            P("mem", None, None, None),
            P("mem", None, None, None),
            P("mem", None, None, None),
            P("mem", None, None, None),
            P("mem", None, None),
            P(),
        ),
        out_specs=P("mem", None, "gy", "gx"),
        check_vma=False,
    )
```

```python
import functools

import jax
import jax.numpy as jnp
import numpy as np
from jax import lax
from jax.experimental import pallas as pl
from jax.experimental.pallas import tpu as pltpu
from jax.sharding import PartitionSpec as P

RELAX = 0.25
REACH = 3
HALO = 3 * REACH
PAD = 16
LANES = 128
FIRST = PAD - 8
THIRD, HALF = 1.0 / 3.0, 0.5

UPWIND = (-2.0, 15.0, -60.0, 20.0, 30.0, -3.0, 0.0)
CENTRAL = (-1.0, 9.0, -45.0, 0.0, 45.0, -9.0, 1.0)
DAMPING = (1.0, -6.0, 15.0, -20.0, 15.0, -6.0, 1.0)


def own_bands(cols):
    bands = np.zeros((2, LANES, LANES), np.float32)
    for col in range(cols):
        for offset in range(-REACH, REACH + 1):
            if 0 <= col + offset < cols:
                bands[0, col + offset, col] = UPWIND[offset + REACH]
                bands[1, col + offset, col] = -UPWIND[REACH - offset]
    return bands


def side_bands(count_f, count_l):
    bands = np.zeros((2, 2**count_l, 3 * LANES, 2 * LANES), np.float32)
    for side, starts in enumerate(((0, -HALO, -HALO - REACH), (-HALO, 0, HALO))):
        cells = [
            (start + k, part * LANES + k)
            for part, start in enumerate(starts)
            for k in range(REACH if part == 2 else HALO)
        ]
        pairs = [
            (at, to, col - target)
            for col, at in cells
            for target, to in cells
            if abs(col - target) <= REACH and to < 2 * LANES
        ]
        for f in range(count_f):
            for l in range(count_l):
                slot = HALO * (f * count_l + l)
                for choice in range(2**count_l):
                    for at, to, offset in pairs:
                        value = UPWIND[offset + REACH]
                        if choice >> l & 1:
                            value = -UPWIND[REACH - offset]
                        bands[side, choice, at + slot, to + slot] = value
    return bands


def iota(shape, dim):
    return lax.broadcasted_iota(jnp.int32, shape, dim)


def edge_weight(distance, width):
    dist = distance.astype(jnp.float32)
    inside = (dist >= 0.0) & (dist < width)
    return jnp.where(inside, jnp.square((width - dist) / width), 0.0)


def slots(count_f, count_l):
    return [(f, l, HALO * (f * count_l + l)) for f in range(count_f) for l in range(count_l)]


def pack_y_kernel(fields, first_round, second_round):
    count_f, count_l, rows, _ = fields.shape
    even = lax.rem(lax.axis_index("gy"), 2) == 0
    for f, l, slot in slots(count_f, count_l):
        top = fields[f, l, 0:HALO, :]
        bottom = fields[f, l, rows - HALO : rows, :]
        first_round[slot : slot + HALO, :] = jnp.where(even, bottom, top)
        second_round[slot : slot + HALO, :] = jnp.where(even, top, bottom)


def halo_rows(gy_count, first_round, second_round, slot):
    gy = lax.axis_index("gy")
    even = lax.rem(gy, 2) == 0
    first = first_round[slot : slot + HALO, :]
    second = second_round[slot : slot + HALO, :]
    north = jnp.where(gy == 0, 0.0, jnp.where(even, second, first))
    south = jnp.where(gy == gy_count - 1, 0.0, jnp.where(even, first, second))
    return north, south


def sent_starts(gx_count, cols):
    if gx_count == 2:
        return [jnp.where(lax.axis_index("gx") == 0, cols - HALO, 0)]
    return [cols - HALO, 0]


def side_ids(gx_count):
    if gx_count == 2:
        return [jnp.where(lax.axis_index("gx") == 0, 0, 1)]
    return [1, 0]


def edge_starts(gx_count, cols):
    near = [jnp.where(side == 0, cols - HALO, 0) for side in side_ids(gx_count)]
    far = [jnp.where(side == 0, cols - HALO - REACH, HALO) for side in side_ids(gx_count)]
    return near, far


def level_weights(coupling, wind_x, wind_y, l, count_f):
    speed, size = wind_y[l] / 60.0, jnp.abs(wind_y[l]) / 60.0
    taps = [size * DAMPING[k] - speed * CENTRAL[k] for k in range(2 * REACH + 1)]
    mix = [
        [coupling[f, l, g] + (taps[REACH] if f == g else 0.0) for g in range(count_f)]
        for f in range(count_f)
    ]
    return [tap for k, tap in enumerate(taps) if k != REACH], mix, -wind_x[l] / 60.0


def prepare_kernel(
    grid_sizes,
    fields,
    north,
    south,
    west,
    east,
    own_band,
    side_band,
    scale,
    widths,
    wind_x,
    wind_y,
    coupling,
    drive,
    relax,
    row_relax,
    inside,
    weights,
    lane_weights,
    own_matrix,
    *rest,
):
    gy_count, gx_count = grid_sizes
    sides = (len(rest) - 2) // 3
    payloads, side_drive, side_matrix = rest[:sides], rest[sides : 2 * sides], rest[2 * sides : -2]
    wide, arrived = rest[-2:]
    choice = sum(jnp.where(wind_x[l] < 0.0, 2**l, 0) for l in range(fields.shape[1]))
    copies = [
        pltpu.make_async_copy(side_band.at[side, choice], matrix, arrived.at[n])
        for n, (side, matrix) in enumerate(zip(side_ids(gx_count), side_matrix))
    ]
    for copy in copies:
        copy.start()
    count_f, count_l, rows, cols = fields.shape
    wide_rows = relax.shape[0]
    strip = north.shape[2]
    total_rows, total_cols = rows * gy_count, cols * gx_count
    gy, gx = lax.axis_index("gy"), lax.axis_index("gx")
    row_start, col_start = gy * rows, gx * cols
    width = [widths[s].astype(jnp.float32) for s in range(4)]
    lane = iota((8, LANES), 1)

    lane_rows = iota((rows, LANES), 1)
    starts = sent_starts(gx_count, cols)
    packed = [jnp.zeros((rows, LANES), jnp.float32) for _ in starts]
    if cols < LANES:
        wide[...] = jnp.zeros_like(wide)
    for f, l, slot in slots(count_f, count_l):
        if cols < LANES:
            wide[:, 0:cols] = fields[f, l]
            own = wide[...]
        else:
            own = fields[f, l]
        for n, start in enumerate(starts):
            moved = pltpu.roll(own, lax.rem(slot + LANES - start, LANES), 1)
            here = (lane_rows >= slot) & (lane_rows < slot + HALO)
            packed[n] = jnp.where(here, moved, packed[n])
    for payload, value in zip(payloads, packed):
        payload[...] = value

    def full(value):
        return jnp.full((8, LANES), value, jnp.float32)

    lane_taps = [full(0.0) for _ in range(2 * REACH)]
    lane_mix = [full(0.0) for _ in range(2 * count_f - 1)]
    lane_speed = full(0.0)
    for l in range(count_l):
        taps, mix, speed = level_weights(coupling, wind_x, wind_y, l, count_f)
        flat = taps + [entry for line in mix for entry in line] + [speed]
        for n, entry in enumerate(flat):
            weights[l, n] = full(entry)
        own_matrix[l] = own_band[jnp.where(wind_x[l] < 0.0, 1, 0)]
        for f in range(count_f):
            slot = HALO * (f * count_l + l)
            here = (lane >= slot) & (lane < slot + HALO)
            lane_taps = [jnp.where(here, tap, old) for tap, old in zip(taps, lane_taps)]
            lane_speed = jnp.where(here, speed, lane_speed)
            for g in range(count_f):
                at = g - f + count_f - 1
                lane_mix[at] = jnp.where(here, mix[f][g], lane_mix[at])
    for n, entry in enumerate(lane_taps + lane_mix + [lane_speed]):
        lane_weights[n] = entry

    row_global = iota((wide_rows, LANES), 0) + (row_start - 8)
    row_weight = RELAX * (
        edge_weight(row_global, width[0]) + edge_weight(total_rows - 1 - row_global, width[1])
    )
    col_weight = RELAX * (
        edge_weight(lane + col_start, width[2])
        + edge_weight(total_cols - 1 - (lane + col_start), width[3])
    )
    row_relax[...] = row_weight
    relax[...] = row_weight + col_weight[0:1, :]
    inside[...] = jnp.where((row_global >= 0) & (row_global < total_rows), 1.0, 0.0)

    pos = iota((strip, LANES), 1)
    depth = iota((strip, LANES), 0)
    pick = jnp.concatenate([pos == depth, pos == depth + (cols - strip)], axis=0)
    pick = pick.astype(jnp.float32).astype(jnp.bfloat16)
    west_weight = RELAX * edge_weight(lane + col_start, width[2])
    east_weight = RELAX * edge_weight(total_cols - 1 - (lane + col_start), width[3])
    west_weight = jnp.where(lane < strip, west_weight, 0.0)
    east_weight = jnp.where((lane >= cols - strip) & (lane < cols), east_weight, 0.0)
    shift = lax.rem(8 + total_rows - row_start, total_rows)
    for f in range(count_f):
        for l in range(count_l):
            both = jnp.concatenate([west[f, l], east[f, l]], axis=0).astype(jnp.float32)
            both = pltpu.roll(both, shift, 1)[:, 0:LANES].astype(jnp.bfloat16)
            raw = lax.dot_general(
                both, pick, (((0,), (0,)), ((), ())), preferred_element_type=jnp.float32
            )
            factor = west_weight * scale[2, l, f] + east_weight * scale[3, l, f]
            drive[f, l] = raw[0:wide_rows] * factor[0:1, :]
    for ref in side_drive:
        ref[...] = jnp.zeros_like(ref)

    own_shift = lax.rem(total_cols - col_start, total_cols)
    for source, side, at, here in (
        (north, 0, 8, gy == 0),
        (south, 1, 8 + rows - strip, gy == gy_count - 1),
    ):

        @pl.when(here)
        def _(source=source, side=side, at=at):
            distance = depth if side == 0 else strip - 1 - depth
            weight = RELAX * edge_weight(distance, width[side])
            packed = [[jnp.zeros((strip, LANES), jnp.float32)] * 2 for _ in side_drive]
            for f, l, slot in slots(count_f, count_l):
                values = source[f, l].astype(jnp.float32)
                factor = weight * scale[side, l, f]
                own = pltpu.roll(values, own_shift, 1)[:, 0:LANES]
                drive[f, l, at : at + strip, :] = drive[f, l, at : at + strip, :] + factor * own
                held = (pos >= slot) & (pos < slot + HALO)
                for n, which in enumerate(side_ids(gx_count)):
                    for part, begin in enumerate(
                        (jnp.where(which == 0, cols, -HALO), jnp.where(which == 0, cols - HALO, 0))
                    ):
                        shift = slot + 2 * total_cols - begin - col_start
                        moved = pltpu.roll(values, lax.rem(shift, total_cols), 1)[:, 0:LANES]
                        packed[n][part] = jnp.where(held, factor * moved, packed[n][part])
            for ref, value in zip(side_drive, packed):
                for part in range(2):
                    ref[part, at : at + strip, :] = value[part]

    for copy in copies:
        copy.wait()


def pack_x_kernel(grid_sizes, first_round, second_round, *rest):
    gy_count, gx_count = grid_sizes
    sides = (len(rest) - 1) // 2
    payloads, outs, ext = rest[:sides], rest[sides:-1], rest[-1]
    cols = first_round.shape[1]
    rows = payloads[0].shape[0]
    lane = iota((2 * PAD, LANES), 1)
    starts = sent_starts(gx_count, cols)
    packed = [jnp.zeros((2 * PAD, LANES), jnp.float32) for _ in starts]
    ext[...] = jnp.zeros_like(ext)
    for index in range(ext.shape[0]):
        slot = index * HALO
        north, south = halo_rows(gy_count, first_round, second_round, slot)
        ext[index, PAD - HALO : PAD, 0:cols] = north
        ext[index, PAD : PAD + HALO, 0:cols] = south
        for n, start in enumerate(starts):
            moved = pltpu.roll(ext[index], lax.rem(slot + LANES - start, LANES), 1)
            packed[n] = jnp.where((lane >= slot) & (lane < slot + HALO), moved, packed[n])
    for out, payload, value in zip(outs, payloads, packed):
        out[0:PAD, :] = value[0:PAD]
        out[PAD : PAD + rows, :] = payload[...]
        out[PAD + rows : 2 * PAD + rows, :] = value[PAD : 2 * PAD]


def loaded(weights, l, fac, count_f):
    flat = [fac * weights[l, n] for n in range(weights.shape[1])]
    taps, flat, speed = flat[: 2 * REACH], flat[2 * REACH : -1], flat[-1]
    return taps, [flat[f * count_f : (f + 1) * count_f] for f in range(count_f)], speed


def y_terms(rows_at, at, taps, total):
    offsets = [k for k in range(-REACH, REACH + 1) if k != 0]
    for tap, offset in zip(taps, offsets):
        total = total + tap * rows_at(at + offset)
    return total


def cell_terms(src, l, f, at, centers, weight, taps, mix, total):
    for g, center in enumerate(centers):
        total = total + (mix[f][g] - weight if g == f else mix[f][g]) * center
    return y_terms(lambda row: src[f, l, pl.ds(row, 8), :], at, taps, total)


def split(value):
    high = value.astype(jnp.bfloat16)
    return high, (value - high.astype(jnp.float32)).astype(jnp.bfloat16)


def x_divergence(src, l, first, height, matrix, xdiv):
    count_f = src.shape[0]
    whole = src[:, l, first : first + height, :].reshape(count_f * height, LANES)
    both = jnp.concatenate(split(whole), axis=1)
    twice = jnp.concatenate([matrix[l], matrix[l]], axis=0)
    moved = jnp.dot(both, twice, preferred_element_type=jnp.float32)
    xdiv[:, 0:height, :] = moved.reshape(count_f, height, LANES)


def begin_kernel(
    grid_sizes,
    fields,
    first_round,
    second_round,
    drive,
    relax,
    weights,
    own_matrix,
    after,
    *rest,
):
    gy_count, gx_count = grid_sizes
    far, (state, own_one, own_two, xdiv) = rest[:-4], rest[-4:]
    count_f, count_l, rows, cols = fields.shape
    wide_rows = relax.shape[0]
    gy = lax.axis_index("gy")
    pad_rows = jnp.zeros((PAD, LANES), jnp.float32)
    for f, l, slot in slots(count_f, count_l):
        north, south = halo_rows(gy_count, first_round, second_round, slot)
        if cols < LANES:
            state[f, l] = jnp.zeros(state.shape[2:], jnp.float32)
        else:
            state[f, l, 0:PAD, :] = pad_rows
            state[f, l, PAD + rows : 2 * PAD + rows, :] = pad_rows
        state[f, l, PAD - HALO : PAD, 0:cols] = north
        state[f, l, PAD : PAD + rows, 0:cols] = fields[f, l]
        state[f, l, PAD + rows : PAD + rows + HALO, 0:cols] = south
    lane = iota((wide_rows, LANES), 1)
    starts = edge_starts(gx_count, cols)[1]

    def keep_far(src, section):
        for ref, start in zip(far, starts):
            packed = jnp.zeros((wide_rows, LANES), jnp.float32)
            here = (lane >= start) & (lane < start + REACH)
            for f, l, slot in slots(count_f, count_l):
                kept = jnp.where(here, src[f, l, FIRST : FIRST + wide_rows, :], 0.0)
                packed = packed + pltpu.roll(kept, lax.rem(slot + LANES - start, LANES), 1)
            ref[section] = packed

    keep_far(state, 0)
    for section, (src, dst, fac) in enumerate(
        ((state, own_one, THIRD), (own_one, own_two, HALF), (own_two, after, 1.0))
    ):
        first, height = (PAD, rows) if dst is after else (FIRST, wide_rows)
        for l in range(count_l):
            x_divergence(src, l, first, height, own_matrix, xdiv)
            taps, mix, speed = loaded(weights, l, fac, count_f)
            for n in range(height // 8):
                at, row = first + n * 8, n * 8
                to = at - FIRST
                centers = [src[g, l, at : at + 8, :] for g in range(count_f)]
                weight = fac * relax[to : to + 8, :]
                for f in range(count_f):
                    base = centers[f] if src is state else state[f, l, at : at + 8, :]
                    total = base + fac * drive[f, l, to : to + 8, :]
                    total = total + speed * xdiv[f, row : row + 8, :]
                    total = cell_terms(src, l, f, at, centers, weight, taps, mix, total)
                    if dst is after:
                        after[f, l, row : row + 8, :] = total[:, 0:cols]
                    else:
                        dst[f, l, at : at + 8, :] = total
        if dst is not after:
            for row, here in ((FIRST, gy == 0), (PAD + rows, gy == gy_count - 1)):

                @pl.when(here)
                def _(dst=dst, row=row):
                    dst[:, :, row : row + 8, :] = jnp.zeros(
                        (count_f, count_l, 8, LANES), jnp.float32
                    )

            keep_far(dst, section + 1)


def finish_kernel(grid_sizes, sides, *refs):
    gy_count, gx_count = grid_sizes
    halos, edges, fars, side_drive, side_matrix = (
        refs[n * sides : (n + 1) * sides] for n in range(5)
    )
    after, row_relax, inside, lane_weights, out, one, two, xdiv = refs[5 * sides :]
    count_f, count_l, rows, cols = out.shape
    wide_rows = row_relax.shape[0]
    gx = lax.axis_index("gx")
    starts = edge_starts(gx_count, cols)[0]
    exists = [None] if sides == 1 else [gx > 0, gx < gx_count - 1]
    taps = [lane_weights[k] for k in range(2 * REACH)]
    mix = [lane_weights[2 * REACH + d] for d in range(2 * count_f - 1)]
    speed = lane_weights[lane_weights.shape[0] - 1]

    def section(parts, s, fac, number, first, height, wanted, store):
        columns = [part[first : first + height, :] for part in parts]
        columns.append(fars[s][number, first - FIRST : first - FIRST + height, :])
        both = jnp.concatenate(split(jnp.concatenate(columns, axis=1)), axis=0)
        moved = jnp.dot(
            both, side_matrix[s][:, wanted[0] * LANES :], preferred_element_type=jnp.float32
        )
        moved = moved[0:height] + moved[height:]
        for n, which in enumerate(wanted):
            xdiv[which, 0:height, :] = moved[:, n * LANES : (n + 1) * LANES]
        for which in wanted:
            part, start = parts[which], (halos, edges)[which][s]
            for n in range(height // 8):
                at, row = first + n * 8, n * 8
                to = at - FIRST
                center = part[at : at + 8, :]
                rate = side_drive[s][which, to : to + 8, :] + speed * xdiv[which, row : row + 8, :]
                rate = rate - row_relax[to : to + 8, :] * center
                for d, entry in enumerate(mix):
                    step = (d - (count_f - 1)) * HALO * count_l
                    other = pltpu.roll(center, -step % LANES, 1) if step else center
                    rate = rate + entry * other
                rate = y_terms(lambda row: part[row : row + 8, :], at, taps, rate)
                store(which, at, to, start[at : at + 8, :] + fac * rate)

    lane = iota((rows, LANES), 1)
    for s in range(sides):
        def keep(ref):
            def store(which, at, to, value):
                kept = inside[to : to + 8, :]
                if exists[s] is not None and which == 0:
                    kept = jnp.where(exists[s], kept, 0.0)
                ref[which, at : at + 8, :] = value * kept

            return store

        section((halos[s], edges[s]), s, THIRD, 0, FIRST, wide_rows, (0, 1), keep(one))
        section((one.at[0], one.at[1]), s, HALF, 1, FIRST, wide_rows, (0, 1), keep(two))

        def last(which, at, to, value):
            one[0, at : at + 8, :] = value

        section((two.at[0], two.at[1]), s, 1.0, 2, PAD, rows, (1,), last)
        right = one[0, PAD : PAD + rows, :]
        near = (lane >= starts[s]) & (lane < starts[s] + HALO)
        if exists[s] is not None:
            near = near & exists[s]
        source = after if s == 0 else out
        for f, l, slot in slots(count_f, count_l):
            moved = pltpu.roll(right, lax.rem(starts[s] + LANES - slot, LANES), 1)
            out[f, l] = jnp.where(near[:, 0:cols], moved[:, 0:cols], source[f, l])


def pair_rounds(gy_count, gx_count):
    rounds = []
    for start in (0, 1):
        partner = {}
        for low in range(start, gy_count - 1, 2):
            partner[low], partner[low + 1] = low + 1, low
        pairs = []
        for y in range(gy_count):
            for x in range(gx_count):
                if y in partner:
                    pairs.append((y * gx_count + x, partner[y] * gx_count + x))
                elif gx_count % 2 == 0:
                    pairs.append((y * gx_count + x, y * gx_count + (x ^ 1)))
        rounds.append(pairs)
    return rounds


def local(
    gy_count, gx_count, fields, wind_x, wind_y, coupling, north, south, west, east, strip_scale, widths
):
    count_f, count_l, rows, cols = fields.shape
    ext_rows = rows + 2 * PAD
    grid_sizes = (gy_count, gx_count)
    packed_rows = -(-HALO * count_f * count_l // 8) * 8
    vmem = pl.BlockSpec(memory_space=pltpu.VMEM)
    smem = pl.BlockSpec(memory_space=pltpu.SMEM)
    f32 = functools.partial(jax.ShapeDtypeStruct, dtype=jnp.float32)

    def call(body, name, out_shape, inputs, scratch=(), limit=4):
        several = isinstance(out_shape, tuple)
        return pl.pallas_call(
            body,
            out_shape=out_shape,
            in_specs=[space for _, space in inputs],
            out_specs=(vmem,) * len(out_shape) if several else vmem,
            scratch_shapes=list(scratch),
            compiler_params=pltpu.CompilerParams(vmem_limit_bytes=limit << 20),
            name=name,
        )(*[value for value, _ in inputs])

    def inputs(space, *values):
        return [(value, space) for value in values]

    strip_shape = f32((packed_rows, cols))
    sent_first, sent_second = call(
        pack_y_kernel, "pack_y", (strip_shape, strip_shape), inputs(vmem, fields)
    )
    first_pairs, second_pairs = pair_rounds(gy_count, gx_count)
    first_round = lax.ppermute(sent_first, ("gy", "gx"), first_pairs)
    second_round = lax.ppermute(sent_second, ("gy", "gx"), second_pairs)

    mixing = jnp.transpose(coupling, (1, 0, 2))
    scales = jnp.transpose(strip_scale, (0, 2, 1))
    sides = 1 if gx_count == 2 else 2
    wide_rows = rows + 16
    state_shape = (count_f, count_l, ext_rows, LANES)
    wide_shape = (count_f, count_l, wide_rows, LANES)
    plane = f32((wide_rows, LANES))
    matrix = functools.partial(jax.ShapeDtypeStruct, dtype=jnp.bfloat16)
    entries = 2 * REACH + count_f * count_f + 1
    lane_entries = 2 * REACH + 2 * count_f
    prepared = call(
        functools.partial(prepare_kernel, grid_sizes),
        "prepare",
        (f32(wide_shape), plane, plane, plane)
        + (f32((count_l, entries, 8, LANES)), f32((lane_entries, 8, LANES)))
        + (matrix((count_l, LANES, LANES)),)
        + (f32((rows, LANES)),) * sides
        + (f32((2, wide_rows, LANES)),) * sides
        + (matrix((3 * LANES, 2 * LANES)),) * sides,
        inputs(vmem, fields, north, south, jnp.swapaxes(west, 2, 3), jnp.swapaxes(east, 2, 3))
        + inputs(vmem, jnp.asarray(own_bands(cols), jnp.bfloat16))
        + inputs(
            pl.BlockSpec(memory_space=pltpu.HBM),
            jnp.asarray(side_bands(count_f, count_l), jnp.bfloat16),
        )
        + inputs(smem, scales, widths, wind_x, wind_y, mixing),
        scratch=[pltpu.VMEM((rows, LANES), jnp.float32), pltpu.SemaphoreType.DMA((sides,))],
    )
    drive, relax, row_relax, inside, weights, lane_weights, own_matrix = prepared[:7]
    payloads, side_drive, side_matrix = (
        prepared[7 + n * sides : 7 + (n + 1) * sides] for n in range(3)
    )

    sent = call(
        functools.partial(pack_x_kernel, grid_sizes),
        "pack_x",
        (f32((ext_rows, LANES)),) * sides,
        inputs(vmem, first_round, second_round, *payloads),
        scratch=[pltpu.VMEM((count_f * count_l, 2 * PAD, LANES), jnp.float32)],
    )
    forward = [(i, i + 1) for i in range(gx_count - 1)]
    backward = [(b, a) for a, b in forward]
    if sides == 1:
        halos = [lax.ppermute(sent[0], "gx", forward + backward)]
    else:
        halos = [lax.ppermute(sent[0], "gx", forward), lax.ppermute(sent[1], "gx", backward)]

    state = pltpu.VMEM(state_shape, jnp.float32)
    after, *far = call(
        functools.partial(begin_kernel, grid_sizes),
        "begin",
        (f32(fields.shape),) + (f32((3, wide_rows, LANES)),) * sides,
        inputs(vmem, fields, first_round, second_round, drive, relax, weights, own_matrix),
        scratch=[state] * 3 + [pltpu.VMEM((count_f, wide_rows, LANES), jnp.float32)],
        limit=8,
    )
    pair = pltpu.VMEM((2, ext_rows, LANES), jnp.float32)
    return call(
        functools.partial(finish_kernel, grid_sizes, sides),
        "finish",
        f32(fields.shape),
        inputs(vmem, *halos, *sent[::-1], *far, *side_drive, *side_matrix)
        + inputs(vmem, after, row_relax, inside, lane_weights),
        scratch=[pair, pair, pltpu.VMEM((2, wide_rows, LANES), jnp.float32)],
    )


def solution(mesh):
    return jax.shard_map(
        functools.partial(local, mesh.shape["gy"], mesh.shape["gx"]),
        mesh=mesh,
        in_specs=(
            P("mem", None, "gy", "gx"),
            P("mem"),
            P("mem"),
            P(),
            P("mem", None, None, None),
            P("mem", None, None, None),
            P("mem", None, None, None),
            P("mem", None, None, None),
            P("mem", None, None),
            P(),
        ),
        out_specs=P("mem", None, "gy", "gx"),
        check_vma=False,
    )
```

```python
import functools

import jax
import jax.numpy as jnp
import numpy as np
from jax import lax
from jax.experimental import pallas as pl
from jax.experimental.pallas import tpu as pltpu
from jax.sharding import PartitionSpec as P

RELAX = 0.25
REACH = 3
HALO = 3 * REACH
PAD = 16
LANES = 128
FIRST = PAD - 8
THIRD, HALF = 1.0 / 3.0, 0.5

UPWIND = (-2.0, 15.0, -60.0, 20.0, 30.0, -3.0, 0.0)
CENTRAL = (-1.0, 9.0, -45.0, 0.0, 45.0, -9.0, 1.0)
DAMPING = (1.0, -6.0, 15.0, -20.0, 15.0, -6.0, 1.0)


def own_bands(cols):
    bands = np.zeros((2, LANES, LANES), np.float32)
    for col in range(cols):
        for offset in range(-REACH, REACH + 1):
            if 0 <= col + offset < cols:
                bands[0, col + offset, col] = UPWIND[offset + REACH]
                bands[1, col + offset, col] = -UPWIND[REACH - offset]
    return bands


def iota(shape, dim):
    return lax.broadcasted_iota(jnp.int32, shape, dim)


def edge_weight(distance, width):
    dist = distance.astype(jnp.float32)
    inside = (dist >= 0.0) & (dist < width)
    return jnp.where(inside, jnp.square((width - dist) / width), 0.0)


def slots(count_f, count_l):
    return [(f, l, HALO * (f * count_l + l)) for f in range(count_f) for l in range(count_l)]


def pack_y_kernel(fields, first_round, second_round):
    count_f, count_l, rows, _ = fields.shape
    even = lax.rem(lax.axis_index("gy"), 2) == 0
    for f, l, slot in slots(count_f, count_l):
        top = fields[f, l, 0:HALO, :]
        bottom = fields[f, l, rows - HALO : rows, :]
        first_round[slot : slot + HALO, :] = jnp.where(even, bottom, top)
        second_round[slot : slot + HALO, :] = jnp.where(even, top, bottom)


def halo_rows(gy_count, first_round, second_round, slot):
    gy = lax.axis_index("gy")
    even = lax.rem(gy, 2) == 0
    first = first_round[slot : slot + HALO, :]
    second = second_round[slot : slot + HALO, :]
    north = jnp.where(gy == 0, 0.0, jnp.where(even, second, first))
    south = jnp.where(gy == gy_count - 1, 0.0, jnp.where(even, first, second))
    return north, south


def sent_starts(gx_count, cols):
    if gx_count == 2:
        return [jnp.where(lax.axis_index("gx") == 0, cols - HALO, 0)]
    return [cols - HALO, 0]


def side_ids(gx_count):
    if gx_count == 2:
        return [jnp.where(lax.axis_index("gx") == 0, 0, 1)]
    return [1, 0]


def edge_starts(gx_count, cols):
    near = [jnp.where(side == 0, cols - HALO, 0) for side in side_ids(gx_count)]
    far = [jnp.where(side == 0, cols - HALO - REACH, HALO) for side in side_ids(gx_count)]
    return near, far


def level_weights(coupling, wind_x, wind_y, l, count_f):
    speed, size = wind_y[l] / 60.0, jnp.abs(wind_y[l]) / 60.0
    taps = [size * DAMPING[k] - speed * CENTRAL[k] for k in range(2 * REACH + 1)]
    mix = [
        [coupling[f, l, g] + (taps[REACH] if f == g else 0.0) for g in range(count_f)]
        for f in range(count_f)
    ]
    return [tap for k, tap in enumerate(taps) if k != REACH], mix, -wind_x[l] / 60.0


def side_bands(side, lane_speed, matrix):
    shape = (LANES, LANES)
    row, col = iota(shape, 0), iota(shape, 1)
    row_plane, col_plane = (row * 57) >> 9, (col * 57) >> 9
    apart = (row - HALO * row_plane) - (col - HALO * col_plane)
    apart = jnp.where(row_plane == col_plane, apart, 4 * HALO)
    sign = jnp.where(lane_speed > 0.0, -1, 1)
    sign_float = sign.astype(jnp.float32)

    def block(base):
        offset = (apart + base) * sign
        value = jnp.zeros(shape, jnp.float32)
        for k, entry in enumerate(UPWIND[:-1]):
            value = jnp.where(offset == k - REACH, entry, value)
        return (value * sign_float).astype(jnp.bfloat16)

    here, step = block(0), jnp.where(side == 0, HALO, -HALO)
    matrix[0:LANES, 0:LANES] = here
    matrix[LANES : 2 * LANES, LANES:] = here
    matrix[LANES : 2 * LANES, 0:LANES] = block(-step)
    matrix[0:LANES, LANES:] = block(step)
    matrix[2 * LANES :, 0:LANES] = jnp.zeros(shape, jnp.bfloat16)
    matrix[2 * LANES :, LANES:] = block(jnp.where(side == 0, -REACH, HALO))


def prepare_kernel(
    grid_sizes,
    fields,
    north,
    south,
    west,
    east,
    own_band,
    scale,
    widths,
    wind_x,
    wind_y,
    coupling,
    drive,
    relax,
    row_relax,
    inside,
    weights,
    lane_weights,
    own_matrix,
    *rest,
):
    gy_count, gx_count = grid_sizes
    sides = (len(rest) - 1) // 3
    payloads, side_drive, side_matrix = rest[:sides], rest[sides : 2 * sides], rest[2 * sides : -1]
    wide = rest[-1]
    count_f, count_l, rows, cols = fields.shape
    wide_rows = relax.shape[0]
    strip = north.shape[2]
    total_rows, total_cols = rows * gy_count, cols * gx_count
    gy, gx = lax.axis_index("gy"), lax.axis_index("gx")
    row_start, col_start = gy * rows, gx * cols
    width = [widths[s].astype(jnp.float32) for s in range(4)]
    lane = iota((8, LANES), 1)

    lane_rows = iota((rows, LANES), 1)
    starts = sent_starts(gx_count, cols)
    packed = [jnp.zeros((rows, LANES), jnp.float32) for _ in starts]
    if cols < LANES:
        wide[...] = jnp.zeros_like(wide)
    for f, l, slot in slots(count_f, count_l):
        if cols < LANES:
            wide[:, 0:cols] = fields[f, l]
            own = wide[...]
        else:
            own = fields[f, l]
        for n, start in enumerate(starts):
            moved = pltpu.roll(own, lax.rem(slot + LANES - start, LANES), 1)
            here = (lane_rows >= slot) & (lane_rows < slot + HALO)
            packed[n] = jnp.where(here, moved, packed[n])
    for payload, value in zip(payloads, packed):
        payload[...] = value

    def full(value):
        return jnp.full((8, LANES), value, jnp.float32)

    lane_taps = [full(0.0) for _ in range(2 * REACH)]
    lane_mix = [full(0.0) for _ in range(2 * count_f - 1)]
    lane_speed = full(0.0)
    for l in range(count_l):
        taps, mix, speed = level_weights(coupling, wind_x, wind_y, l, count_f)
        flat = taps + [entry for line in mix for entry in line] + [speed]
        for n, entry in enumerate(flat):
            weights[l, n] = full(entry)
        own_matrix[l] = own_band[jnp.where(wind_x[l] < 0.0, 1, 0)]
        for f in range(count_f):
            slot = HALO * (f * count_l + l)
            here = (lane >= slot) & (lane < slot + HALO)
            lane_taps = [jnp.where(here, tap, old) for tap, old in zip(taps, lane_taps)]
            lane_speed = jnp.where(here, speed, lane_speed)
            for g in range(count_f):
                at = g - f + count_f - 1
                lane_mix[at] = jnp.where(here, mix[f][g], lane_mix[at])
    for n, entry in enumerate(lane_taps + lane_mix + [lane_speed]):
        lane_weights[n] = entry
    for side, matrix in zip(side_ids(gx_count), side_matrix):
        side_bands(side, lane_speed[0:1, :], matrix)

    row_global = iota((wide_rows, LANES), 0) + (row_start - 8)
    row_weight = RELAX * (
        edge_weight(row_global, width[0]) + edge_weight(total_rows - 1 - row_global, width[1])
    )
    col_weight = RELAX * (
        edge_weight(lane + col_start, width[2])
        + edge_weight(total_cols - 1 - (lane + col_start), width[3])
    )
    row_relax[...] = row_weight
    relax[...] = row_weight + col_weight[0:1, :]
    inside[...] = jnp.where((row_global >= 0) & (row_global < total_rows), 1.0, 0.0)

    pos = iota((strip, LANES), 1)
    depth = iota((strip, LANES), 0)
    pick = jnp.concatenate([pos == depth, pos == depth + (cols - strip)], axis=0)
    pick = pick.astype(jnp.float32).astype(jnp.bfloat16)
    west_weight = RELAX * edge_weight(lane + col_start, width[2])
    east_weight = RELAX * edge_weight(total_cols - 1 - (lane + col_start), width[3])
    west_weight = jnp.where(lane < strip, west_weight, 0.0)
    east_weight = jnp.where((lane >= cols - strip) & (lane < cols), east_weight, 0.0)
    shift = lax.rem(8 + total_rows - row_start, total_rows)
    for f in range(count_f):
        for l in range(count_l):
            both = jnp.concatenate([west[f, l], east[f, l]], axis=0).astype(jnp.float32)
            both = pltpu.roll(both, shift, 1)[:, 0:LANES].astype(jnp.bfloat16)
            raw = lax.dot_general(
                both, pick, (((0,), (0,)), ((), ())), preferred_element_type=jnp.float32
            )
            factor = west_weight * scale[2, l, f] + east_weight * scale[3, l, f]
            drive[f, l] = raw[0:wide_rows] * factor[0:1, :]
    for ref in side_drive:
        ref[...] = jnp.zeros_like(ref)

    own_shift = lax.rem(total_cols - col_start, total_cols)
    for source, side, at, here in (
        (north, 0, 8, gy == 0),
        (south, 1, 8 + rows - strip, gy == gy_count - 1),
    ):

        @pl.when(here)
        def _(source=source, side=side, at=at):
            distance = depth if side == 0 else strip - 1 - depth
            weight = RELAX * edge_weight(distance, width[side])
            packed = [[jnp.zeros((strip, LANES), jnp.float32)] * 2 for _ in side_drive]
            for f, l, slot in slots(count_f, count_l):
                values = source[f, l].astype(jnp.float32)
                factor = weight * scale[side, l, f]
                own = pltpu.roll(values, own_shift, 1)[:, 0:LANES]
                drive[f, l, at : at + strip, :] = drive[f, l, at : at + strip, :] + factor * own
                held = (pos >= slot) & (pos < slot + HALO)
                for n, which in enumerate(side_ids(gx_count)):
                    for part, begin in enumerate(
                        (jnp.where(which == 0, cols, -HALO), jnp.where(which == 0, cols - HALO, 0))
                    ):
                        shift = slot + 2 * total_cols - begin - col_start
                        moved = pltpu.roll(values, lax.rem(shift, total_cols), 1)[:, 0:LANES]
                        packed[n][part] = jnp.where(held, factor * moved, packed[n][part])
            for ref, value in zip(side_drive, packed):
                for part in range(2):
                    ref[part, at : at + strip, :] = value[part]


def pack_x_kernel(grid_sizes, first_round, second_round, *rest):
    gy_count, gx_count = grid_sizes
    sides = (len(rest) - 1) // 2
    payloads, outs, ext = rest[:sides], rest[sides:-1], rest[-1]
    cols = first_round.shape[1]
    rows = payloads[0].shape[0]
    lane = iota((2 * PAD, LANES), 1)
    starts = sent_starts(gx_count, cols)
    packed = [jnp.zeros((2 * PAD, LANES), jnp.float32) for _ in starts]
    ext[...] = jnp.zeros_like(ext)
    for index in range(ext.shape[0]):
        slot = index * HALO
        north, south = halo_rows(gy_count, first_round, second_round, slot)
        ext[index, PAD - HALO : PAD, 0:cols] = north
        ext[index, PAD : PAD + HALO, 0:cols] = south
        for n, start in enumerate(starts):
            moved = pltpu.roll(ext[index], lax.rem(slot + LANES - start, LANES), 1)
            packed[n] = jnp.where((lane >= slot) & (lane < slot + HALO), moved, packed[n])
    for out, payload, value in zip(outs, payloads, packed):
        out[0:PAD, :] = value[0:PAD]
        out[PAD : PAD + rows, :] = payload[...]
        out[PAD + rows : 2 * PAD + rows, :] = value[PAD : 2 * PAD]


def loaded(weights, l, fac, count_f):
    flat = [fac * weights[l, n] for n in range(weights.shape[1])]
    taps, flat, speed = flat[: 2 * REACH], flat[2 * REACH : -1], flat[-1]
    return taps, [flat[f * count_f : (f + 1) * count_f] for f in range(count_f)], speed


def y_terms(rows_at, at, taps, total):
    offsets = [k for k in range(-REACH, REACH + 1) if k != 0]
    for tap, offset in zip(taps, offsets):
        total = total + tap * rows_at(at + offset)
    return total


def cell_terms(src, l, f, at, centers, weight, taps, mix, total):
    for g, center in enumerate(centers):
        total = total + (mix[f][g] - weight if g == f else mix[f][g]) * center
    return y_terms(lambda row: src[f, l, pl.ds(row, 8), :], at, taps, total)


def split(value):
    high = value.astype(jnp.bfloat16)
    return high, (value - high.astype(jnp.float32)).astype(jnp.bfloat16)


def x_divergence(src, l, first, height, matrix, xdiv):
    count_f = src.shape[0]
    whole = src[:, l, first : first + height, :].reshape(count_f * height, LANES)
    both = jnp.concatenate(split(whole), axis=1)
    twice = jnp.concatenate([matrix[l], matrix[l]], axis=0)
    moved = jnp.dot(both, twice, preferred_element_type=jnp.float32)
    xdiv[:, 0:height, :] = moved.reshape(count_f, height, LANES)


def begin_kernel(
    grid_sizes,
    fields,
    first_round,
    second_round,
    drive,
    relax,
    weights,
    own_matrix,
    after,
    *rest,
):
    gy_count, gx_count = grid_sizes
    far, (state, own_one, own_two, xdiv) = rest[:-4], rest[-4:]
    count_f, count_l, rows, cols = fields.shape
    wide_rows = relax.shape[0]
    gy = lax.axis_index("gy")
    pad_rows = jnp.zeros((PAD, LANES), jnp.float32)
    for f, l, slot in slots(count_f, count_l):
        north, south = halo_rows(gy_count, first_round, second_round, slot)
        if cols < LANES:
            state[f, l] = jnp.zeros(state.shape[2:], jnp.float32)
        else:
            state[f, l, 0:PAD, :] = pad_rows
            state[f, l, PAD + rows : 2 * PAD + rows, :] = pad_rows
        state[f, l, PAD - HALO : PAD, 0:cols] = north
        state[f, l, PAD : PAD + rows, 0:cols] = fields[f, l]
        state[f, l, PAD + rows : PAD + rows + HALO, 0:cols] = south
    lane = iota((wide_rows, LANES), 1)
    starts = edge_starts(gx_count, cols)[1]

    def keep_far(src, section):
        for ref, start in zip(far, starts):
            packed = jnp.zeros((wide_rows, LANES), jnp.float32)
            here = (lane >= start) & (lane < start + REACH)
            for f, l, slot in slots(count_f, count_l):
                kept = jnp.where(here, src[f, l, FIRST : FIRST + wide_rows, :], 0.0)
                packed = packed + pltpu.roll(kept, lax.rem(slot + LANES - start, LANES), 1)
            ref[section] = packed

    keep_far(state, 0)
    for section, (src, dst, fac) in enumerate(
        ((state, own_one, THIRD), (own_one, own_two, HALF), (own_two, after, 1.0))
    ):
        first, height = (PAD, rows) if dst is after else (FIRST, wide_rows)
        for l in range(count_l):
            x_divergence(src, l, first, height, own_matrix, xdiv)
            taps, mix, speed = loaded(weights, l, fac, count_f)
            for n in range(height // 8):
                at, row = first + n * 8, n * 8
                to = at - FIRST
                centers = [src[g, l, at : at + 8, :] for g in range(count_f)]
                weight = fac * relax[to : to + 8, :]
                for f in range(count_f):
                    base = centers[f] if src is state else state[f, l, at : at + 8, :]
                    total = base + fac * drive[f, l, to : to + 8, :]
                    total = total + speed * xdiv[f, row : row + 8, :]
                    total = cell_terms(src, l, f, at, centers, weight, taps, mix, total)
                    if dst is after:
                        after[f, l, row : row + 8, :] = total[:, 0:cols]
                    else:
                        dst[f, l, at : at + 8, :] = total
        if dst is not after:
            for row, here in ((FIRST, gy == 0), (PAD + rows, gy == gy_count - 1)):

                @pl.when(here)
                def _(dst=dst, row=row):
                    dst[:, :, row : row + 8, :] = jnp.zeros(
                        (count_f, count_l, 8, LANES), jnp.float32
                    )

            keep_far(dst, section + 1)


def finish_kernel(grid_sizes, sides, *refs):
    gy_count, gx_count = grid_sizes
    halos, edges, fars, side_drive, side_matrix = (
        refs[n * sides : (n + 1) * sides] for n in range(5)
    )
    after, row_relax, inside, lane_weights, out, one, two, xdiv = refs[5 * sides :]
    count_f, count_l, rows, cols = out.shape
    wide_rows = row_relax.shape[0]
    gx = lax.axis_index("gx")
    starts = edge_starts(gx_count, cols)[0]
    exists = [None] if sides == 1 else [gx > 0, gx < gx_count - 1]
    taps = [lane_weights[k] for k in range(2 * REACH)]
    mix = [lane_weights[2 * REACH + d] for d in range(2 * count_f - 1)]
    speed = lane_weights[lane_weights.shape[0] - 1]

    def section(parts, s, fac, number, first, height, wanted, store):
        columns = [part[first : first + height, :] for part in parts]
        columns.append(fars[s][number, first - FIRST : first - FIRST + height, :])
        both = jnp.concatenate(split(jnp.concatenate(columns, axis=1)), axis=0)
        moved = jnp.dot(
            both, side_matrix[s][:, wanted[0] * LANES :], preferred_element_type=jnp.float32
        )
        moved = moved[0:height] + moved[height:]
        for n, which in enumerate(wanted):
            xdiv[which, 0:height, :] = moved[:, n * LANES : (n + 1) * LANES]
        for which in wanted:
            part, start = parts[which], (halos, edges)[which][s]
            for n in range(height // 8):
                at, row = first + n * 8, n * 8
                to = at - FIRST
                center = part[at : at + 8, :]
                rate = side_drive[s][which, to : to + 8, :] + speed * xdiv[which, row : row + 8, :]
                rate = rate - row_relax[to : to + 8, :] * center
                for d, entry in enumerate(mix):
                    step = (d - (count_f - 1)) * HALO * count_l
                    other = pltpu.roll(center, -step % LANES, 1) if step else center
                    rate = rate + entry * other
                rate = y_terms(lambda row: part[row : row + 8, :], at, taps, rate)
                store(which, at, to, start[at : at + 8, :] + fac * rate)

    lane = iota((rows, LANES), 1)
    for s in range(sides):
        def keep(ref):
            def store(which, at, to, value):
                kept = inside[to : to + 8, :]
                if exists[s] is not None and which == 0:
                    kept = jnp.where(exists[s], kept, 0.0)
                ref[which, at : at + 8, :] = value * kept

            return store

        section((halos[s], edges[s]), s, THIRD, 0, FIRST, wide_rows, (0, 1), keep(one))
        section((one.at[0], one.at[1]), s, HALF, 1, FIRST, wide_rows, (0, 1), keep(two))

        def last(which, at, to, value):
            one[0, at : at + 8, :] = value

        section((two.at[0], two.at[1]), s, 1.0, 2, PAD, rows, (1,), last)
        right = one[0, PAD : PAD + rows, :]
        near = (lane >= starts[s]) & (lane < starts[s] + HALO)
        if exists[s] is not None:
            near = near & exists[s]
        source = after if s == 0 else out
        for f, l, slot in slots(count_f, count_l):
            moved = pltpu.roll(right, lax.rem(starts[s] + LANES - slot, LANES), 1)
            out[f, l] = jnp.where(near[:, 0:cols], moved[:, 0:cols], source[f, l])


def pair_rounds(gy_count, gx_count):
    rounds = []
    for start in (0, 1):
        partner = {}
        for low in range(start, gy_count - 1, 2):
            partner[low], partner[low + 1] = low + 1, low
        pairs = []
        for y in range(gy_count):
            for x in range(gx_count):
                if y in partner:
                    pairs.append((y * gx_count + x, partner[y] * gx_count + x))
                elif gx_count % 2 == 0:
                    pairs.append((y * gx_count + x, y * gx_count + (x ^ 1)))
        rounds.append(pairs)
    return rounds


def local(
    gy_count, gx_count, fields, wind_x, wind_y, coupling, north, south, west, east, strip_scale, widths
):
    count_f, count_l, rows, cols = fields.shape
    ext_rows = rows + 2 * PAD
    grid_sizes = (gy_count, gx_count)
    packed_rows = -(-HALO * count_f * count_l // 8) * 8
    vmem = pl.BlockSpec(memory_space=pltpu.VMEM)
    smem = pl.BlockSpec(memory_space=pltpu.SMEM)
    f32 = functools.partial(jax.ShapeDtypeStruct, dtype=jnp.float32)

    def call(body, name, out_shape, inputs, scratch=(), limit=4):
        several = isinstance(out_shape, tuple)
        return pl.pallas_call(
            body,
            out_shape=out_shape,
            in_specs=[space for _, space in inputs],
            out_specs=(vmem,) * len(out_shape) if several else vmem,
            scratch_shapes=list(scratch),
            compiler_params=pltpu.CompilerParams(vmem_limit_bytes=limit << 20),
            name=name,
        )(*[value for value, _ in inputs])

    def inputs(space, *values):
        return [(value, space) for value in values]

    strip_shape = f32((packed_rows, cols))
    sent_first, sent_second = call(
        pack_y_kernel, "pack_y", (strip_shape, strip_shape), inputs(vmem, fields)
    )
    first_pairs, second_pairs = pair_rounds(gy_count, gx_count)
    first_round = lax.ppermute(sent_first, ("gy", "gx"), first_pairs)
    second_round = lax.ppermute(sent_second, ("gy", "gx"), second_pairs)

    mixing = jnp.transpose(coupling, (1, 0, 2))
    scales = jnp.transpose(strip_scale, (0, 2, 1))
    sides = 1 if gx_count == 2 else 2
    wide_rows = rows + 16
    state_shape = (count_f, count_l, ext_rows, LANES)
    wide_shape = (count_f, count_l, wide_rows, LANES)
    plane = f32((wide_rows, LANES))
    matrix = functools.partial(jax.ShapeDtypeStruct, dtype=jnp.bfloat16)
    entries = 2 * REACH + count_f * count_f + 1
    lane_entries = 2 * REACH + 2 * count_f
    prepared = call(
        functools.partial(prepare_kernel, grid_sizes),
        "prepare",
        (f32(wide_shape), plane, plane, plane)
        + (f32((count_l, entries, 8, LANES)), f32((lane_entries, 8, LANES)))
        + (matrix((count_l, LANES, LANES)),)
        + (f32((rows, LANES)),) * sides
        + (f32((2, wide_rows, LANES)),) * sides
        + (matrix((3 * LANES, 2 * LANES)),) * sides,
        inputs(vmem, fields, north, south, jnp.swapaxes(west, 2, 3), jnp.swapaxes(east, 2, 3))
        + inputs(vmem, jnp.asarray(own_bands(cols), jnp.bfloat16))
        + inputs(smem, scales, widths, wind_x, wind_y, mixing),
        scratch=[pltpu.VMEM((rows, LANES), jnp.float32)],
    )
    drive, relax, row_relax, inside, weights, lane_weights, own_matrix = prepared[:7]
    payloads, side_drive, side_matrix = (
        prepared[7 + n * sides : 7 + (n + 1) * sides] for n in range(3)
    )

    sent = call(
        functools.partial(pack_x_kernel, grid_sizes),
        "pack_x",
        (f32((ext_rows, LANES)),) * sides,
        inputs(vmem, first_round, second_round, *payloads),
        scratch=[pltpu.VMEM((count_f * count_l, 2 * PAD, LANES), jnp.float32)],
    )
    forward = [(i, i + 1) for i in range(gx_count - 1)]
    backward = [(b, a) for a, b in forward]
    if sides == 1:
        halos = [lax.ppermute(sent[0], "gx", forward + backward)]
    else:
        halos = [lax.ppermute(sent[0], "gx", forward), lax.ppermute(sent[1], "gx", backward)]

    state = pltpu.VMEM(state_shape, jnp.float32)
    after, *far = call(
        functools.partial(begin_kernel, grid_sizes),
        "begin",
        (f32(fields.shape),) + (f32((3, wide_rows, LANES)),) * sides,
        inputs(vmem, fields, first_round, second_round, drive, relax, weights, own_matrix),
        scratch=[state] * 3 + [pltpu.VMEM((count_f, wide_rows, LANES), jnp.float32)],
        limit=8,
    )
    pair = pltpu.VMEM((2, ext_rows, LANES), jnp.float32)
    return call(
        functools.partial(finish_kernel, grid_sizes, sides),
        "finish",
        f32(fields.shape),
        inputs(vmem, *halos, *sent[::-1], *far, *side_drive, *side_matrix)
        + inputs(vmem, after, row_relax, inside, lane_weights),
        scratch=[pair, pair, pltpu.VMEM((2, wide_rows, LANES), jnp.float32)],
    )


def solution(mesh):
    return jax.shard_map(
        functools.partial(local, mesh.shape["gy"], mesh.shape["gx"]),
        mesh=mesh,
        in_specs=(
            P("mem", None, "gy", "gx"),
            P("mem"),
            P("mem"),
            P(),
            P("mem", None, None, None),
            P("mem", None, None, None),
            P("mem", None, None, None),
            P("mem", None, None, None),
            P("mem", None, None),
            P(),
        ),
        out_specs=P("mem", None, "gy", "gx"),
        check_vma=False,
    )
```

```python
import functools

import jax
import jax.numpy as jnp
import numpy as np
from jax import lax
from jax.experimental import pallas as pl
from jax.experimental.pallas import tpu as pltpu
from jax.sharding import PartitionSpec as P

RELAX = 0.25
REACH = 3
HALO = 3 * REACH
PAD = 16
LANES = 128
FIRST = PAD - 8
THIRD, HALF = 1.0 / 3.0, 0.5

UPWIND = (-2.0, 15.0, -60.0, 20.0, 30.0, -3.0, 0.0)
CENTRAL = (-1.0, 9.0, -45.0, 0.0, 45.0, -9.0, 1.0)
DAMPING = (1.0, -6.0, 15.0, -20.0, 15.0, -6.0, 1.0)


def own_bands(cols):
    bands = np.zeros((2, LANES, LANES), np.float32)
    for col in range(cols):
        for offset in range(-REACH, REACH + 1):
            if 0 <= col + offset < cols:
                bands[0, col + offset, col] = UPWIND[offset + REACH]
                bands[1, col + offset, col] = -UPWIND[REACH - offset]
    return bands


def iota(shape, dim):
    return lax.broadcasted_iota(jnp.int32, shape, dim)


def edge_weight(distance, width):
    dist = distance.astype(jnp.float32)
    inside = (dist >= 0.0) & (dist < width)
    return jnp.where(inside, jnp.square((width - dist) / width), 0.0)


def slots(count_f, count_l):
    return [(f, l, HALO * (f * count_l + l)) for f in range(count_f) for l in range(count_l)]


def pack_y_kernel(fields, first_round, second_round):
    count_f, count_l, rows, _ = fields.shape
    even = lax.rem(lax.axis_index("gy"), 2) == 0
    for f, l, slot in slots(count_f, count_l):
        top = fields[f, l, 0:HALO, :]
        bottom = fields[f, l, rows - HALO : rows, :]
        first_round[slot : slot + HALO, :] = jnp.where(even, bottom, top)
        second_round[slot : slot + HALO, :] = jnp.where(even, top, bottom)


def halo_rows(gy_count, first_round, second_round, slot):
    gy = lax.axis_index("gy")
    even = lax.rem(gy, 2) == 0
    first = first_round[slot : slot + HALO, :]
    second = second_round[slot : slot + HALO, :]
    north = jnp.where(gy == 0, 0.0, jnp.where(even, second, first))
    south = jnp.where(gy == gy_count - 1, 0.0, jnp.where(even, first, second))
    return north, south


def sent_starts(gx_count, cols):
    if gx_count == 2:
        return [jnp.where(lax.axis_index("gx") == 0, cols - HALO, 0)]
    return [cols - HALO, 0]


def side_ids(gx_count):
    if gx_count == 2:
        return [jnp.where(lax.axis_index("gx") == 0, 0, 1)]
    return [1, 0]


def edge_starts(gx_count, cols):
    near = [jnp.where(side == 0, cols - HALO, 0) for side in side_ids(gx_count)]
    far = [jnp.where(side == 0, cols - HALO - REACH, HALO) for side in side_ids(gx_count)]
    return near, far


def level_weights(coupling, wind_x, wind_y, l, count_f):
    speed, size = wind_y[l] / 60.0, jnp.abs(wind_y[l]) / 60.0
    taps = [size * DAMPING[k] - speed * CENTRAL[k] for k in range(2 * REACH + 1)]
    mix = [
        [coupling[f, l, g] + (taps[REACH] if f == g else 0.0) for g in range(count_f)]
        for f in range(count_f)
    ]
    return [tap for k, tap in enumerate(taps) if k != REACH], mix, -wind_x[l] / 60.0


def side_bands(side, lane_speed, matrix):
    shape = (LANES, LANES)
    row, col = iota(shape, 0), iota(shape, 1)
    row_plane, col_plane = (row * 57) >> 9, (col * 57) >> 9
    apart = (row - HALO * row_plane) - (col - HALO * col_plane)
    apart = jnp.where(row_plane == col_plane, apart, 4 * HALO)
    sign = jnp.where(lane_speed > 0.0, -1, 1)
    sign_float = sign.astype(jnp.float32)

    def block(base):
        offset = (apart + base) * sign
        value = jnp.zeros(shape, jnp.float32)
        for k, entry in enumerate(UPWIND[:-1]):
            value = jnp.where(offset == k - REACH, entry, value)
        return (value * sign_float).astype(jnp.bfloat16)

    here, step = block(0), jnp.where(side == 0, HALO, -HALO)
    matrix[0:LANES, 0:LANES] = here
    matrix[LANES : 2 * LANES, LANES:] = here
    matrix[LANES : 2 * LANES, 0:LANES] = block(-step)
    matrix[0:LANES, LANES:] = block(step)
    matrix[2 * LANES :, 0:LANES] = jnp.zeros(shape, jnp.bfloat16)
    matrix[2 * LANES :, LANES:] = block(jnp.where(side == 0, -REACH, HALO))


def prepare_kernel(
    grid_sizes,
    fields,
    north,
    south,
    west,
    east,
    own_band,
    scale,
    widths,
    wind_x,
    wind_y,
    coupling,
    drive,
    relax,
    row_relax,
    inside,
    weights,
    lane_weights,
    own_matrix,
    *rest,
):
    gy_count, gx_count = grid_sizes
    sides = (len(rest) - 1) // 3
    payloads, side_drive, side_matrix = rest[:sides], rest[sides : 2 * sides], rest[2 * sides : -1]
    wide = rest[-1]
    count_f, count_l, rows, cols = fields.shape
    wide_rows = relax.shape[0]
    strip = north.shape[2]
    total_rows, total_cols = rows * gy_count, cols * gx_count
    gy, gx = lax.axis_index("gy"), lax.axis_index("gx")
    row_start, col_start = gy * rows, gx * cols
    width = [widths[s].astype(jnp.float32) for s in range(4)]
    lane = iota((8, LANES), 1)

    lane_rows = iota((rows, LANES), 1)
    starts = sent_starts(gx_count, cols)
    packed = [jnp.zeros((rows, LANES), jnp.float32) for _ in starts]
    if cols < LANES:
        wide[...] = jnp.zeros_like(wide)
    for f, l, slot in slots(count_f, count_l):
        if cols < LANES:
            wide[:, 0:cols] = fields[f, l]
            own = wide[...]
        else:
            own = fields[f, l]
        for n, start in enumerate(starts):
            moved = pltpu.roll(own, lax.rem(slot + LANES - start, LANES), 1)
            here = (lane_rows >= slot) & (lane_rows < slot + HALO)
            packed[n] = jnp.where(here, moved, packed[n])
    for payload, value in zip(payloads, packed):
        payload[...] = value

    def full(value):
        return jnp.full((8, LANES), value, jnp.float32)

    lane_taps = [full(0.0) for _ in range(2 * REACH)]
    lane_mix = [full(0.0) for _ in range(2 * count_f - 1)]
    lane_speed = full(0.0)
    for l in range(count_l):
        taps, mix, speed = level_weights(coupling, wind_x, wind_y, l, count_f)
        flat = taps + [entry for line in mix for entry in line] + [speed]
        for n, entry in enumerate(flat):
            weights[l, n] = full(entry)
        own_matrix[l] = own_band[jnp.where(wind_x[l] < 0.0, 1, 0)]
        for f in range(count_f):
            slot = HALO * (f * count_l + l)
            here = (lane >= slot) & (lane < slot + HALO)
            lane_taps = [jnp.where(here, tap, old) for tap, old in zip(taps, lane_taps)]
            lane_speed = jnp.where(here, speed, lane_speed)
            for g in range(count_f):
                at = g - f + count_f - 1
                lane_mix[at] = jnp.where(here, mix[f][g], lane_mix[at])
    for n, entry in enumerate(lane_taps + lane_mix + [lane_speed]):
        lane_weights[n] = entry
    for side, matrix in zip(side_ids(gx_count), side_matrix):
        side_bands(side, lane_speed[0:1, :], matrix)

    row_global = iota((wide_rows, LANES), 0) + (row_start - 8)
    row_weight = RELAX * (
        edge_weight(row_global, width[0]) + edge_weight(total_rows - 1 - row_global, width[1])
    )
    col_weight = RELAX * (
        edge_weight(lane + col_start, width[2])
        + edge_weight(total_cols - 1 - (lane + col_start), width[3])
    )
    row_relax[...] = row_weight
    relax[...] = row_weight + col_weight[0:1, :]
    inside[...] = jnp.where((row_global >= 0) & (row_global < total_rows), 1.0, 0.0)

    pos = iota((strip, LANES), 1)
    depth = iota((strip, LANES), 0)
    pick = jnp.concatenate([pos == depth, pos == depth + (cols - strip)], axis=0)
    pick = pick.astype(jnp.float32).astype(jnp.bfloat16)
    west_weight = RELAX * edge_weight(lane + col_start, width[2])
    east_weight = RELAX * edge_weight(total_cols - 1 - (lane + col_start), width[3])
    west_weight = jnp.where(lane < strip, west_weight, 0.0)
    east_weight = jnp.where((lane >= cols - strip) & (lane < cols), east_weight, 0.0)
    shift = lax.rem(8 + total_rows - row_start, total_rows)
    for f in range(count_f):
        for l in range(count_l):
            both = jnp.concatenate([west[f, l], east[f, l]], axis=0).astype(jnp.float32)
            both = pltpu.roll(both, shift, 1)[:, 0:LANES].astype(jnp.bfloat16)
            raw = lax.dot_general(
                both, pick, (((0,), (0,)), ((), ())), preferred_element_type=jnp.float32
            )
            factor = west_weight * scale[2, l, f] + east_weight * scale[3, l, f]
            drive[f, l] = raw[0:wide_rows] * factor[0:1, :]
    for ref in side_drive:
        ref[...] = jnp.zeros_like(ref)

    own_shift = lax.rem(total_cols - col_start, total_cols)
    for source, side, at, here in (
        (north, 0, 8, gy == 0),
        (south, 1, 8 + rows - strip, gy == gy_count - 1),
    ):

        @pl.when(here)
        def _(source=source, side=side, at=at):
            distance = depth if side == 0 else strip - 1 - depth
            weight = RELAX * edge_weight(distance, width[side])
            packed = [[jnp.zeros((strip, LANES), jnp.float32)] * 2 for _ in side_drive]
            for f, l, slot in slots(count_f, count_l):
                values = source[f, l].astype(jnp.float32)
                factor = weight * scale[side, l, f]
                own = pltpu.roll(values, own_shift, 1)[:, 0:LANES]
                drive[f, l, at : at + strip, :] = drive[f, l, at : at + strip, :] + factor * own
                held = (pos >= slot) & (pos < slot + HALO)
                for n, which in enumerate(side_ids(gx_count)):
                    for part, begin in enumerate(
                        (jnp.where(which == 0, cols, -HALO), jnp.where(which == 0, cols - HALO, 0))
                    ):
                        shift = slot + 2 * total_cols - begin - col_start
                        moved = pltpu.roll(values, lax.rem(shift, total_cols), 1)[:, 0:LANES]
                        packed[n][part] = jnp.where(held, factor * moved, packed[n][part])
            for ref, value in zip(side_drive, packed):
                for part in range(2):
                    ref[part, at : at + strip, :] = value[part]


def pack_x_kernel(grid_sizes, first_round, second_round, *rest):
    gy_count, gx_count = grid_sizes
    sides = (len(rest) - 1) // 2
    payloads, outs, ext = rest[:sides], rest[sides:-1], rest[-1]
    cols = first_round.shape[1]
    rows = payloads[0].shape[0]
    lane = iota((2 * PAD, LANES), 1)
    starts = sent_starts(gx_count, cols)
    packed = [jnp.zeros((2 * PAD, LANES), jnp.float32) for _ in starts]
    ext[...] = jnp.zeros_like(ext)
    for index in range(ext.shape[0]):
        slot = index * HALO
        north, south = halo_rows(gy_count, first_round, second_round, slot)
        ext[index, PAD - HALO : PAD, 0:cols] = north
        ext[index, PAD : PAD + HALO, 0:cols] = south
        for n, start in enumerate(starts):
            moved = pltpu.roll(ext[index], lax.rem(slot + LANES - start, LANES), 1)
            packed[n] = jnp.where((lane >= slot) & (lane < slot + HALO), moved, packed[n])
    for out, payload, value in zip(outs, payloads, packed):
        out[0:PAD, :] = value[0:PAD]
        out[PAD : PAD + rows, :] = payload[...]
        out[PAD + rows : 2 * PAD + rows, :] = value[PAD : 2 * PAD]


def loaded(weights, l, fac, count_f):
    flat = [fac * weights[l, n] for n in range(weights.shape[1])]
    taps, flat, speed = flat[: 2 * REACH], flat[2 * REACH : -1], flat[-1]
    return taps, [flat[f * count_f : (f + 1) * count_f] for f in range(count_f)], speed


def y_terms(rows_at, at, taps, total):
    offsets = [k for k in range(-REACH, REACH + 1) if k != 0]
    for tap, offset in zip(taps, offsets):
        total = total + tap * rows_at(at + offset)
    return total


def cell_terms(src, l, f, at, centers, weight, taps, mix, total):
    for g, center in enumerate(centers):
        total = total + (mix[f][g] - weight if g == f else mix[f][g]) * center
    return y_terms(lambda row: src[f, l, pl.ds(row, 8), :], at, taps, total)


def split(value):
    high = value.astype(jnp.bfloat16)
    return high, (value - high.astype(jnp.float32)).astype(jnp.bfloat16)


def x_divergence(src, l, first, height, matrix, xdiv):
    count_f = src.shape[0]
    whole = src[:, l, first : first + height, :].reshape(count_f * height, LANES)
    both = jnp.concatenate(split(whole), axis=1)
    twice = jnp.concatenate([matrix[l], matrix[l]], axis=0)
    moved = jnp.dot(both, twice, preferred_element_type=jnp.float32)
    xdiv[:, 0:height, :] = moved.reshape(count_f, height, LANES)


def begin_kernel(
    grid_sizes,
    fields,
    first_round,
    second_round,
    drive,
    relax,
    weights,
    own_matrix,
    after,
    *rest,
):
    gy_count, gx_count = grid_sizes
    far, (state, own_one, own_two, xdiv) = rest[:-4], rest[-4:]
    count_f, count_l, rows, cols = fields.shape
    wide_rows = relax.shape[0]
    gy = lax.axis_index("gy")
    pad_rows = jnp.zeros((PAD, LANES), jnp.float32)
    for f, l, slot in slots(count_f, count_l):
        north, south = halo_rows(gy_count, first_round, second_round, slot)
        if cols < LANES:
            state[f, l] = jnp.zeros(state.shape[2:], jnp.float32)
        else:
            state[f, l, 0:PAD, :] = pad_rows
            state[f, l, PAD + rows : 2 * PAD + rows, :] = pad_rows
        state[f, l, PAD - HALO : PAD, 0:cols] = north
        state[f, l, PAD : PAD + rows, 0:cols] = fields[f, l]
        state[f, l, PAD + rows : PAD + rows + HALO, 0:cols] = south
    lane = iota((wide_rows, LANES), 1)
    starts = edge_starts(gx_count, cols)[1]

    def keep_far(src, section):
        for ref, start in zip(far, starts):
            packed = jnp.zeros((wide_rows, LANES), jnp.float32)
            here = (lane >= start) & (lane < start + REACH)
            for f, l, slot in slots(count_f, count_l):
                kept = jnp.where(here, src[f, l, FIRST : FIRST + wide_rows, :], 0.0)
                packed = packed + pltpu.roll(kept, lax.rem(slot + LANES - start, LANES), 1)
            ref[section] = packed

    keep_far(state, 0)
    for section, (src, dst, fac) in enumerate(
        ((state, own_one, THIRD), (own_one, own_two, HALF), (own_two, after, 1.0))
    ):
        first, height = (PAD, rows) if dst is after else (FIRST, wide_rows)
        for l in range(count_l):
            x_divergence(src, l, first, height, own_matrix, xdiv)
            taps, mix, speed = loaded(weights, l, fac, count_f)
            for n in range(height // 8):
                at, row = first + n * 8, n * 8
                to = at - FIRST
                centers = [src[g, l, at : at + 8, :] for g in range(count_f)]
                weight = fac * relax[to : to + 8, :]
                for f in range(count_f):
                    base = centers[f] if src is state else state[f, l, at : at + 8, :]
                    total = base + fac * drive[f, l, to : to + 8, :]
                    total = total + speed * xdiv[f, row : row + 8, :]
                    total = cell_terms(src, l, f, at, centers, weight, taps, mix, total)
                    if dst is after:
                        after[f, l, row : row + 8, :] = total[:, 0:cols]
                    else:
                        dst[f, l, at : at + 8, :] = total
        if dst is not after:
            for row, here in ((FIRST, gy == 0), (PAD + rows, gy == gy_count - 1)):

                @pl.when(here)
                def _(dst=dst, row=row):
                    dst[:, :, row : row + 8, :] = jnp.zeros(
                        (count_f, count_l, 8, LANES), jnp.float32
                    )

            keep_far(dst, section + 1)


def finish_kernel(grid_sizes, sides, *refs):
    gy_count, gx_count = grid_sizes
    halos, edges, fars, side_drive, side_matrix = (
        refs[n * sides : (n + 1) * sides] for n in range(5)
    )
    after, row_relax, inside, lane_weights, out, one, two, xdiv = refs[5 * sides :]
    count_f, count_l, rows, cols = out.shape
    wide_rows = row_relax.shape[0]
    gx = lax.axis_index("gx")
    starts = edge_starts(gx_count, cols)[0]
    exists = [None] if sides == 1 else [gx > 0, gx < gx_count - 1]
    taps = [lane_weights[k] for k in range(2 * REACH)]
    mix = [lane_weights[2 * REACH + d] for d in range(2 * count_f - 1)]
    speed = lane_weights[lane_weights.shape[0] - 1]

    def section(parts, s, fac, number, first, height, wanted, store):
        columns = [part[first : first + height, :] for part in parts]
        columns.append(fars[s][number, first - FIRST : first - FIRST + height, :])
        both = jnp.concatenate(split(jnp.concatenate(columns, axis=1)), axis=0)
        moved = jnp.dot(
            both, side_matrix[s][:, wanted[0] * LANES :], preferred_element_type=jnp.float32
        )
        moved = moved[0:height] + moved[height:]
        for n, which in enumerate(wanted):
            xdiv[which, 0:height, :] = moved[:, n * LANES : (n + 1) * LANES]
        for which in wanted:
            part, start = parts[which], (halos, edges)[which][s]
            for n in range(height // 8):
                at, row = first + n * 8, n * 8
                to = at - FIRST
                center = part[at : at + 8, :]
                rate = side_drive[s][which, to : to + 8, :] + speed * xdiv[which, row : row + 8, :]
                rate = rate - row_relax[to : to + 8, :] * center
                for d, entry in enumerate(mix):
                    step = (d - (count_f - 1)) * HALO * count_l
                    other = pltpu.roll(center, -step % LANES, 1) if step else center
                    rate = rate + entry * other
                rate = y_terms(lambda row: part[row : row + 8, :], at, taps, rate)
                store(which, at, to, start[at : at + 8, :] + fac * rate)

    lane = iota((rows, LANES), 1)
    for s in range(sides):
        def keep(ref):
            def store(which, at, to, value):
                kept = inside[to : to + 8, :]
                if exists[s] is not None and which == 0:
                    kept = jnp.where(exists[s], kept, 0.0)
                ref[which, at : at + 8, :] = value * kept

            return store

        section((halos[s], edges[s]), s, THIRD, 0, FIRST, wide_rows, (0, 1), keep(one))
        section((one.at[0], one.at[1]), s, HALF, 1, FIRST, wide_rows, (0, 1), keep(two))

        def last(which, at, to, value):
            one[0, at : at + 8, :] = value

        section((two.at[0], two.at[1]), s, 1.0, 2, PAD, rows, (1,), last)
        right = one[0, PAD : PAD + rows, :]
        near = (lane >= starts[s]) & (lane < starts[s] + HALO)
        if exists[s] is not None:
            near = near & exists[s]
        source = after if s == 0 else out
        for f, l, slot in slots(count_f, count_l):
            moved = pltpu.roll(right, lax.rem(starts[s] + LANES - slot, LANES), 1)
            out[f, l] = jnp.where(near[:, 0:cols], moved[:, 0:cols], source[f, l])


def pair_rounds(part_count, gy_count, gx_count):
    rounds = []
    for start in (0, 1):
        partner = {}
        for low in range(start, gy_count - 1, 2):
            partner[low], partner[low + 1] = low + 1, low
        pairs = []
        for place in np.ndindex(part_count, gy_count, gx_count):
            part, y, x = place
            if y in partner:
                to = part, partner[y], x
            elif part_count % 2 == 0:
                to = part ^ 1, y, x
            elif gx_count % 2 == 0:
                to = part, y, x ^ 1
            else:
                continue
            shape = (part_count, gy_count, gx_count)
            pairs.append(tuple(int(np.ravel_multi_index(at, shape)) for at in (place, to)))
        rounds.append(pairs)
    return rounds


def local(
    gy_count, gx_count, fields, wind_x, wind_y, coupling, north, south, west, east, strip_scale, widths
):
    count_f, count_l, rows, cols = fields.shape
    ext_rows = rows + 2 * PAD
    grid_sizes = (gy_count, gx_count)
    packed_rows = -(-HALO * count_f * count_l // 8) * 8
    vmem = pl.BlockSpec(memory_space=pltpu.VMEM)
    smem = pl.BlockSpec(memory_space=pltpu.SMEM)
    f32 = functools.partial(jax.ShapeDtypeStruct, dtype=jnp.float32)

    def call(body, name, out_shape, inputs, scratch=(), limit=4):
        several = isinstance(out_shape, tuple)
        return pl.pallas_call(
            body,
            out_shape=out_shape,
            in_specs=[space for _, space in inputs],
            out_specs=(vmem,) * len(out_shape) if several else vmem,
            scratch_shapes=list(scratch),
            compiler_params=pltpu.CompilerParams(vmem_limit_bytes=limit << 20),
            name=name,
        )(*[value for value, _ in inputs])

    def inputs(space, *values):
        return [(value, space) for value in values]

    strip_shape = f32((packed_rows, cols))
    sent_first, sent_second = call(
        pack_y_kernel, "pack_y", (strip_shape, strip_shape), inputs(vmem, fields)
    )
    axes = ("mem", "gy", "gx")
    first_pairs, second_pairs = pair_rounds(lax.axis_size("mem"), gy_count, gx_count)
    first_round = lax.ppermute(sent_first, axes, first_pairs)
    second_round = lax.ppermute(sent_second, axes, second_pairs)

    mixing = jnp.transpose(coupling, (1, 0, 2))
    scales = jnp.transpose(strip_scale, (0, 2, 1))
    sides = 1 if gx_count == 2 else 2
    wide_rows = rows + 16
    state_shape = (count_f, count_l, ext_rows, LANES)
    wide_shape = (count_f, count_l, wide_rows, LANES)
    plane = f32((wide_rows, LANES))
    matrix = functools.partial(jax.ShapeDtypeStruct, dtype=jnp.bfloat16)
    entries = 2 * REACH + count_f * count_f + 1
    lane_entries = 2 * REACH + 2 * count_f
    prepared = call(
        functools.partial(prepare_kernel, grid_sizes),
        "prepare",
        (f32(wide_shape), plane, plane, plane)
        + (f32((count_l, entries, 8, LANES)), f32((lane_entries, 8, LANES)))
        + (matrix((count_l, LANES, LANES)),)
        + (f32((rows, LANES)),) * sides
        + (f32((2, wide_rows, LANES)),) * sides
        + (matrix((3 * LANES, 2 * LANES)),) * sides,
        inputs(vmem, fields, north, south, jnp.swapaxes(west, 2, 3), jnp.swapaxes(east, 2, 3))
        + inputs(vmem, jnp.asarray(own_bands(cols), jnp.bfloat16))
        + inputs(smem, scales, widths, wind_x, wind_y, mixing),
        scratch=[pltpu.VMEM((rows, LANES), jnp.float32)],
    )
    drive, relax, row_relax, inside, weights, lane_weights, own_matrix = prepared[:7]
    payloads, side_drive, side_matrix = (
        prepared[7 + n * sides : 7 + (n + 1) * sides] for n in range(3)
    )

    sent = call(
        functools.partial(pack_x_kernel, grid_sizes),
        "pack_x",
        (f32((ext_rows, LANES)),) * sides,
        inputs(vmem, first_round, second_round, *payloads),
        scratch=[pltpu.VMEM((count_f * count_l, 2 * PAD, LANES), jnp.float32)],
    )
    forward = [(i, i + 1) for i in range(gx_count - 1)]
    backward = [(b, a) for a, b in forward]
    if sides == 1:
        halos = [lax.ppermute(sent[0], "gx", forward + backward)]
    else:
        halos = [lax.ppermute(sent[0], "gx", forward), lax.ppermute(sent[1], "gx", backward)]

    state = pltpu.VMEM(state_shape, jnp.float32)
    after, *far = call(
        functools.partial(begin_kernel, grid_sizes),
        "begin",
        (f32(fields.shape),) + (f32((3, wide_rows, LANES)),) * sides,
        inputs(vmem, fields, first_round, second_round, drive, relax, weights, own_matrix),
        scratch=[state] * 3 + [pltpu.VMEM((count_f, wide_rows, LANES), jnp.float32)],
        limit=8,
    )
    pair = pltpu.VMEM((2, ext_rows, LANES), jnp.float32)
    return call(
        functools.partial(finish_kernel, grid_sizes, sides),
        "finish",
        f32(fields.shape),
        inputs(vmem, *halos, *sent[::-1], *far, *side_drive, *side_matrix)
        + inputs(vmem, after, row_relax, inside, lane_weights),
        scratch=[pair, pair, pltpu.VMEM((2, wide_rows, LANES), jnp.float32)],
    )


def solution(mesh):
    return jax.shard_map(
        functools.partial(local, mesh.shape["gy"], mesh.shape["gx"]),
        mesh=mesh,
        in_specs=(
            P("mem", None, "gy", "gx"),
            P("mem"),
            P("mem"),
            P(),
            P("mem", None, None, None),
            P("mem", None, None, None),
            P("mem", None, None, None),
            P("mem", None, None, None),
            P("mem", None, None),
            P(),
        ),
        out_specs=P("mem", None, "gy", "gx"),
        check_vma=False,
    )
```

```python
import functools

import jax
import jax.numpy as jnp
import numpy as np
from jax import lax
from jax.experimental import pallas as pl
from jax.experimental.pallas import tpu as pltpu
from jax.sharding import PartitionSpec as P

RELAX = 0.25
REACH = 3
HALO = 3 * REACH
PAD = 16
LANES = 128
FIRST = PAD - 8
THIRD, HALF = 1.0 / 3.0, 0.5

UPWIND = (-2.0, 15.0, -60.0, 20.0, 30.0, -3.0, 0.0)
CENTRAL = (-1.0, 9.0, -45.0, 0.0, 45.0, -9.0, 1.0)
DAMPING = (1.0, -6.0, 15.0, -20.0, 15.0, -6.0, 1.0)


def own_bands(cols):
    bands = np.zeros((2, LANES, LANES), np.float32)
    for col in range(cols):
        for offset in range(-REACH, REACH + 1):
            if 0 <= col + offset < cols:
                bands[0, col + offset, col] = UPWIND[offset + REACH]
                bands[1, col + offset, col] = -UPWIND[REACH - offset]
    return bands


def iota(shape, dim):
    return lax.broadcasted_iota(jnp.int32, shape, dim)


def edge_weight(distance, width):
    dist = distance.astype(jnp.float32)
    inside = (dist >= 0.0) & (dist < width)
    return jnp.where(inside, jnp.square((width - dist) / width), 0.0)


def slots(count_f, count_l):
    return [(f, l, HALO * (f * count_l + l)) for f in range(count_f) for l in range(count_l)]


def pack_y_kernel(fields, first_round, second_round):
    count_f, count_l, rows, _ = fields.shape
    even = lax.rem(lax.axis_index("gy"), 2) == 0
    for f, l, slot in slots(count_f, count_l):
        top = fields[f, l, 0:HALO, :]
        bottom = fields[f, l, rows - HALO : rows, :]
        first_round[slot : slot + HALO, :] = jnp.where(even, bottom, top)
        second_round[slot : slot + HALO, :] = jnp.where(even, top, bottom)


def halo_rows(gy_count, first_round, second_round, slot):
    gy = lax.axis_index("gy")
    even = lax.rem(gy, 2) == 0
    first = first_round[slot : slot + HALO, :]
    second = second_round[slot : slot + HALO, :]
    north = jnp.where(gy == 0, 0.0, jnp.where(even, second, first))
    south = jnp.where(gy == gy_count - 1, 0.0, jnp.where(even, first, second))
    return north, south


def sent_starts(gx_count, cols):
    if gx_count == 2:
        return [jnp.where(lax.axis_index("gx") == 0, cols - HALO, 0)]
    return [cols - HALO, 0]


def side_ids(gx_count):
    if gx_count == 2:
        return [jnp.where(lax.axis_index("gx") == 0, 0, 1)]
    return [1, 0]


def edge_starts(gx_count, cols):
    near = [jnp.where(side == 0, cols - HALO, 0) for side in side_ids(gx_count)]
    far = [jnp.where(side == 0, cols - HALO - REACH, HALO) for side in side_ids(gx_count)]
    return near, far


def level_weights(coupling, wind_x, wind_y, l, count_f):
    speed, size = wind_y[l] / 60.0, jnp.abs(wind_y[l]) / 60.0
    taps = [size * DAMPING[k] - speed * CENTRAL[k] for k in range(2 * REACH + 1)]
    mix = [
        [coupling[f, l, g] + (taps[REACH] if f == g else 0.0) for g in range(count_f)]
        for f in range(count_f)
    ]
    return [tap for k, tap in enumerate(taps) if k != REACH], mix, -wind_x[l] / 60.0


def side_bands(side, lane_speed, matrix):
    shape = (LANES, LANES)
    row, col = iota(shape, 0), iota(shape, 1)
    row_plane, col_plane = (row * 57) >> 9, (col * 57) >> 9
    apart = (row - HALO * row_plane) - (col - HALO * col_plane)
    apart = jnp.where(row_plane == col_plane, apart, 4 * HALO)
    sign = jnp.where(lane_speed > 0.0, -1, 1)
    sign_float = sign.astype(jnp.float32)

    def block(base):
        offset = (apart + base) * sign
        value = jnp.zeros(shape, jnp.float32)
        for k, entry in enumerate(UPWIND[:-1]):
            value = jnp.where(offset == k - REACH, entry, value)
        return (value * sign_float).astype(jnp.bfloat16)

    here, step = block(0), jnp.where(side == 0, HALO, -HALO)
    matrix[0:LANES, 0:LANES] = here
    matrix[LANES : 2 * LANES, LANES:] = here
    matrix[LANES : 2 * LANES, 0:LANES] = block(-step)
    matrix[0:LANES, LANES:] = block(step)
    matrix[2 * LANES :, 0:LANES] = jnp.zeros(shape, jnp.bfloat16)
    matrix[2 * LANES :, LANES:] = block(jnp.where(side == 0, -REACH, HALO))


def prepare_kernel(
    grid_sizes,
    fields,
    north,
    south,
    west,
    east,
    own_band,
    scale,
    widths,
    wind_x,
    wind_y,
    coupling,
    drive,
    relax,
    row_relax,
    inside,
    weights,
    lane_weights,
    own_matrix,
    *rest,
):
    gy_count, gx_count = grid_sizes
    sides = (len(rest) - 1) // 3
    payloads, side_drive, side_matrix = rest[:sides], rest[sides : 2 * sides], rest[2 * sides : -1]
    wide = rest[-1]
    count_f, count_l, rows, cols = fields.shape
    wide_rows = relax.shape[0]
    strip = north.shape[2]
    total_rows, total_cols = rows * gy_count, cols * gx_count
    gy, gx = lax.axis_index("gy"), lax.axis_index("gx")
    row_start, col_start = gy * rows, gx * cols
    width = [widths[s].astype(jnp.float32) for s in range(4)]
    lane = iota((8, LANES), 1)

    lane_rows = iota((rows, LANES), 1)
    starts = sent_starts(gx_count, cols)
    packed = [jnp.zeros((rows, LANES), jnp.float32) for _ in starts]
    if cols < LANES:
        wide[...] = jnp.zeros_like(wide)
    for f, l, slot in slots(count_f, count_l):
        if cols < LANES:
            wide[:, 0:cols] = fields[f, l]
            own = wide[...]
        else:
            own = fields[f, l]
        for n, start in enumerate(starts):
            moved = pltpu.roll(own, lax.rem(slot + LANES - start, LANES), 1)
            here = (lane_rows >= slot) & (lane_rows < slot + HALO)
            packed[n] = jnp.where(here, moved, packed[n])
    for payload, value in zip(payloads, packed):
        payload[...] = value

    def full(value):
        return jnp.full((8, LANES), value, jnp.float32)

    lane_taps = [full(0.0) for _ in range(2 * REACH)]
    lane_mix = [full(0.0) for _ in range(2 * count_f - 1)]
    lane_speed = full(0.0)
    for l in range(count_l):
        taps, mix, speed = level_weights(coupling, wind_x, wind_y, l, count_f)
        flat = taps + [entry for line in mix for entry in line] + [speed]
        for n, entry in enumerate(flat):
            weights[l, n] = full(entry)
        own_matrix[l] = own_band[jnp.where(wind_x[l] < 0.0, 1, 0)]
        for f in range(count_f):
            slot = HALO * (f * count_l + l)
            here = (lane >= slot) & (lane < slot + HALO)
            lane_taps = [jnp.where(here, tap, old) for tap, old in zip(taps, lane_taps)]
            lane_speed = jnp.where(here, speed, lane_speed)
            for g in range(count_f):
                at = g - f + count_f - 1
                lane_mix[at] = jnp.where(here, mix[f][g], lane_mix[at])
    for n, entry in enumerate(lane_taps + lane_mix + [lane_speed]):
        lane_weights[n] = entry
    for side, matrix in zip(side_ids(gx_count), side_matrix):
        side_bands(side, lane_speed[0:1, :], matrix)

    row_global = iota((wide_rows, LANES), 0) + (row_start - 8)
    row_weight = RELAX * (
        edge_weight(row_global, width[0]) + edge_weight(total_rows - 1 - row_global, width[1])
    )
    col_weight = RELAX * (
        edge_weight(lane + col_start, width[2])
        + edge_weight(total_cols - 1 - (lane + col_start), width[3])
    )
    row_relax[...] = row_weight
    relax[...] = row_weight + col_weight[0:1, :]
    inside[...] = jnp.where((row_global >= 0) & (row_global < total_rows), 1.0, 0.0)

    pos = iota((strip, LANES), 1)
    depth = iota((strip, LANES), 0)
    pick = jnp.concatenate([pos == depth, pos == depth + (cols - strip)], axis=0)
    pick = pick.astype(jnp.float32).astype(jnp.bfloat16)
    west_weight = RELAX * edge_weight(lane + col_start, width[2])
    east_weight = RELAX * edge_weight(total_cols - 1 - (lane + col_start), width[3])
    west_weight = jnp.where(lane < strip, west_weight, 0.0)
    east_weight = jnp.where((lane >= cols - strip) & (lane < cols), east_weight, 0.0)
    shift = lax.rem(8 + total_rows - row_start, total_rows)
    for f in range(count_f):
        for l in range(count_l):
            both = jnp.concatenate([west[f, l], east[f, l]], axis=0).astype(jnp.float32)
            both = pltpu.roll(both, shift, 1)[:, 0:LANES].astype(jnp.bfloat16)
            raw = lax.dot_general(
                both, pick, (((0,), (0,)), ((), ())), preferred_element_type=jnp.float32
            )
            factor = west_weight * scale[2, l, f] + east_weight * scale[3, l, f]
            drive[f, l] = raw[0:wide_rows] * factor[0:1, :]
    for ref in side_drive:
        ref[...] = jnp.zeros_like(ref)

    own_shift = lax.rem(total_cols - col_start, total_cols)
    for source, side, at, here in (
        (north, 0, 8, gy == 0),
        (south, 1, 8 + rows - strip, gy == gy_count - 1),
    ):

        @pl.when(here)
        def _(source=source, side=side, at=at):
            distance = depth if side == 0 else strip - 1 - depth
            weight = RELAX * edge_weight(distance, width[side])
            packed = [[jnp.zeros((strip, LANES), jnp.float32)] * 2 for _ in side_drive]
            for f, l, slot in slots(count_f, count_l):
                values = source[f, l].astype(jnp.float32)
                factor = weight * scale[side, l, f]
                own = pltpu.roll(values, own_shift, 1)[:, 0:LANES]
                drive[f, l, at : at + strip, :] = drive[f, l, at : at + strip, :] + factor * own
                held = (pos >= slot) & (pos < slot + HALO)
                for n, which in enumerate(side_ids(gx_count)):
                    for part, begin in enumerate(
                        (jnp.where(which == 0, cols, -HALO), jnp.where(which == 0, cols - HALO, 0))
                    ):
                        shift = slot + 2 * total_cols - begin - col_start
                        moved = pltpu.roll(values, lax.rem(shift, total_cols), 1)[:, 0:LANES]
                        packed[n][part] = jnp.where(held, factor * moved, packed[n][part])
            for ref, value in zip(side_drive, packed):
                for part in range(2):
                    ref[part, at : at + strip, :] = value[part]


def corner_slot(index, count, rows):
    planes = rows // PAD
    return HALO * (count + index // planes), PAD * (index % planes)


def pack_x_kernel(grid_sizes, first_round, second_round, *rest):
    gy_count, gx_count = grid_sizes
    sides = (len(rest) - 1) // 3
    payloads, outs, edges, ext = rest[:sides], rest[sides : 2 * sides], rest[2 * sides : -1], rest[-1]
    cols = first_round.shape[1]
    rows = payloads[0].shape[0]
    count = ext.shape[0]
    lane = iota((2 * PAD, LANES), 1)
    starts = sent_starts(gx_count, cols)
    packed = [jnp.zeros((2 * PAD, LANES), jnp.float32) for _ in starts]
    ext[...] = jnp.zeros_like(ext)
    blocks = [
        [payload[row : row + PAD, :] for row in range(0, rows, PAD)] for payload in payloads
    ]
    for index in range(count):
        slot = index * HALO
        corner, row = corner_slot(index, count, rows)
        north, south = halo_rows(gy_count, first_round, second_round, slot)
        ext[index, PAD - HALO : PAD, 0:cols] = north
        ext[index, PAD : PAD + HALO, 0:cols] = south
        for n, start in enumerate(starts):
            moved = pltpu.roll(ext[index], lax.rem(slot + LANES - start, LANES), 1)
            packed[n] = jnp.where((lane >= slot) & (lane < slot + HALO), moved, packed[n])
            near = ext[index, FIRST : FIRST + PAD, :]
            moved = pltpu.roll(near, lax.rem(corner + LANES - start, LANES), 1)
            here = (lane[0:PAD] >= corner) & (lane[0:PAD] < corner + HALO)
            blocks[n][row // PAD] = jnp.where(here, moved, blocks[n][row // PAD])
    for n, payload in enumerate(payloads):
        for block, value in enumerate(blocks[n]):
            outs[n][block * PAD : (block + 1) * PAD, :] = value
        edges[n][0:PAD, :] = packed[n][0:PAD]
        edges[n][PAD : PAD + rows, :] = payload[...]
        edges[n][PAD + rows : 2 * PAD + rows, :] = packed[n][PAD : 2 * PAD]


def loaded(weights, l, fac, count_f):
    flat = [fac * weights[l, n] for n in range(weights.shape[1])]
    taps, flat, speed = flat[: 2 * REACH], flat[2 * REACH : -1], flat[-1]
    return taps, [flat[f * count_f : (f + 1) * count_f] for f in range(count_f)], speed


def y_terms(rows_at, at, taps, total):
    offsets = [k for k in range(-REACH, REACH + 1) if k != 0]
    for tap, offset in zip(taps, offsets):
        total = total + tap * rows_at(at + offset)
    return total


def cell_terms(src, l, f, at, centers, weight, taps, mix, total):
    for g, center in enumerate(centers):
        total = total + (mix[f][g] - weight if g == f else mix[f][g]) * center
    return y_terms(lambda row: src[f, l, pl.ds(row, 8), :], at, taps, total)


def split(value):
    high = value.astype(jnp.bfloat16)
    return high, (value - high.astype(jnp.float32)).astype(jnp.bfloat16)


def x_divergence(src, l, first, height, matrix, xdiv):
    count_f = src.shape[0]
    whole = src[:, l, first : first + height, :].reshape(count_f * height, LANES)
    both = jnp.concatenate(split(whole), axis=1)
    twice = jnp.concatenate([matrix[l], matrix[l]], axis=0)
    moved = jnp.dot(both, twice, preferred_element_type=jnp.float32)
    xdiv[:, 0:height, :] = moved.reshape(count_f, height, LANES)


def begin_kernel(
    grid_sizes,
    fields,
    first_round,
    second_round,
    drive,
    relax,
    weights,
    own_matrix,
    after,
    *rest,
):
    gy_count, gx_count = grid_sizes
    far, (state, own_one, own_two, xdiv) = rest[:-4], rest[-4:]
    count_f, count_l, rows, cols = fields.shape
    wide_rows = relax.shape[0]
    gy = lax.axis_index("gy")
    pad_rows = jnp.zeros((PAD, LANES), jnp.float32)
    for f, l, slot in slots(count_f, count_l):
        north, south = halo_rows(gy_count, first_round, second_round, slot)
        if cols < LANES:
            state[f, l] = jnp.zeros(state.shape[2:], jnp.float32)
        else:
            state[f, l, 0:PAD, :] = pad_rows
            state[f, l, PAD + rows : 2 * PAD + rows, :] = pad_rows
        state[f, l, PAD - HALO : PAD, 0:cols] = north
        state[f, l, PAD : PAD + rows, 0:cols] = fields[f, l]
        state[f, l, PAD + rows : PAD + rows + HALO, 0:cols] = south
    lane = iota((wide_rows, LANES), 1)
    starts = edge_starts(gx_count, cols)[1]

    def keep_far(src, section):
        for ref, start in zip(far, starts):
            packed = jnp.zeros((wide_rows, LANES), jnp.float32)
            here = (lane >= start) & (lane < start + REACH)
            for f, l, slot in slots(count_f, count_l):
                kept = jnp.where(here, src[f, l, FIRST : FIRST + wide_rows, :], 0.0)
                packed = packed + pltpu.roll(kept, lax.rem(slot + LANES - start, LANES), 1)
            ref[section] = packed

    keep_far(state, 0)
    for section, (src, dst, fac) in enumerate(
        ((state, own_one, THIRD), (own_one, own_two, HALF), (own_two, after, 1.0))
    ):
        first, height = (PAD, rows) if dst is after else (FIRST, wide_rows)
        for l in range(count_l):
            x_divergence(src, l, first, height, own_matrix, xdiv)
            taps, mix, speed = loaded(weights, l, fac, count_f)
            for n in range(height // 8):
                at, row = first + n * 8, n * 8
                to = at - FIRST
                centers = [src[g, l, at : at + 8, :] for g in range(count_f)]
                weight = fac * relax[to : to + 8, :]
                for f in range(count_f):
                    base = centers[f] if src is state else state[f, l, at : at + 8, :]
                    total = base + fac * drive[f, l, to : to + 8, :]
                    total = total + speed * xdiv[f, row : row + 8, :]
                    total = cell_terms(src, l, f, at, centers, weight, taps, mix, total)
                    if dst is after:
                        after[f, l, row : row + 8, :] = total[:, 0:cols]
                    else:
                        dst[f, l, at : at + 8, :] = total
        if dst is not after:
            for row, here in ((FIRST, gy == 0), (PAD + rows, gy == gy_count - 1)):

                @pl.when(here)
                def _(dst=dst, row=row):
                    dst[:, :, row : row + 8, :] = jnp.zeros(
                        (count_f, count_l, 8, LANES), jnp.float32
                    )

            keep_far(dst, section + 1)


def finish_kernel(grid_sizes, sides, *refs):
    gy_count, gx_count = grid_sizes
    halos, edges, fars, side_drive, side_matrix = (
        refs[n * sides : (n + 1) * sides] for n in range(5)
    )
    after, row_relax, inside, lane_weights, out, outer, one, two = refs[5 * sides :]
    count_f, count_l, rows, cols = out.shape
    wide_rows = row_relax.shape[0]
    gx = lax.axis_index("gx")
    starts = edge_starts(gx_count, cols)[0]
    exists = [None] if sides == 1 else [gx > 0, gx < gx_count - 1]
    taps = [lane_weights[k] for k in range(2 * REACH)]
    mix = [lane_weights[2 * REACH + d] for d in range(2 * count_f - 1)]
    speed = lane_weights[lane_weights.shape[0] - 1]

    def unpack(halo):
        count = count_f * count_l
        outer[0:8, :] = jnp.zeros((8, LANES), jnp.float32)
        outer[PAD + rows + 8 : 2 * PAD + rows, :] = jnp.zeros((8, LANES), jnp.float32)
        lane = iota((rows, LANES), 1)
        outer[PAD : PAD + rows, :] = jnp.where(lane < HALO * count, halo[...], 0.0)
        lane = iota((PAD, LANES), 1)
        corners = jnp.zeros((PAD, LANES), jnp.float32)
        for index in range(count):
            slot = HALO * index
            corner, row = corner_slot(index, count, rows)
            moved = pltpu.roll(halo[row : row + PAD, :], (slot - corner) % LANES, 1)
            corners = jnp.where((lane >= slot) & (lane < slot + HALO), moved, corners)
        outer[8:PAD, :] = corners[0:8]
        outer[PAD + rows : PAD + rows + 8, :] = corners[8:PAD]

    def section(parts, s, fac, number, first, height, wanted, store):
        columns = [part[first : first + height, :] for part in parts]
        columns.append(fars[s][number, first - FIRST : first - FIRST + height, :])
        both = jnp.concatenate(split(jnp.concatenate(columns, axis=1)), axis=0)
        moved = jnp.dot(
            both, side_matrix[s][:, wanted[0] * LANES :], preferred_element_type=jnp.float32
        )
        rates = {}
        for which in wanted:
            part = parts[which]
            for n in range(height // 8):
                at = first + n * 8
                to = at - FIRST
                center = part[at : at + 8, :]
                rate = side_drive[s][which, to : to + 8, :] - row_relax[to : to + 8, :] * center
                rate = y_terms(lambda row: part[row : row + 8, :], at, taps, rate)
                for d, entry in enumerate(mix):
                    step = (d - (count_f - 1)) * HALO * count_l
                    other = pltpu.roll(center, -step % LANES, 1) if step else center
                    rate = rate + entry * other
                rates[which, n] = rate
        for place, which in enumerate(wanted):
            start = (outer, edges[s])[which]
            lanes = slice(place * LANES, (place + 1) * LANES)
            for n in range(height // 8):
                at, row = first + n * 8, n * 8
                x_rate = moved[row : row + 8, lanes] + moved[height + row : height + row + 8, lanes]
                rate = rates[which, n] + speed * x_rate
                store(which, at, at - FIRST, start[at : at + 8, :] + fac * rate)

    lane = iota((rows, LANES), 1)
    for s in range(sides):
        def keep(ref):
            def store(which, at, to, value):
                kept = inside[to : to + 8, :]
                if exists[s] is not None and which == 0:
                    kept = jnp.where(exists[s], kept, 0.0)
                ref[which, at : at + 8, :] = value * kept

            return store

        unpack(halos[s])
        section((outer, edges[s]), s, THIRD, 0, FIRST, wide_rows, (0, 1), keep(one))
        section((one.at[0], one.at[1]), s, HALF, 1, FIRST, wide_rows, (0, 1), keep(two))

        def last(which, at, to, value):
            one[0, at : at + 8, :] = value

        section((two.at[0], two.at[1]), s, 1.0, 2, PAD, rows, (1,), last)
        right = one[0, PAD : PAD + rows, :]
        near = (lane >= starts[s]) & (lane < starts[s] + HALO)
        if exists[s] is not None:
            near = near & exists[s]
        source = after if s == 0 else out
        for f, l, slot in slots(count_f, count_l):
            moved = pltpu.roll(right, lax.rem(starts[s] + LANES - slot, LANES), 1)
            out[f, l] = jnp.where(near[:, 0:cols], moved[:, 0:cols], source[f, l])


def pair_rounds(part_count, gy_count, gx_count):
    rounds = []
    for start in (0, 1):
        partner = {}
        for low in range(start, gy_count - 1, 2):
            partner[low], partner[low + 1] = low + 1, low
        pairs = []
        for place in np.ndindex(part_count, gy_count, gx_count):
            part, y, x = place
            if y in partner:
                to = part, partner[y], x
            elif part_count % 2 == 0:
                to = part ^ 1, y, x
            elif gx_count % 2 == 0:
                to = part, y, x ^ 1
            else:
                continue
            shape = (part_count, gy_count, gx_count)
            pairs.append(tuple(int(np.ravel_multi_index(at, shape)) for at in (place, to)))
        rounds.append(pairs)
    return rounds


def local(
    gy_count, gx_count, fields, wind_x, wind_y, coupling, north, south, west, east, strip_scale, widths
):
    count_f, count_l, rows, cols = fields.shape
    ext_rows = rows + 2 * PAD
    grid_sizes = (gy_count, gx_count)
    packed_rows = -(-HALO * count_f * count_l // 8) * 8
    vmem = pl.BlockSpec(memory_space=pltpu.VMEM)
    smem = pl.BlockSpec(memory_space=pltpu.SMEM)
    f32 = functools.partial(jax.ShapeDtypeStruct, dtype=jnp.float32)

    def call(body, name, out_shape, inputs, scratch=(), limit=4):
        several = isinstance(out_shape, tuple)
        return pl.pallas_call(
            body,
            out_shape=out_shape,
            in_specs=[space for _, space in inputs],
            out_specs=(vmem,) * len(out_shape) if several else vmem,
            scratch_shapes=list(scratch),
            compiler_params=pltpu.CompilerParams(vmem_limit_bytes=limit << 20),
            name=name,
        )(*[value for value, _ in inputs])

    def inputs(space, *values):
        return [(value, space) for value in values]

    strip_shape = f32((packed_rows, cols))
    sent_first, sent_second = call(
        pack_y_kernel, "pack_y", (strip_shape, strip_shape), inputs(vmem, fields)
    )
    axes = ("mem", "gy", "gx")
    first_pairs, second_pairs = pair_rounds(lax.axis_size("mem"), gy_count, gx_count)
    first_round = lax.ppermute(sent_first, axes, first_pairs)
    second_round = lax.ppermute(sent_second, axes, second_pairs)

    mixing = jnp.transpose(coupling, (1, 0, 2))
    scales = jnp.transpose(strip_scale, (0, 2, 1))
    sides = 1 if gx_count == 2 else 2
    wide_rows = rows + 16
    state_shape = (count_f, count_l, ext_rows, LANES)
    wide_shape = (count_f, count_l, wide_rows, LANES)
    plane = f32((wide_rows, LANES))
    matrix = functools.partial(jax.ShapeDtypeStruct, dtype=jnp.bfloat16)
    entries = 2 * REACH + count_f * count_f + 1
    lane_entries = 2 * REACH + 2 * count_f
    prepared = call(
        functools.partial(prepare_kernel, grid_sizes),
        "prepare",
        (f32(wide_shape), plane, plane, plane)
        + (f32((count_l, entries, 8, LANES)), f32((lane_entries, 8, LANES)))
        + (matrix((count_l, LANES, LANES)),)
        + (f32((rows, LANES)),) * sides
        + (f32((2, wide_rows, LANES)),) * sides
        + (matrix((3 * LANES, 2 * LANES)),) * sides,
        inputs(vmem, fields, north, south, jnp.swapaxes(west, 2, 3), jnp.swapaxes(east, 2, 3))
        + inputs(vmem, jnp.asarray(own_bands(cols), jnp.bfloat16))
        + inputs(smem, scales, widths, wind_x, wind_y, mixing),
        scratch=[pltpu.VMEM((rows, LANES), jnp.float32)],
    )
    drive, relax, row_relax, inside, weights, lane_weights, own_matrix = prepared[:7]
    payloads, side_drive, side_matrix = (
        prepared[7 + n * sides : 7 + (n + 1) * sides] for n in range(3)
    )

    packed_x = call(
        functools.partial(pack_x_kernel, grid_sizes),
        "pack_x",
        (f32((rows, LANES)),) * sides + (f32((ext_rows, LANES)),) * sides,
        inputs(vmem, first_round, second_round, *payloads),
        scratch=[pltpu.VMEM((count_f * count_l, 2 * PAD, LANES), jnp.float32)],
    )
    sent, edges = packed_x[:sides], packed_x[sides:]
    forward = [(i, i + 1) for i in range(gx_count - 1)]
    backward = [(b, a) for a, b in forward]
    if sides == 1:
        halos = [lax.ppermute(sent[0], "gx", forward + backward)]
    else:
        halos = [lax.ppermute(sent[0], "gx", forward), lax.ppermute(sent[1], "gx", backward)]

    state = pltpu.VMEM(state_shape, jnp.float32)
    after, *far = call(
        functools.partial(begin_kernel, grid_sizes),
        "begin",
        (f32(fields.shape),) + (f32((3, wide_rows, LANES)),) * sides,
        inputs(vmem, fields, first_round, second_round, drive, relax, weights, own_matrix),
        scratch=[state] * 3 + [pltpu.VMEM((count_f, wide_rows, LANES), jnp.float32)],
        limit=8,
    )
    pair = pltpu.VMEM((2, ext_rows, LANES), jnp.float32)
    return call(
        functools.partial(finish_kernel, grid_sizes, sides),
        "finish",
        f32(fields.shape),
        inputs(vmem, *halos, *edges[::-1], *far, *side_drive, *side_matrix)
        + inputs(vmem, after, row_relax, inside, lane_weights),
        scratch=[pltpu.VMEM((ext_rows, LANES), jnp.float32), pair, pair],
    )


def solution(mesh):
    return jax.shard_map(
        functools.partial(local, mesh.shape["gy"], mesh.shape["gx"]),
        mesh=mesh,
        in_specs=(
            P("mem", None, "gy", "gx"),
            P("mem"),
            P("mem"),
            P(),
            P("mem", None, None, None),
            P("mem", None, None, None),
            P("mem", None, None, None),
            P("mem", None, None, None),
            P("mem", None, None),
            P(),
        ),
        out_specs=P("mem", None, "gy", "gx"),
        check_vma=False,
    )
```

```python
import functools

import jax
import jax.numpy as jnp
import numpy as np
from jax import lax
from jax.experimental import pallas as pl
from jax.experimental.pallas import tpu as pltpu
from jax.sharding import PartitionSpec as P

RELAX = 0.25
REACH = 3
HALO = 3 * REACH
PAD = 16
LANES = 128
FIRST = PAD - 8
THIRD, HALF = 1.0 / 3.0, 0.5

UPWIND = (-2.0, 15.0, -60.0, 20.0, 30.0, -3.0, 0.0)
CENTRAL = (-1.0, 9.0, -45.0, 0.0, 45.0, -9.0, 1.0)
DAMPING = (1.0, -6.0, 15.0, -20.0, 15.0, -6.0, 1.0)


def own_bands(cols):
    bands = np.zeros((2, LANES, LANES), np.float32)
    for col in range(cols):
        for offset in range(-REACH, REACH + 1):
            if 0 <= col + offset < cols:
                bands[0, col + offset, col] = UPWIND[offset + REACH]
                bands[1, col + offset, col] = -UPWIND[REACH - offset]
    return bands


def iota(shape, dim):
    return lax.broadcasted_iota(jnp.int32, shape, dim)


def edge_weight(distance, width):
    dist = distance.astype(jnp.float32)
    inside = (dist >= 0.0) & (dist < width)
    return jnp.where(inside, jnp.square((width - dist) / width), 0.0)


def slots(count_f, count_l):
    return [(f, l, HALO * (f * count_l + l)) for f in range(count_f) for l in range(count_l)]


def pack_y_kernel(fields, first_round, second_round):
    count_f, count_l, rows, _ = fields.shape
    even = lax.rem(lax.axis_index("gy"), 2) == 0
    for f, l, slot in slots(count_f, count_l):
        top = fields[f, l, 0:HALO, :]
        bottom = fields[f, l, rows - HALO : rows, :]
        first_round[slot : slot + HALO, :] = jnp.where(even, bottom, top)
        second_round[slot : slot + HALO, :] = jnp.where(even, top, bottom)


def halo_rows(gy_count, first_round, second_round, slot):
    gy = lax.axis_index("gy")
    even = lax.rem(gy, 2) == 0
    first = first_round[slot : slot + HALO, :]
    second = second_round[slot : slot + HALO, :]
    north = jnp.where(gy == 0, 0.0, jnp.where(even, second, first))
    south = jnp.where(gy == gy_count - 1, 0.0, jnp.where(even, first, second))
    return north, south


def sent_starts(gx_count, cols):
    if gx_count == 2:
        return [jnp.where(lax.axis_index("gx") == 0, cols - HALO, 0)]
    return [cols - HALO, 0]


def side_ids(gx_count):
    if gx_count == 2:
        return [jnp.where(lax.axis_index("gx") == 0, 0, 1)]
    return [1, 0]


def edge_starts(gx_count, cols):
    near = [jnp.where(side == 0, cols - HALO, 0) for side in side_ids(gx_count)]
    far = [jnp.where(side == 0, cols - HALO - REACH, HALO) for side in side_ids(gx_count)]
    return near, far


def level_weights(coupling, wind_x, wind_y, l, count_f):
    speed, size = wind_y[l] / 60.0, jnp.abs(wind_y[l]) / 60.0
    taps = [size * DAMPING[k] - speed * CENTRAL[k] for k in range(2 * REACH + 1)]
    mix = [
        [coupling[f, l, g] + (taps[REACH] if f == g else 0.0) for g in range(count_f)]
        for f in range(count_f)
    ]
    return [tap for k, tap in enumerate(taps) if k != REACH], mix, -wind_x[l] / 60.0


def side_bands(side, lane_speed, matrix):
    shape = (LANES, LANES)
    row, col = iota(shape, 0), iota(shape, 1)
    row_plane, col_plane = (row * 57) >> 9, (col * 57) >> 9
    apart = (row - HALO * row_plane) - (col - HALO * col_plane)
    apart = jnp.where(row_plane == col_plane, apart, 4 * HALO)
    sign = jnp.where(lane_speed > 0.0, -1, 1)
    sign_float = sign.astype(jnp.float32)

    def block(base):
        offset = (apart + base) * sign
        value = jnp.zeros(shape, jnp.float32)
        for k, entry in enumerate(UPWIND[:-1]):
            value = jnp.where(offset == k - REACH, entry, value)
        return (value * sign_float).astype(jnp.bfloat16)

    here, step = block(0), jnp.where(side == 0, HALO, -HALO)
    matrix[0:LANES, 0:LANES] = here
    matrix[LANES : 2 * LANES, LANES:] = here
    matrix[LANES : 2 * LANES, 0:LANES] = block(-step)
    matrix[0:LANES, LANES:] = block(step)
    matrix[2 * LANES :, 0:LANES] = jnp.zeros(shape, jnp.bfloat16)
    matrix[2 * LANES :, LANES:] = block(jnp.where(side == 0, -REACH, HALO))


def prepare_kernel(
    grid_sizes,
    fields,
    north,
    south,
    west,
    east,
    own_band,
    scale,
    widths,
    wind_x,
    wind_y,
    coupling,
    drive,
    relax,
    row_relax,
    inside,
    weights,
    lane_weights,
    own_matrix,
    *rest,
):
    gy_count, gx_count = grid_sizes
    sides = (len(rest) - 1) // 3
    payloads, side_drive, side_matrix = rest[:sides], rest[sides : 2 * sides], rest[2 * sides : -1]
    wide = rest[-1]
    count_f, count_l, rows, cols = fields.shape
    wide_rows = relax.shape[0]
    strip = north.shape[2]
    total_rows, total_cols = rows * gy_count, cols * gx_count
    gy, gx = lax.axis_index("gy"), lax.axis_index("gx")
    row_start, col_start = gy * rows, gx * cols
    width = [widths[s].astype(jnp.float32) for s in range(4)]
    lane = iota((8, LANES), 1)

    lane_rows = iota((rows, LANES), 1)
    starts = sent_starts(gx_count, cols)
    packed = [jnp.zeros((rows, LANES), jnp.float32) for _ in starts]
    if cols < LANES:
        wide[...] = jnp.zeros_like(wide)
    for f, l, slot in slots(count_f, count_l):
        if cols < LANES:
            wide[:, 0:cols] = fields[f, l]
            own = wide[...]
        else:
            own = fields[f, l]
        for n, start in enumerate(starts):
            moved = pltpu.roll(own, lax.rem(slot + LANES - start, LANES), 1)
            here = (lane_rows >= slot) & (lane_rows < slot + HALO)
            packed[n] = jnp.where(here, moved, packed[n])
    for payload, value in zip(payloads, packed):
        payload[...] = value

    def full(value):
        return jnp.full((8, LANES), value, jnp.float32)

    lane_taps = [full(0.0) for _ in range(2 * REACH)]
    lane_mix = [full(0.0) for _ in range(2 * count_f - 1)]
    lane_speed = full(0.0)
    for l in range(count_l):
        taps, mix, speed = level_weights(coupling, wind_x, wind_y, l, count_f)
        flat = taps + [entry for line in mix for entry in line] + [speed]
        for n, entry in enumerate(flat):
            weights[l, n] = full(entry)
        own_matrix[l] = own_band[jnp.where(wind_x[l] < 0.0, 1, 0)]
        for f in range(count_f):
            slot = HALO * (f * count_l + l)
            here = (lane >= slot) & (lane < slot + HALO)
            lane_taps = [jnp.where(here, tap, old) for tap, old in zip(taps, lane_taps)]
            lane_speed = jnp.where(here, speed, lane_speed)
            for g in range(count_f):
                at = g - f + count_f - 1
                lane_mix[at] = jnp.where(here, mix[f][g], lane_mix[at])
    for n, entry in enumerate(lane_taps + lane_mix + [lane_speed]):
        lane_weights[n] = entry
    for side, matrix in zip(side_ids(gx_count), side_matrix):
        side_bands(side, lane_speed[0:1, :], matrix)

    row_global = iota((wide_rows, LANES), 0) + (row_start - 8)
    row_weight = RELAX * (
        edge_weight(row_global, width[0]) + edge_weight(total_rows - 1 - row_global, width[1])
    )
    col_weight = RELAX * (
        edge_weight(lane + col_start, width[2])
        + edge_weight(total_cols - 1 - (lane + col_start), width[3])
    )
    row_relax[...] = row_weight
    relax[...] = row_weight + col_weight[0:1, :]
    inside[...] = jnp.where((row_global >= 0) & (row_global < total_rows), 1.0, 0.0)

    pos = iota((strip, LANES), 1)
    depth = iota((strip, LANES), 0)
    pick = jnp.concatenate([pos == depth, pos == depth + (cols - strip)], axis=0)
    pick = pick.astype(jnp.float32).astype(jnp.bfloat16)
    west_weight = RELAX * edge_weight(lane + col_start, width[2])
    east_weight = RELAX * edge_weight(total_cols - 1 - (lane + col_start), width[3])
    west_weight = jnp.where(lane < strip, west_weight, 0.0)
    east_weight = jnp.where((lane >= cols - strip) & (lane < cols), east_weight, 0.0)
    shift = lax.rem(8 + total_rows - row_start, total_rows)
    for f in range(count_f):
        for l in range(count_l):
            both = jnp.concatenate([west[f, l], east[f, l]], axis=0).astype(jnp.float32)
            both = pltpu.roll(both, shift, 1)[:, 0:LANES].astype(jnp.bfloat16)
            raw = lax.dot_general(
                both, pick, (((0,), (0,)), ((), ())), preferred_element_type=jnp.float32
            )
            factor = west_weight * scale[2, l, f] + east_weight * scale[3, l, f]
            drive[f, l] = raw[0:wide_rows] * factor[0:1, :]
    for ref in side_drive:
        ref[...] = jnp.zeros_like(ref)

    own_shift = lax.rem(total_cols - col_start, total_cols)
    for source, side, at, here in (
        (north, 0, 8, gy == 0),
        (south, 1, 8 + rows - strip, gy == gy_count - 1),
    ):

        @pl.when(here)
        def _(source=source, side=side, at=at):
            distance = depth if side == 0 else strip - 1 - depth
            weight = RELAX * edge_weight(distance, width[side])
            packed = [[jnp.zeros((strip, LANES), jnp.float32)] * 2 for _ in side_drive]
            for f, l, slot in slots(count_f, count_l):
                values = source[f, l].astype(jnp.float32)
                factor = weight * scale[side, l, f]
                own = pltpu.roll(values, own_shift, 1)[:, 0:LANES]
                drive[f, l, at : at + strip, :] = drive[f, l, at : at + strip, :] + factor * own
                held = (pos >= slot) & (pos < slot + HALO)
                for n, which in enumerate(side_ids(gx_count)):
                    for part, begin in enumerate(
                        (jnp.where(which == 0, cols, -HALO), jnp.where(which == 0, cols - HALO, 0))
                    ):
                        shift = slot + 2 * total_cols - begin - col_start
                        moved = pltpu.roll(values, lax.rem(shift, total_cols), 1)[:, 0:LANES]
                        packed[n][part] = jnp.where(held, factor * moved, packed[n][part])
            for ref, value in zip(side_drive, packed):
                for part in range(2):
                    ref[part, at : at + strip, :] = value[part]


def corner_slot(index, count, rows):
    planes = rows // PAD
    return HALO * (count + index // planes), PAD * (index % planes)


def pack_x_kernel(grid_sizes, first_round, second_round, *rest):
    gy_count, gx_count = grid_sizes
    sides = (len(rest) - 1) // 3
    payloads, outs, edges, ext = rest[:sides], rest[sides : 2 * sides], rest[2 * sides : -1], rest[-1]
    cols = first_round.shape[1]
    rows = payloads[0].shape[0]
    count = ext.shape[0]
    lane = iota((2 * PAD, LANES), 1)
    starts = sent_starts(gx_count, cols)
    packed = [jnp.zeros((2 * PAD, LANES), jnp.float32) for _ in starts]
    ext[...] = jnp.zeros_like(ext)
    blocks = [
        [payload[row : row + PAD, :] for row in range(0, rows, PAD)] for payload in payloads
    ]
    for index in range(count):
        slot = index * HALO
        corner, row = corner_slot(index, count, rows)
        north, south = halo_rows(gy_count, first_round, second_round, slot)
        ext[index, PAD - HALO : PAD, 0:cols] = north
        ext[index, PAD : PAD + HALO, 0:cols] = south
        for n, start in enumerate(starts):
            moved = pltpu.roll(ext[index], lax.rem(slot + LANES - start, LANES), 1)
            packed[n] = jnp.where((lane >= slot) & (lane < slot + HALO), moved, packed[n])
            near = ext[index, FIRST : FIRST + PAD, :]
            moved = pltpu.roll(near, lax.rem(corner + LANES - start, LANES), 1)
            here = (lane[0:PAD] >= corner) & (lane[0:PAD] < corner + HALO)
            blocks[n][row // PAD] = jnp.where(here, moved, blocks[n][row // PAD])
    for n, payload in enumerate(payloads):
        for block, value in enumerate(blocks[n]):
            outs[n][block * PAD : (block + 1) * PAD, :] = value
        edges[n][0:PAD, :] = packed[n][0:PAD]
        edges[n][PAD : PAD + rows, :] = payload[...]
        edges[n][PAD + rows : 2 * PAD + rows, :] = packed[n][PAD : 2 * PAD]


def loaded(weights, l, fac, count_f):
    flat = [fac * weights[l, n] for n in range(weights.shape[1])]
    taps, flat, speed = flat[: 2 * REACH], flat[2 * REACH : -1], flat[-1]
    return taps, [flat[f * count_f : (f + 1) * count_f] for f in range(count_f)], speed


def y_terms(rows_at, at, taps, total):
    offsets = [k for k in range(-REACH, REACH + 1) if k != 0]
    for tap, offset in zip(taps, offsets):
        total = total + tap * rows_at(at + offset)
    return total


def cell_terms(src, l, f, at, centers, weight, taps, mix, total):
    for g, center in enumerate(centers):
        total = total + (mix[f][g] - weight if g == f else mix[f][g]) * center
    return y_terms(lambda row: src[f, l, pl.ds(row, 8), :], at, taps, total)


def split(value):
    high = value.astype(jnp.bfloat16)
    return high, (value - high.astype(jnp.float32)).astype(jnp.bfloat16)


def x_divergence(src, l, first, height, matrix, xdiv):
    count_f = src.shape[0]
    whole = src[:, l, first : first + height, :].reshape(count_f * height, LANES)
    both = jnp.concatenate(split(whole), axis=1)
    twice = jnp.concatenate([matrix[l], matrix[l]], axis=0)
    moved = jnp.dot(both, twice, preferred_element_type=jnp.float32)
    xdiv[:, 0:height, :] = moved.reshape(count_f, height, LANES)


def packed_rate(part, at, forced, row_relax, lane_weights, count_f, count_l):
    to = at - FIRST
    center = part[at : at + 8, :]
    rate = forced - row_relax[to : to + 8, :] * center
    taps = [lane_weights[k] for k in range(2 * REACH)]
    rate = y_terms(lambda row: part[row : row + 8, :], at, taps, rate)
    for d in range(2 * count_f - 1):
        step = (d - (count_f - 1)) * HALO * count_l
        other = pltpu.roll(center, -step % LANES, 1) if step else center
        rate = rate + lane_weights[2 * REACH + d] * other
    return rate


def begin_kernel(
    grid_sizes,
    fields,
    first_round,
    second_round,
    drive,
    relax,
    weights,
    own_matrix,
    row_relax,
    lane_weights,
    *rest,
):
    gy_count, gx_count = grid_sizes
    sides = (len(rest) - 5) // 4
    edges, side_drive, after = rest[:sides], rest[sides : 2 * sides], rest[2 * sides]
    far, edge_one = rest[2 * sides + 1 : 3 * sides + 1], rest[3 * sides + 1 : -4]
    state, own_one, own_two, xdiv = rest[-4:]
    count_f, count_l, rows, cols = fields.shape
    wide_rows = relax.shape[0]
    gy = lax.axis_index("gy")
    pad_rows = jnp.zeros((PAD, LANES), jnp.float32)
    for f, l, slot in slots(count_f, count_l):
        north, south = halo_rows(gy_count, first_round, second_round, slot)
        if cols < LANES:
            state[f, l] = jnp.zeros(state.shape[2:], jnp.float32)
        else:
            state[f, l, 0:PAD, :] = pad_rows
            state[f, l, PAD + rows : 2 * PAD + rows, :] = pad_rows
        state[f, l, PAD - HALO : PAD, 0:cols] = north
        state[f, l, PAD : PAD + rows, 0:cols] = fields[f, l]
        state[f, l, PAD + rows : PAD + rows + HALO, 0:cols] = south
    lane = iota((wide_rows, LANES), 1)
    starts = edge_starts(gx_count, cols)[1]

    def keep_far(src, section):
        for ref, start in zip(far, starts):
            packed = jnp.zeros((wide_rows, LANES), jnp.float32)
            here = (lane >= start) & (lane < start + REACH)
            for f, l, slot in slots(count_f, count_l):
                kept = jnp.where(here, src[f, l, FIRST : FIRST + wide_rows, :], 0.0)
                packed = packed + pltpu.roll(kept, lax.rem(slot + LANES - start, LANES), 1)
            ref[section] = packed

    keep_far(state, 0)
    for edge, forced, ref in zip(edges, side_drive, edge_one):
        for to in range(0, wide_rows, 8):
            rate = packed_rate(edge, FIRST + to, forced[1, to : to + 8, :], row_relax, lane_weights, count_f, count_l)
            ref[to : to + 8, :] = edge[FIRST + to : FIRST + to + 8, :] + THIRD * rate
    for section, (src, dst, fac) in enumerate(
        ((state, own_one, THIRD), (own_one, own_two, HALF), (own_two, after, 1.0))
    ):
        first, height = (PAD, rows) if dst is after else (FIRST, wide_rows)
        for l in range(count_l):
            x_divergence(src, l, first, height, own_matrix, xdiv)
            taps, mix, speed = loaded(weights, l, fac, count_f)
            for n in range(height // 8):
                at, row = first + n * 8, n * 8
                to = at - FIRST
                centers = [src[g, l, at : at + 8, :] for g in range(count_f)]
                weight = fac * relax[to : to + 8, :]
                for f in range(count_f):
                    base = centers[f] if src is state else state[f, l, at : at + 8, :]
                    total = base + fac * drive[f, l, to : to + 8, :]
                    total = total + speed * xdiv[f, row : row + 8, :]
                    total = cell_terms(src, l, f, at, centers, weight, taps, mix, total)
                    if dst is after:
                        after[f, l, row : row + 8, :] = total[:, 0:cols]
                    else:
                        dst[f, l, at : at + 8, :] = total
        if dst is not after:
            for row, here in ((FIRST, gy == 0), (PAD + rows, gy == gy_count - 1)):

                @pl.when(here)
                def _(dst=dst, row=row):
                    dst[:, :, row : row + 8, :] = jnp.zeros(
                        (count_f, count_l, 8, LANES), jnp.float32
                    )

            keep_far(dst, section + 1)


def finish_kernel(grid_sizes, sides, *refs):
    gy_count, gx_count = grid_sizes
    halos, edges, fars, edge_one, side_drive, side_matrix = (
        refs[n * sides : (n + 1) * sides] for n in range(6)
    )
    after, row_relax, inside, lane_weights, out, outer, one, two = refs[6 * sides :]
    count_f, count_l, rows, cols = out.shape
    wide_rows = row_relax.shape[0]
    gx = lax.axis_index("gx")
    starts = edge_starts(gx_count, cols)[0]
    exists = [None] if sides == 1 else [gx > 0, gx < gx_count - 1]
    speed = lane_weights[lane_weights.shape[0] - 1]

    def unpack(halo):
        count = count_f * count_l
        outer[0:8, :] = jnp.zeros((8, LANES), jnp.float32)
        outer[PAD + rows + 8 : 2 * PAD + rows, :] = jnp.zeros((8, LANES), jnp.float32)
        lane = iota((rows, LANES), 1)
        outer[PAD : PAD + rows, :] = jnp.where(lane < HALO * count, halo[...], 0.0)
        lane = iota((PAD, LANES), 1)
        corners = jnp.zeros((PAD, LANES), jnp.float32)
        for index in range(count):
            slot = HALO * index
            corner, row = corner_slot(index, count, rows)
            moved = pltpu.roll(halo[row : row + PAD, :], (slot - corner) % LANES, 1)
            corners = jnp.where((lane >= slot) & (lane < slot + HALO), moved, corners)
        outer[8:PAD, :] = corners[0:8]
        outer[PAD + rows : PAD + rows + 8, :] = corners[8:PAD]

    def section(parts, s, fac, number, first, height, wanted, store):
        columns = [part[first : first + height, :] for part in parts]
        columns.append(fars[s][number, first - FIRST : first - FIRST + height, :])
        both = jnp.concatenate(split(jnp.concatenate(columns, axis=1)), axis=1)
        matrix = side_matrix[s][:, wanted[0] * LANES :]
        moved = jnp.dot(
            both, jnp.concatenate([matrix, matrix], axis=0), preferred_element_type=jnp.float32
        )
        places = []
        for place, which in enumerate(wanted):
            short = number == 1 and which == 0
            for n in range(short, height // 8 - short):
                at = first + n * 8
                rate = None
                if number > 0 or which == 0:
                    forced = side_drive[s][which, at - FIRST : at - FIRST + 8, :]
                    rate = packed_rate(
                        parts[which], at, forced, row_relax, lane_weights, count_f, count_l
                    )
                places.append((place, which, n, at, rate))
        for place, which, n, at, rate in places:
            lanes, row = slice(place * LANES, (place + 1) * LANES), n * 8
            x_rate = moved[row : row + 8, lanes]
            if rate is None:
                value = edge_one[s][row : row + 8, :] + fac * (speed * x_rate)
            else:
                start = (outer, edges[s])[which]
                value = start[at : at + 8, :] + fac * (rate + speed * x_rate)
            store(which, at, at - FIRST, value)

    lane = iota((rows, LANES), 1)
    for s in range(sides):
        def keep(ref):
            def store(which, at, to, value):
                kept = inside[to : to + 8, :]
                if exists[s] is not None and which == 0:
                    kept = jnp.where(exists[s], kept, 0.0)
                ref[which, at : at + 8, :] = value * kept

            return store

        unpack(halos[s])
        section((outer, edges[s]), s, THIRD, 0, FIRST, wide_rows, (0, 1), keep(one))
        section((one.at[0], one.at[1]), s, HALF, 1, FIRST, wide_rows, (0, 1), keep(two))

        def last(which, at, to, value):
            one[0, at : at + 8, :] = value

        section((two.at[0], two.at[1]), s, 1.0, 2, PAD, rows, (1,), last)
        right = one[0, PAD : PAD + rows, :]
        near = (lane >= starts[s]) & (lane < starts[s] + HALO)
        if exists[s] is not None:
            near = near & exists[s]
        source = after if s == 0 else out
        for f, l, slot in slots(count_f, count_l):
            moved = pltpu.roll(right, lax.rem(starts[s] + LANES - slot, LANES), 1)
            out[f, l] = jnp.where(near[:, 0:cols], moved[:, 0:cols], source[f, l])


def pair_rounds(part_count, gy_count, gx_count):
    rounds = []
    for start in (0, 1):
        partner = {}
        for low in range(start, gy_count - 1, 2):
            partner[low], partner[low + 1] = low + 1, low
        pairs = []
        for place in np.ndindex(part_count, gy_count, gx_count):
            part, y, x = place
            if y in partner:
                to = part, partner[y], x
            elif part_count % 2 == 0:
                to = part ^ 1, y, x
            elif gx_count % 2 == 0:
                to = part, y, x ^ 1
            else:
                continue
            shape = (part_count, gy_count, gx_count)
            pairs.append(tuple(int(np.ravel_multi_index(at, shape)) for at in (place, to)))
        rounds.append(pairs)
    return rounds


def local(
    gy_count, gx_count, fields, wind_x, wind_y, coupling, north, south, west, east, strip_scale, widths
):
    count_f, count_l, rows, cols = fields.shape
    ext_rows = rows + 2 * PAD
    grid_sizes = (gy_count, gx_count)
    packed_rows = -(-HALO * count_f * count_l // 8) * 8
    vmem = pl.BlockSpec(memory_space=pltpu.VMEM)
    smem = pl.BlockSpec(memory_space=pltpu.SMEM)
    f32 = functools.partial(jax.ShapeDtypeStruct, dtype=jnp.float32)

    def call(body, name, out_shape, inputs, scratch=(), limit=4):
        several = isinstance(out_shape, tuple)
        return pl.pallas_call(
            body,
            out_shape=out_shape,
            in_specs=[space for _, space in inputs],
            out_specs=(vmem,) * len(out_shape) if several else vmem,
            scratch_shapes=list(scratch),
            compiler_params=pltpu.CompilerParams(vmem_limit_bytes=limit << 20),
            name=name,
        )(*[value for value, _ in inputs])

    def inputs(space, *values):
        return [(value, space) for value in values]

    strip_shape = f32((packed_rows, cols))
    sent_first, sent_second = call(
        pack_y_kernel, "pack_y", (strip_shape, strip_shape), inputs(vmem, fields)
    )
    axes = ("mem", "gy", "gx")
    first_pairs, second_pairs = pair_rounds(lax.axis_size("mem"), gy_count, gx_count)
    first_round = lax.ppermute(sent_first, axes, first_pairs)
    second_round = lax.ppermute(sent_second, axes, second_pairs)

    mixing = jnp.transpose(coupling, (1, 0, 2))
    scales = jnp.transpose(strip_scale, (0, 2, 1))
    sides = 1 if gx_count == 2 else 2
    wide_rows = rows + 16
    state_shape = (count_f, count_l, ext_rows, LANES)
    wide_shape = (count_f, count_l, wide_rows, LANES)
    plane = f32((wide_rows, LANES))
    matrix = functools.partial(jax.ShapeDtypeStruct, dtype=jnp.bfloat16)
    entries = 2 * REACH + count_f * count_f + 1
    lane_entries = 2 * REACH + 2 * count_f
    prepared = call(
        functools.partial(prepare_kernel, grid_sizes),
        "prepare",
        (f32(wide_shape), plane, plane, plane)
        + (f32((count_l, entries, 8, LANES)), f32((lane_entries, 8, LANES)))
        + (matrix((count_l, LANES, LANES)),)
        + (f32((rows, LANES)),) * sides
        + (f32((2, wide_rows, LANES)),) * sides
        + (matrix((3 * LANES, 2 * LANES)),) * sides,
        inputs(vmem, fields, north, south, jnp.swapaxes(west, 2, 3), jnp.swapaxes(east, 2, 3))
        + inputs(vmem, jnp.asarray(own_bands(cols), jnp.bfloat16))
        + inputs(smem, scales, widths, wind_x, wind_y, mixing),
        scratch=[pltpu.VMEM((rows, LANES), jnp.float32)],
    )
    drive, relax, row_relax, inside, weights, lane_weights, own_matrix = prepared[:7]
    payloads, side_drive, side_matrix = (
        prepared[7 + n * sides : 7 + (n + 1) * sides] for n in range(3)
    )

    packed_x = call(
        functools.partial(pack_x_kernel, grid_sizes),
        "pack_x",
        (f32((rows, LANES)),) * sides + (f32((ext_rows, LANES)),) * sides,
        inputs(vmem, first_round, second_round, *payloads),
        scratch=[pltpu.VMEM((count_f * count_l, 2 * PAD, LANES), jnp.float32)],
    )
    sent, edges = packed_x[:sides], packed_x[sides:]
    forward = [(i, i + 1) for i in range(gx_count - 1)]
    backward = [(b, a) for a, b in forward]
    if sides == 1:
        halos = [lax.ppermute(sent[0], "gx", forward + backward)]
    else:
        halos = [lax.ppermute(sent[0], "gx", forward), lax.ppermute(sent[1], "gx", backward)]

    state = pltpu.VMEM(state_shape, jnp.float32)
    edges = edges[::-1]
    after, *begun = call(
        functools.partial(begin_kernel, grid_sizes),
        "begin",
        (f32(fields.shape),) + (f32((3, wide_rows, LANES)),) * sides + (plane,) * sides,
        inputs(vmem, fields, first_round, second_round, drive, relax, weights, own_matrix)
        + inputs(vmem, row_relax, lane_weights, *edges, *side_drive),
        scratch=[state] * 3 + [pltpu.VMEM((count_f, wide_rows, LANES), jnp.float32)],
        limit=8,
    )
    pair = pltpu.VMEM((2, ext_rows, LANES), jnp.float32)
    return call(
        functools.partial(finish_kernel, grid_sizes, sides),
        "finish",
        f32(fields.shape),
        inputs(vmem, *halos, *edges, *begun, *side_drive, *side_matrix)
        + inputs(vmem, after, row_relax, inside, lane_weights),
        scratch=[pltpu.VMEM((ext_rows, LANES), jnp.float32), pair, pair],
    )


def solution(mesh):
    return jax.shard_map(
        functools.partial(local, mesh.shape["gy"], mesh.shape["gx"]),
        mesh=mesh,
        in_specs=(
            P("mem", None, "gy", "gx"),
            P("mem"),
            P("mem"),
            P(),
            P("mem", None, None, None),
            P("mem", None, None, None),
            P("mem", None, None, None),
            P("mem", None, None, None),
            P("mem", None, None),
            P(),
        ),
        out_specs=P("mem", None, "gy", "gx"),
        check_vma=False,
    )
```

```python
import functools

import jax
import jax.numpy as jnp
import numpy as np
from jax import lax
from jax.experimental import pallas as pl
from jax.experimental.pallas import tpu as pltpu
from jax.sharding import PartitionSpec as P

RELAX = 0.25
REACH = 3
HALO = 3 * REACH
PAD = 16
LANES = 128
FIRST = PAD - 8
THIRD, HALF = 1.0 / 3.0, 0.5

UPWIND = (-2.0, 15.0, -60.0, 20.0, 30.0, -3.0, 0.0)
CENTRAL = (-1.0, 9.0, -45.0, 0.0, 45.0, -9.0, 1.0)
DAMPING = (1.0, -6.0, 15.0, -20.0, 15.0, -6.0, 1.0)


def own_bands(cols):
    bands = np.zeros((2, LANES, LANES), np.float32)
    for col in range(cols):
        for offset in range(-REACH, REACH + 1):
            if 0 <= col + offset < cols:
                bands[0, col + offset, col] = UPWIND[offset + REACH]
                bands[1, col + offset, col] = -UPWIND[REACH - offset]
    return bands


def iota(shape, dim):
    return lax.broadcasted_iota(jnp.int32, shape, dim)


def edge_weight(distance, width):
    dist = distance.astype(jnp.float32)
    inside = (dist >= 0.0) & (dist < width)
    return jnp.where(inside, jnp.square((width - dist) / width), 0.0)


def slots(count_f, count_l):
    return [(f, l, HALO * (f * count_l + l)) for f in range(count_f) for l in range(count_l)]


def pack_y_kernel(fields, first_round, second_round):
    count_f, count_l, rows, _ = fields.shape
    even = lax.rem(lax.axis_index("gy"), 2) == 0
    for f, l, slot in slots(count_f, count_l):
        top = fields[f, l, 0:HALO, :]
        bottom = fields[f, l, rows - HALO : rows, :]
        first_round[slot : slot + HALO, :] = jnp.where(even, bottom, top)
        second_round[slot : slot + HALO, :] = jnp.where(even, top, bottom)


def halo_rows(gy_count, first_round, second_round, slot):
    gy = lax.axis_index("gy")
    even = lax.rem(gy, 2) == 0
    first = first_round[slot : slot + HALO, :]
    second = second_round[slot : slot + HALO, :]
    north = jnp.where(gy == 0, 0.0, jnp.where(even, second, first))
    south = jnp.where(gy == gy_count - 1, 0.0, jnp.where(even, first, second))
    return north, south


def sent_starts(gx_count, cols):
    if gx_count == 2:
        return [jnp.where(lax.axis_index("gx") == 0, cols - HALO, 0)]
    return [cols - HALO, 0]


def side_ids(gx_count):
    if gx_count == 2:
        return [jnp.where(lax.axis_index("gx") == 0, 0, 1)]
    return [1, 0]


def edge_starts(gx_count, cols):
    near = [jnp.where(side == 0, cols - HALO, 0) for side in side_ids(gx_count)]
    far = [jnp.where(side == 0, cols - HALO - REACH, HALO) for side in side_ids(gx_count)]
    return near, far


def level_weights(coupling, wind_x, wind_y, l, count_f):
    speed, size = wind_y[l] / 60.0, jnp.abs(wind_y[l]) / 60.0
    taps = [size * DAMPING[k] - speed * CENTRAL[k] for k in range(2 * REACH + 1)]
    mix = [
        [coupling[f, l, g] + (taps[REACH] if f == g else 0.0) for g in range(count_f)]
        for f in range(count_f)
    ]
    return [tap for k, tap in enumerate(taps) if k != REACH], mix, -wind_x[l] / 60.0


def side_bands(side, lane_speed, matrix):
    shape = (LANES, LANES)
    row, col = iota(shape, 0), iota(shape, 1)
    row_plane, col_plane = (row * 57) >> 9, (col * 57) >> 9
    apart = (row - HALO * row_plane) - (col - HALO * col_plane)
    apart = jnp.where(row_plane == col_plane, apart, 4 * HALO)
    sign = jnp.where(lane_speed > 0.0, -1, 1)
    sign_float = sign.astype(jnp.float32)

    def block(base):
        offset = (apart + base) * sign
        value = jnp.zeros(shape, jnp.float32)
        for k, entry in enumerate(UPWIND[:-1]):
            value = jnp.where(offset == k - REACH, entry, value)
        return (value * sign_float).astype(jnp.bfloat16)

    here, step = block(0), jnp.where(side == 0, HALO, -HALO)
    matrix[0:LANES, 0:LANES] = here
    matrix[LANES : 2 * LANES, LANES:] = here
    matrix[LANES : 2 * LANES, 0:LANES] = block(-step)
    matrix[0:LANES, LANES:] = block(step)
    matrix[2 * LANES :, 0:LANES] = jnp.zeros(shape, jnp.bfloat16)
    matrix[2 * LANES :, LANES:] = block(jnp.where(side == 0, -REACH, HALO))


def prepare_kernel(
    grid_sizes,
    fields,
    north,
    south,
    west,
    east,
    own_band,
    scale,
    widths,
    wind_x,
    wind_y,
    coupling,
    drive,
    relax,
    row_relax,
    inside,
    weights,
    lane_weights,
    own_matrix,
    *rest,
):
    gy_count, gx_count = grid_sizes
    sides = (len(rest) - 1) // 3
    payloads, side_drive, side_matrix = rest[:sides], rest[sides : 2 * sides], rest[2 * sides : -1]
    wide = rest[-1]
    count_f, count_l, rows, cols = fields.shape
    wide_rows = relax.shape[0]
    strip = north.shape[2]
    total_rows, total_cols = rows * gy_count, cols * gx_count
    gy, gx = lax.axis_index("gy"), lax.axis_index("gx")
    row_start, col_start = gy * rows, gx * cols
    width = [widths[s].astype(jnp.float32) for s in range(4)]
    lane = iota((8, LANES), 1)

    lane_rows = iota((rows, LANES), 1)
    starts = sent_starts(gx_count, cols)
    packed = [jnp.zeros((rows, LANES), jnp.float32) for _ in starts]
    if cols < LANES:
        wide[...] = jnp.zeros_like(wide)
    for f, l, slot in slots(count_f, count_l):
        if cols < LANES:
            wide[:, 0:cols] = fields[f, l]
            own = wide[...]
        else:
            own = fields[f, l]
        for n, start in enumerate(starts):
            moved = pltpu.roll(own, lax.rem(slot + LANES - start, LANES), 1)
            here = (lane_rows >= slot) & (lane_rows < slot + HALO)
            packed[n] = jnp.where(here, moved, packed[n])
    for payload, value in zip(payloads, packed):
        payload[...] = value

    def full(value):
        return jnp.full((8, LANES), value, jnp.float32)

    lane_taps = [full(0.0) for _ in range(2 * REACH)]
    lane_mix = [full(0.0) for _ in range(2 * count_f - 1)]
    lane_speed = full(0.0)
    for l in range(count_l):
        taps, mix, speed = level_weights(coupling, wind_x, wind_y, l, count_f)
        flat = taps + [entry for line in mix for entry in line] + [speed]
        for n, entry in enumerate(flat):
            weights[l, n] = full(entry)
        own_matrix[l] = own_band[jnp.where(wind_x[l] < 0.0, 1, 0)]
        for f in range(count_f):
            slot = HALO * (f * count_l + l)
            here = (lane >= slot) & (lane < slot + HALO)
            lane_taps = [jnp.where(here, tap, old) for tap, old in zip(taps, lane_taps)]
            lane_speed = jnp.where(here, speed, lane_speed)
            for g in range(count_f):
                at = g - f + count_f - 1
                lane_mix[at] = jnp.where(here, mix[f][g], lane_mix[at])
    for n, entry in enumerate(lane_taps + lane_mix + [lane_speed]):
        lane_weights[n] = entry
    for side, matrix in zip(side_ids(gx_count), side_matrix):
        side_bands(side, lane_speed[0:1, :], matrix)

    row_global = iota((wide_rows, LANES), 0) + (row_start - 8)
    row_weight = RELAX * (
        edge_weight(row_global, width[0]) + edge_weight(total_rows - 1 - row_global, width[1])
    )
    col_weight = RELAX * (
        edge_weight(lane + col_start, width[2])
        + edge_weight(total_cols - 1 - (lane + col_start), width[3])
    )
    row_relax[...] = row_weight
    relax[...] = row_weight + col_weight[0:1, :]
    inside[...] = jnp.where((row_global >= 0) & (row_global < total_rows), 1.0, 0.0)

    pos = iota((strip, LANES), 1)
    depth = iota((strip, LANES), 0)
    pick = jnp.concatenate([pos == depth, pos == depth + (cols - strip)], axis=0)
    pick = pick.astype(jnp.float32).astype(jnp.bfloat16)
    west_weight = RELAX * edge_weight(lane + col_start, width[2])
    east_weight = RELAX * edge_weight(total_cols - 1 - (lane + col_start), width[3])
    west_weight = jnp.where(lane < strip, west_weight, 0.0)
    east_weight = jnp.where((lane >= cols - strip) & (lane < cols), east_weight, 0.0)
    shift = lax.rem(8 + total_rows - row_start, total_rows)
    for f in range(count_f):
        for l in range(count_l):
            both = jnp.concatenate([west[f, l], east[f, l]], axis=0).astype(jnp.float32)
            both = pltpu.roll(both, shift, 1)[:, 0:LANES].astype(jnp.bfloat16)
            raw = lax.dot_general(
                both, pick, (((0,), (0,)), ((), ())), preferred_element_type=jnp.float32
            )
            factor = west_weight * scale[2, l, f] + east_weight * scale[3, l, f]
            drive[f, l] = raw[0:wide_rows] * factor[0:1, :]
    for ref in side_drive:
        ref[...] = jnp.zeros_like(ref)

    own_shift = lax.rem(total_cols - col_start, total_cols)
    for source, side, at, here in (
        (north, 0, 8, gy == 0),
        (south, 1, 8 + rows - strip, gy == gy_count - 1),
    ):

        @pl.when(here)
        def _(source=source, side=side, at=at):
            distance = depth if side == 0 else strip - 1 - depth
            weight = RELAX * edge_weight(distance, width[side])
            packed = [[jnp.zeros((strip, LANES), jnp.float32)] * 2 for _ in side_drive]
            for f, l, slot in slots(count_f, count_l):
                values = source[f, l].astype(jnp.float32)
                factor = weight * scale[side, l, f]
                own = pltpu.roll(values, own_shift, 1)[:, 0:LANES]
                drive[f, l, at : at + strip, :] = drive[f, l, at : at + strip, :] + factor * own
                held = (pos >= slot) & (pos < slot + HALO)
                for n, which in enumerate(side_ids(gx_count)):
                    for part, begin in enumerate(
                        (jnp.where(which == 0, cols, -HALO), jnp.where(which == 0, cols - HALO, 0))
                    ):
                        shift = slot + 2 * total_cols - begin - col_start
                        moved = pltpu.roll(values, lax.rem(shift, total_cols), 1)[:, 0:LANES]
                        packed[n][part] = jnp.where(held, factor * moved, packed[n][part])
            for ref, value in zip(side_drive, packed):
                for part in range(2):
                    ref[part, at : at + strip, :] = value[part]


def corner_slot(index, count, rows):
    planes = rows // PAD
    return HALO * (count + index // planes), PAD * (index % planes)


def pack_x_kernel(grid_sizes, first_round, second_round, *rest):
    gy_count, gx_count = grid_sizes
    sides = (len(rest) - 1) // 2
    payloads, outs, ext = rest[:sides], rest[sides:-1], rest[-1]
    cols = first_round.shape[1]
    rows = payloads[0].shape[0]
    count = ext.shape[0]
    lane = iota((PAD, LANES), 1)
    starts = sent_starts(gx_count, cols)
    ext[...] = jnp.zeros_like(ext)
    blocks = [
        [payload[row : row + PAD, :] for row in range(0, rows, PAD)] for payload in payloads
    ]
    for index in range(count):
        slot = index * HALO
        corner, row = corner_slot(index, count, rows)
        north, south = halo_rows(gy_count, first_round, second_round, slot)
        ext[index, PAD - HALO : PAD, 0:cols] = north
        ext[index, PAD : PAD + HALO, 0:cols] = south
        for n, start in enumerate(starts):
            near = ext[index, FIRST : FIRST + PAD, :]
            moved = pltpu.roll(near, lax.rem(corner + LANES - start, LANES), 1)
            here = (lane >= corner) & (lane < corner + HALO)
            blocks[n][row // PAD] = jnp.where(here, moved, blocks[n][row // PAD])
    for n in range(sides):
        for block, value in enumerate(blocks[n]):
            outs[n][block * PAD : (block + 1) * PAD, :] = value


def loaded(weights, l, fac, count_f):
    flat = [fac * weights[l, n] for n in range(weights.shape[1])]
    taps, flat, speed = flat[: 2 * REACH], flat[2 * REACH : -1], flat[-1]
    return taps, [flat[f * count_f : (f + 1) * count_f] for f in range(count_f)], speed


def y_terms(rows_at, at, taps, total):
    offsets = [k for k in range(-REACH, REACH + 1) if k != 0]
    for tap, offset in zip(taps, offsets):
        total = total + tap * rows_at(at + offset)
    return total


def cell_terms(src, l, f, at, centers, weight, taps, mix, total):
    for g, center in enumerate(centers):
        total = total + (mix[f][g] - weight if g == f else mix[f][g]) * center
    return y_terms(lambda row: src[f, l, pl.ds(row, 8), :], at, taps, total)


def split(value):
    high = value.astype(jnp.bfloat16)
    return high, (value - high.astype(jnp.float32)).astype(jnp.bfloat16)


def x_divergence(src, l, first, height, matrix, xdiv):
    count_f = src.shape[0]
    whole = src[:, l, first : first + height, :].reshape(count_f * height, LANES)
    both = jnp.concatenate(split(whole), axis=1)
    twice = jnp.concatenate([matrix[l], matrix[l]], axis=0)
    moved = jnp.dot(both, twice, preferred_element_type=jnp.float32)
    xdiv[:, 0:height, :] = moved.reshape(count_f, height, LANES)


def packed_rate(part, at, forced, row_relax, lane_weights, count_f, count_l):
    to = at - FIRST
    center = part[at : at + 8, :]
    rate = forced - row_relax[to : to + 8, :] * center
    taps = [lane_weights[k] for k in range(2 * REACH)]
    rate = y_terms(lambda row: part[row : row + 8, :], at, taps, rate)
    for d in range(2 * count_f - 1):
        step = (d - (count_f - 1)) * HALO * count_l
        other = pltpu.roll(center, -step % LANES, 1) if step else center
        rate = rate + lane_weights[2 * REACH + d] * other
    return rate


def begin_kernel(
    grid_sizes,
    fields,
    first_round,
    second_round,
    drive,
    relax,
    weights,
    own_matrix,
    row_relax,
    lane_weights,
    *rest,
):
    gy_count, gx_count = grid_sizes
    sides = (len(rest) - 5) // 5
    payloads, side_drive, after = rest[:sides], rest[sides : 2 * sides], rest[2 * sides]
    edges, far, edge_one = (
        rest[2 * sides + 1 + n * sides : 2 * sides + 1 + (n + 1) * sides] for n in range(3)
    )
    state, own_one, own_two, xdiv = rest[-4:]
    count_f, count_l, rows, cols = fields.shape
    wide_rows = relax.shape[0]
    gy = lax.axis_index("gy")
    pad_rows = jnp.zeros((PAD, LANES), jnp.float32)
    for f, l, slot in slots(count_f, count_l):
        north, south = halo_rows(gy_count, first_round, second_round, slot)
        if cols < LANES:
            state[f, l] = jnp.zeros(state.shape[2:], jnp.float32)
        else:
            state[f, l, 0:PAD, :] = pad_rows
            state[f, l, PAD + rows : 2 * PAD + rows, :] = pad_rows
        state[f, l, PAD - HALO : PAD, 0:cols] = north
        state[f, l, PAD : PAD + rows, 0:cols] = fields[f, l]
        state[f, l, PAD + rows : PAD + rows + HALO, 0:cols] = south
    lane = iota((wide_rows, LANES), 1)
    near, starts = edge_starts(gx_count, cols)
    short = iota((PAD, LANES), 1)
    for edge, payload, start in zip(edges, payloads, near):
        edge[PAD : PAD + rows, :] = payload[...]
        for at in (0, PAD + rows):
            packed = jnp.zeros((PAD, LANES), jnp.float32)
            for f, l, slot in slots(count_f, count_l):
                shift = lax.rem(slot + LANES - start, LANES)
                moved = pltpu.roll(state[f, l, at : at + PAD, :], shift, 1)
                packed = jnp.where((short >= slot) & (short < slot + HALO), moved, packed)
            edge[at : at + PAD, :] = packed

    def keep_far(src, section):
        for ref, start in zip(far, starts):
            packed = jnp.zeros((wide_rows, LANES), jnp.float32)
            here = (lane >= start) & (lane < start + REACH)
            for f, l, slot in slots(count_f, count_l):
                kept = jnp.where(here, src[f, l, FIRST : FIRST + wide_rows, :], 0.0)
                packed = packed + pltpu.roll(kept, lax.rem(slot + LANES - start, LANES), 1)
            ref[section] = packed

    keep_far(state, 0)
    for edge, forced, ref in zip(edges, side_drive, edge_one):
        for to in range(0, wide_rows, 8):
            rate = packed_rate(edge, FIRST + to, forced[1, to : to + 8, :], row_relax, lane_weights, count_f, count_l)
            ref[to : to + 8, :] = edge[FIRST + to : FIRST + to + 8, :] + THIRD * rate
    for section, (src, dst, fac) in enumerate(
        ((state, own_one, THIRD), (own_one, own_two, HALF), (own_two, after, 1.0))
    ):
        first, height = (PAD, rows) if dst is after else (FIRST, wide_rows)
        for l in range(count_l):
            x_divergence(src, l, first, height, own_matrix, xdiv)
            taps, mix, speed = loaded(weights, l, fac, count_f)
            for n in range(height // 8):
                at, row = first + n * 8, n * 8
                to = at - FIRST
                centers = [src[g, l, at : at + 8, :] for g in range(count_f)]
                weight = fac * relax[to : to + 8, :]
                for f in range(count_f):
                    base = centers[f] if src is state else state[f, l, at : at + 8, :]
                    total = base + fac * drive[f, l, to : to + 8, :]
                    total = total + speed * xdiv[f, row : row + 8, :]
                    total = cell_terms(src, l, f, at, centers, weight, taps, mix, total)
                    if dst is after:
                        after[f, l, row : row + 8, :] = total[:, 0:cols]
                    else:
                        dst[f, l, at : at + 8, :] = total
        if dst is not after:
            for row, here in ((FIRST, gy == 0), (PAD + rows, gy == gy_count - 1)):

                @pl.when(here)
                def _(dst=dst, row=row):
                    dst[:, :, row : row + 8, :] = jnp.zeros(
                        (count_f, count_l, 8, LANES), jnp.float32
                    )

            keep_far(dst, section + 1)


def finish_kernel(grid_sizes, sides, *refs):
    gy_count, gx_count = grid_sizes
    halos, edges, fars, edge_one, side_drive, side_matrix = (
        refs[n * sides : (n + 1) * sides] for n in range(6)
    )
    after, row_relax, inside, lane_weights, out, outer, one, two = refs[6 * sides :]
    count_f, count_l, rows, cols = out.shape
    wide_rows = row_relax.shape[0]
    gx = lax.axis_index("gx")
    starts = edge_starts(gx_count, cols)[0]
    exists = [None] if sides == 1 else [gx > 0, gx < gx_count - 1]
    speed = lane_weights[lane_weights.shape[0] - 1]

    def unpack(halo):
        count = count_f * count_l
        outer[0:8, :] = jnp.zeros((8, LANES), jnp.float32)
        outer[PAD + rows + 8 : 2 * PAD + rows, :] = jnp.zeros((8, LANES), jnp.float32)
        lane = iota((rows, LANES), 1)
        outer[PAD : PAD + rows, :] = jnp.where(lane < HALO * count, halo[...], 0.0)
        lane = iota((PAD, LANES), 1)
        corners = jnp.zeros((PAD, LANES), jnp.float32)
        for index in range(count):
            slot = HALO * index
            corner, row = corner_slot(index, count, rows)
            moved = pltpu.roll(halo[row : row + PAD, :], (slot - corner) % LANES, 1)
            corners = jnp.where((lane >= slot) & (lane < slot + HALO), moved, corners)
        outer[8:PAD, :] = corners[0:8]
        outer[PAD + rows : PAD + rows + 8, :] = corners[8:PAD]

    def section(parts, s, fac, number, first, height, wanted, store):
        columns = [part[first : first + height, :] for part in parts]
        columns.append(fars[s][number, first - FIRST : first - FIRST + height, :])
        both = jnp.concatenate(split(jnp.concatenate(columns, axis=1)), axis=1)
        matrix = side_matrix[s][:, wanted[0] * LANES :]
        moved = jnp.dot(
            both, jnp.concatenate([matrix, matrix], axis=0), preferred_element_type=jnp.float32
        )
        places = []
        for place, which in enumerate(wanted):
            short = number == 1 and which == 0
            for n in range(short, height // 8 - short):
                at = first + n * 8
                rate = None
                if number > 0 or which == 0:
                    forced = side_drive[s][which, at - FIRST : at - FIRST + 8, :]
                    rate = packed_rate(
                        parts[which], at, forced, row_relax, lane_weights, count_f, count_l
                    )
                places.append((place, which, n, at, rate))
        for place, which, n, at, rate in places:
            lanes, row = slice(place * LANES, (place + 1) * LANES), n * 8
            x_rate = moved[row : row + 8, lanes]
            if rate is None:
                value = edge_one[s][row : row + 8, :] + fac * (speed * x_rate)
            else:
                start = (outer, edges[s])[which]
                value = start[at : at + 8, :] + fac * (rate + speed * x_rate)
            store(which, at, at - FIRST, value)

    lane = iota((rows, LANES), 1)
    for s in range(sides):
        def keep(ref):
            def store(which, at, to, value):
                kept = inside[to : to + 8, :]
                if exists[s] is not None and which == 0:
                    kept = jnp.where(exists[s], kept, 0.0)
                ref[which, at : at + 8, :] = value * kept

            return store

        unpack(halos[s])
        section((outer, edges[s]), s, THIRD, 0, FIRST, wide_rows, (0, 1), keep(one))
        section((one.at[0], one.at[1]), s, HALF, 1, FIRST, wide_rows, (0, 1), keep(two))

        def last(which, at, to, value):
            one[0, at : at + 8, :] = value

        section((two.at[0], two.at[1]), s, 1.0, 2, PAD, rows, (1,), last)
        right = one[0, PAD : PAD + rows, :]
        near = (lane >= starts[s]) & (lane < starts[s] + HALO)
        if exists[s] is not None:
            near = near & exists[s]
        source = after if s == 0 else out
        for f, l, slot in slots(count_f, count_l):
            moved = pltpu.roll(right, lax.rem(starts[s] + LANES - slot, LANES), 1)
            out[f, l] = jnp.where(near[:, 0:cols], moved[:, 0:cols], source[f, l])


def pair_rounds(part_count, gy_count, gx_count):
    rounds = []
    for start in (0, 1):
        partner = {}
        for low in range(start, gy_count - 1, 2):
            partner[low], partner[low + 1] = low + 1, low
        pairs = []
        for place in np.ndindex(part_count, gy_count, gx_count):
            part, y, x = place
            if y in partner:
                to = part, partner[y], x
            elif part_count % 2 == 0:
                to = part ^ 1, y, x
            elif gx_count % 2 == 0:
                to = part, y, x ^ 1
            else:
                continue
            shape = (part_count, gy_count, gx_count)
            pairs.append(tuple(int(np.ravel_multi_index(at, shape)) for at in (place, to)))
        rounds.append(pairs)
    return rounds


def local(
    gy_count, gx_count, fields, wind_x, wind_y, coupling, north, south, west, east, strip_scale, widths
):
    count_f, count_l, rows, cols = fields.shape
    ext_rows = rows + 2 * PAD
    grid_sizes = (gy_count, gx_count)
    packed_rows = -(-HALO * count_f * count_l // 8) * 8
    vmem = pl.BlockSpec(memory_space=pltpu.VMEM)
    smem = pl.BlockSpec(memory_space=pltpu.SMEM)
    f32 = functools.partial(jax.ShapeDtypeStruct, dtype=jnp.float32)

    def call(body, name, out_shape, inputs, scratch=(), limit=4):
        several = isinstance(out_shape, tuple)
        return pl.pallas_call(
            body,
            out_shape=out_shape,
            in_specs=[space for _, space in inputs],
            out_specs=(vmem,) * len(out_shape) if several else vmem,
            scratch_shapes=list(scratch),
            compiler_params=pltpu.CompilerParams(vmem_limit_bytes=limit << 20),
            name=name,
        )(*[value for value, _ in inputs])

    def inputs(space, *values):
        return [(value, space) for value in values]

    strip_shape = f32((packed_rows, cols))
    sent_first, sent_second = call(
        pack_y_kernel, "pack_y", (strip_shape, strip_shape), inputs(vmem, fields)
    )
    axes = ("mem", "gy", "gx")
    first_pairs, second_pairs = pair_rounds(lax.axis_size("mem"), gy_count, gx_count)
    first_round = lax.ppermute(sent_first, axes, first_pairs)
    second_round = lax.ppermute(sent_second, axes, second_pairs)

    mixing = jnp.transpose(coupling, (1, 0, 2))
    scales = jnp.transpose(strip_scale, (0, 2, 1))
    sides = 1 if gx_count == 2 else 2
    wide_rows = rows + 16
    state_shape = (count_f, count_l, ext_rows, LANES)
    wide_shape = (count_f, count_l, wide_rows, LANES)
    plane = f32((wide_rows, LANES))
    matrix = functools.partial(jax.ShapeDtypeStruct, dtype=jnp.bfloat16)
    entries = 2 * REACH + count_f * count_f + 1
    lane_entries = 2 * REACH + 2 * count_f
    prepared = call(
        functools.partial(prepare_kernel, grid_sizes),
        "prepare",
        (f32(wide_shape), plane, plane, plane)
        + (f32((count_l, entries, 8, LANES)), f32((lane_entries, 8, LANES)))
        + (matrix((count_l, LANES, LANES)),)
        + (f32((rows, LANES)),) * sides
        + (f32((2, wide_rows, LANES)),) * sides
        + (matrix((3 * LANES, 2 * LANES)),) * sides,
        inputs(vmem, fields, north, south, jnp.swapaxes(west, 2, 3), jnp.swapaxes(east, 2, 3))
        + inputs(vmem, jnp.asarray(own_bands(cols), jnp.bfloat16))
        + inputs(smem, scales, widths, wind_x, wind_y, mixing),
        scratch=[pltpu.VMEM((rows, LANES), jnp.float32)],
    )
    drive, relax, row_relax, inside, weights, lane_weights, own_matrix = prepared[:7]
    payloads, side_drive, side_matrix = (
        prepared[7 + n * sides : 7 + (n + 1) * sides] for n in range(3)
    )

    sent = call(
        functools.partial(pack_x_kernel, grid_sizes),
        "pack_x",
        (f32((rows, LANES)),) * sides,
        inputs(vmem, first_round, second_round, *payloads),
        scratch=[pltpu.VMEM((count_f * count_l, 2 * PAD, LANES), jnp.float32)],
    )
    forward = [(i, i + 1) for i in range(gx_count - 1)]
    backward = [(b, a) for a, b in forward]
    if sides == 1:
        halos = [lax.ppermute(sent[0], "gx", forward + backward)]
    else:
        halos = [lax.ppermute(sent[0], "gx", forward), lax.ppermute(sent[1], "gx", backward)]

    state = pltpu.VMEM(state_shape, jnp.float32)
    after, *begun = call(
        functools.partial(begin_kernel, grid_sizes),
        "begin",
        (f32(fields.shape),)
        + (f32((ext_rows, LANES)),) * sides
        + (f32((3, wide_rows, LANES)),) * sides
        + (plane,) * sides,
        inputs(vmem, fields, first_round, second_round, drive, relax, weights, own_matrix)
        + inputs(vmem, row_relax, lane_weights, *payloads[::-1], *side_drive),
        scratch=[state] * 3 + [pltpu.VMEM((count_f, wide_rows, LANES), jnp.float32)],
        limit=8,
    )
    pair = pltpu.VMEM((2, ext_rows, LANES), jnp.float32)
    return call(
        functools.partial(finish_kernel, grid_sizes, sides),
        "finish",
        f32(fields.shape),
        inputs(vmem, *halos, *begun, *side_drive, *side_matrix)
        + inputs(vmem, after, row_relax, inside, lane_weights),
        scratch=[pltpu.VMEM((ext_rows, LANES), jnp.float32), pair, pair],
    )


def solution(mesh):
    return jax.shard_map(
        functools.partial(local, mesh.shape["gy"], mesh.shape["gx"]),
        mesh=mesh,
        in_specs=(
            P("mem", None, "gy", "gx"),
            P("mem"),
            P("mem"),
            P(),
            P("mem", None, None, None),
            P("mem", None, None, None),
            P("mem", None, None, None),
            P("mem", None, None, None),
            P("mem", None, None),
            P(),
        ),
        out_specs=P("mem", None, "gy", "gx"),
        check_vma=False,
    )
```

```python
import functools

import jax
import jax.numpy as jnp
import numpy as np
from jax import lax
from jax.experimental import pallas as pl
from jax.experimental.pallas import tpu as pltpu
from jax.sharding import PartitionSpec as P

RELAX = 0.25
REACH = 3
HALO = 3 * REACH
PAD = 16
LANES = 128
FIRST = PAD - 8
THIRD, HALF = 1.0 / 3.0, 0.5

UPWIND = (-2.0, 15.0, -60.0, 20.0, 30.0, -3.0, 0.0)
CENTRAL = (-1.0, 9.0, -45.0, 0.0, 45.0, -9.0, 1.0)
DAMPING = (1.0, -6.0, 15.0, -20.0, 15.0, -6.0, 1.0)


def own_bands(cols):
    bands = np.zeros((2, LANES, LANES), np.float32)
    for col in range(cols):
        for offset in range(-REACH, REACH + 1):
            if 0 <= col + offset < cols:
                bands[0, col + offset, col] = UPWIND[offset + REACH]
                bands[1, col + offset, col] = -UPWIND[REACH - offset]
    return bands


def iota(shape, dim):
    return lax.broadcasted_iota(jnp.int32, shape, dim)


def edge_weight(distance, width):
    dist = distance.astype(jnp.float32)
    inside = (dist >= 0.0) & (dist < width)
    return jnp.where(inside, jnp.square((width - dist) / width), 0.0)


def slots(count_f, count_l):
    return [(f, l, HALO * (f * count_l + l)) for f in range(count_f) for l in range(count_l)]


def pack_y_kernel(fields, first_round, second_round):
    count_f, count_l, rows, _ = fields.shape
    even = lax.rem(lax.axis_index("gy"), 2) == 0
    for f, l, slot in slots(count_f, count_l):
        top = fields[f, l, 0:HALO, :]
        bottom = fields[f, l, rows - HALO : rows, :]
        first_round[slot : slot + HALO, :] = jnp.where(even, bottom, top)
        second_round[slot : slot + HALO, :] = jnp.where(even, top, bottom)


def halo_rows(gy_count, first_round, second_round, slot):
    gy = lax.axis_index("gy")
    even = lax.rem(gy, 2) == 0
    first = first_round[slot : slot + HALO, :]
    second = second_round[slot : slot + HALO, :]
    north = jnp.where(gy == 0, 0.0, jnp.where(even, second, first))
    south = jnp.where(gy == gy_count - 1, 0.0, jnp.where(even, first, second))
    return north, south


def sent_starts(gx_count, cols):
    if gx_count == 2:
        return [jnp.where(lax.axis_index("gx") == 0, cols - HALO, 0)]
    return [cols - HALO, 0]


def side_ids(gx_count):
    if gx_count == 2:
        return [jnp.where(lax.axis_index("gx") == 0, 0, 1)]
    return [1, 0]


def edge_starts(gx_count, cols):
    near = [jnp.where(side == 0, cols - HALO, 0) for side in side_ids(gx_count)]
    far = [jnp.where(side == 0, cols - HALO - REACH, HALO) for side in side_ids(gx_count)]
    return near, far


def level_weights(coupling, wind_x, wind_y, l, count_f):
    speed, size = wind_y[l] / 60.0, jnp.abs(wind_y[l]) / 60.0
    taps = [size * DAMPING[k] - speed * CENTRAL[k] for k in range(2 * REACH + 1)]
    mix = [
        [coupling[f, l, g] + (taps[REACH] if f == g else 0.0) for g in range(count_f)]
        for f in range(count_f)
    ]
    return [tap for k, tap in enumerate(taps) if k != REACH], mix, -wind_x[l] / 60.0


def side_bands(side, lane_speed, matrix):
    shape = (LANES, LANES)
    row, col = iota(shape, 0), iota(shape, 1)
    row_plane, col_plane = (row * 57) >> 9, (col * 57) >> 9
    apart = (row - HALO * row_plane) - (col - HALO * col_plane)
    apart = jnp.where(row_plane == col_plane, apart, 4 * HALO)
    sign = jnp.where(lane_speed > 0.0, -1, 1)
    sign_float = sign.astype(jnp.float32)

    def block(base):
        offset = (apart + base) * sign
        value = jnp.zeros(shape, jnp.float32)
        for k, entry in enumerate(UPWIND[:-1]):
            value = jnp.where(offset == k - REACH, entry, value)
        return (value * sign_float).astype(jnp.bfloat16)

    here, step = block(0), jnp.where(side == 0, HALO, -HALO)
    matrix[0:LANES, 0:LANES] = here
    matrix[LANES : 2 * LANES, LANES:] = here
    matrix[LANES : 2 * LANES, 0:LANES] = block(-step)
    matrix[0:LANES, LANES:] = block(step)
    matrix[2 * LANES :, 0:LANES] = jnp.zeros(shape, jnp.bfloat16)
    matrix[2 * LANES :, LANES:] = block(jnp.where(side == 0, -REACH, HALO))


def prepare_kernel(
    grid_sizes,
    fields,
    north,
    south,
    west,
    east,
    own_band,
    scale,
    widths,
    wind_x,
    wind_y,
    coupling,
    drive,
    relax,
    row_relax,
    inside,
    weights,
    lane_weights,
    own_matrix,
    *rest,
):
    gy_count, gx_count = grid_sizes
    sides = (len(rest) - 1) // 3
    payloads, side_drive, side_matrix = rest[:sides], rest[sides : 2 * sides], rest[2 * sides : -1]
    wide = rest[-1]
    count_f, count_l, rows, cols = fields.shape
    wide_rows = relax.shape[0]
    strip = north.shape[2]
    total_rows, total_cols = rows * gy_count, cols * gx_count
    gy, gx = lax.axis_index("gy"), lax.axis_index("gx")
    row_start, col_start = gy * rows, gx * cols
    width = [widths[s].astype(jnp.float32) for s in range(4)]
    lane = iota((8, LANES), 1)

    lane_rows = iota((rows, LANES), 1)
    starts = sent_starts(gx_count, cols)
    packed = [jnp.zeros((rows, LANES), jnp.float32) for _ in starts]
    if cols < LANES:
        wide[...] = jnp.zeros_like(wide)
    for f, l, slot in slots(count_f, count_l):
        if cols < LANES:
            wide[:, 0:cols] = fields[f, l]
            own = wide[...]
        else:
            own = fields[f, l]
        for n, start in enumerate(starts):
            moved = pltpu.roll(own, lax.rem(slot + LANES - start, LANES), 1)
            here = (lane_rows >= slot) & (lane_rows < slot + HALO)
            packed[n] = jnp.where(here, moved, packed[n])
    for payload, value in zip(payloads, packed):
        payload[...] = value

    def full(value):
        return jnp.full((8, LANES), value, jnp.float32)

    lane_taps = [full(0.0) for _ in range(2 * REACH)]
    lane_mix = [full(0.0) for _ in range(2 * count_f - 1)]
    lane_speed = full(0.0)
    for l in range(count_l):
        taps, mix, speed = level_weights(coupling, wind_x, wind_y, l, count_f)
        flat = taps + [entry for line in mix for entry in line] + [speed]
        for n, entry in enumerate(flat):
            weights[l, n] = full(entry)
        own_matrix[l] = own_band[jnp.where(wind_x[l] < 0.0, 1, 0)]
        for f in range(count_f):
            slot = HALO * (f * count_l + l)
            here = (lane >= slot) & (lane < slot + HALO)
            lane_taps = [jnp.where(here, tap, old) for tap, old in zip(taps, lane_taps)]
            lane_speed = jnp.where(here, speed, lane_speed)
            for g in range(count_f):
                at = g - f + count_f - 1
                lane_mix[at] = jnp.where(here, mix[f][g], lane_mix[at])
    for n, entry in enumerate(lane_taps + lane_mix + [lane_speed]):
        lane_weights[n] = entry
    for side, matrix in zip(side_ids(gx_count), side_matrix):
        side_bands(side, lane_speed[0:1, :], matrix)

    row_global = iota((wide_rows, LANES), 0) + (row_start - 8)
    row_weight = RELAX * (
        edge_weight(row_global, width[0]) + edge_weight(total_rows - 1 - row_global, width[1])
    )
    col_weight = RELAX * (
        edge_weight(lane + col_start, width[2])
        + edge_weight(total_cols - 1 - (lane + col_start), width[3])
    )
    row_relax[...] = row_weight
    relax[...] = row_weight + col_weight[0:1, :]
    inside[...] = jnp.where((row_global >= 0) & (row_global < total_rows), 1.0, 0.0)

    pos = iota((strip, LANES), 1)
    depth = iota((strip, LANES), 0)
    pick = jnp.concatenate([pos == depth, pos == depth + (cols - strip)], axis=0)
    pick = pick.astype(jnp.float32).astype(jnp.bfloat16)
    west_weight = RELAX * edge_weight(lane + col_start, width[2])
    east_weight = RELAX * edge_weight(total_cols - 1 - (lane + col_start), width[3])
    west_weight = jnp.where(lane < strip, west_weight, 0.0)
    east_weight = jnp.where((lane >= cols - strip) & (lane < cols), east_weight, 0.0)
    shift = lax.rem(8 + total_rows - row_start, total_rows)
    for f in range(count_f):
        for l in range(count_l):
            both = jnp.concatenate([west[f, l], east[f, l]], axis=0).astype(jnp.float32)
            both = pltpu.roll(both, shift, 1)[:, 0:LANES].astype(jnp.bfloat16)
            raw = lax.dot_general(
                both, pick, (((0,), (0,)), ((), ())), preferred_element_type=jnp.float32
            )
            factor = west_weight * scale[2, l, f] + east_weight * scale[3, l, f]
            drive[f, l] = raw[0:wide_rows] * factor[0:1, :]
    for ref in side_drive:
        ref[...] = jnp.zeros_like(ref)

    own_shift = lax.rem(total_cols - col_start, total_cols)
    for source, side, at, here in (
        (north, 0, 8, gy == 0),
        (south, 1, 8 + rows - strip, gy == gy_count - 1),
    ):

        @pl.when(here)
        def _(source=source, side=side, at=at):
            distance = depth if side == 0 else strip - 1 - depth
            weight = RELAX * edge_weight(distance, width[side])
            packed = [[jnp.zeros((strip, LANES), jnp.float32)] * 2 for _ in side_drive]
            for f, l, slot in slots(count_f, count_l):
                values = source[f, l].astype(jnp.float32)
                factor = weight * scale[side, l, f]
                own = pltpu.roll(values, own_shift, 1)[:, 0:LANES]
                drive[f, l, at : at + strip, :] = drive[f, l, at : at + strip, :] + factor * own
                held = (pos >= slot) & (pos < slot + HALO)
                for n, which in enumerate(side_ids(gx_count)):
                    for part, begin in enumerate(
                        (jnp.where(which == 0, cols, -HALO), jnp.where(which == 0, cols - HALO, 0))
                    ):
                        shift = slot + 2 * total_cols - begin - col_start
                        moved = pltpu.roll(values, lax.rem(shift, total_cols), 1)[:, 0:LANES]
                        packed[n][part] = jnp.where(held, factor * moved, packed[n][part])
            for ref, value in zip(side_drive, packed):
                for part in range(2):
                    ref[part, at : at + strip, :] = value[part]


def corner_slot(index, count, rows):
    planes = rows // PAD
    return HALO * (count + index // planes), PAD * (index % planes)


def pack_x_kernel(grid_sizes, first_round, second_round, *rest):
    gy_count, gx_count = grid_sizes
    sides = (len(rest) - 1) // 2
    payloads, outs, ext = rest[:sides], rest[sides:-1], rest[-1]
    cols = first_round.shape[1]
    rows = payloads[0].shape[0]
    count = ext.shape[0]
    lane = iota((PAD, LANES), 1)
    starts = sent_starts(gx_count, cols)
    ext[...] = jnp.zeros_like(ext)
    blocks = [
        [payload[row : row + PAD, :] for row in range(0, rows, PAD)] for payload in payloads
    ]
    for index in range(count):
        slot = index * HALO
        corner, row = corner_slot(index, count, rows)
        north, south = halo_rows(gy_count, first_round, second_round, slot)
        ext[index, PAD - HALO : PAD, 0:cols] = north
        ext[index, PAD : PAD + HALO, 0:cols] = south
        for n, start in enumerate(starts):
            near = ext[index, FIRST : FIRST + PAD, :]
            moved = pltpu.roll(near, lax.rem(corner + LANES - start, LANES), 1)
            here = (lane >= corner) & (lane < corner + HALO)
            blocks[n][row // PAD] = jnp.where(here, moved, blocks[n][row // PAD])
    for n in range(sides):
        for block, value in enumerate(blocks[n]):
            outs[n][block * PAD : (block + 1) * PAD, :] = value


def loaded(weights, l, fac, count_f):
    flat = [fac * weights[l, n] for n in range(weights.shape[1])]
    taps, flat, speed = flat[: 2 * REACH], flat[2 * REACH : -1], flat[-1]
    return taps, [flat[f * count_f : (f + 1) * count_f] for f in range(count_f)], speed


def y_terms(rows_at, at, taps, total):
    offsets = [k for k in range(-REACH, REACH + 1) if k != 0]
    for tap, offset in zip(taps, offsets):
        total = total + tap * rows_at(at + offset)
    return total


def cell_terms(src, l, f, at, centers, weight, taps, mix, total):
    for g, center in enumerate(centers):
        total = total + (mix[f][g] - weight if g == f else mix[f][g]) * center
    return y_terms(lambda row: src[f, l, pl.ds(row, 8), :], at, taps, total)


def split(value):
    high = value.astype(jnp.bfloat16)
    return high, (value - high.astype(jnp.float32)).astype(jnp.bfloat16)


def x_divergence(src, l, first, height, matrix, xdiv):
    count_f = src.shape[0]
    whole = src[:, l, first : first + height, :].reshape(count_f * height, LANES)
    both = jnp.concatenate(split(whole), axis=1)
    twice = jnp.concatenate([matrix[l], matrix[l]], axis=0)
    moved = jnp.dot(both, twice, preferred_element_type=jnp.float32)
    xdiv[:, 0:height, :] = moved.reshape(count_f, height, LANES)


def packed_rate(part, at, forced, row_relax, lane_weights, count_f, count_l):
    to = at - FIRST
    center = part[at : at + 8, :]
    rate = forced - row_relax[to : to + 8, :] * center
    taps = [lane_weights[k] for k in range(2 * REACH)]
    rate = y_terms(lambda row: part[row : row + 8, :], at, taps, rate)
    for d in range(2 * count_f - 1):
        step = (d - (count_f - 1)) * HALO * count_l
        other = pltpu.roll(center, -step % LANES, 1) if step else center
        rate = rate + lane_weights[2 * REACH + d] * other
    return rate


def begin_kernel(
    grid_sizes,
    fields,
    first_round,
    second_round,
    drive,
    relax,
    weights,
    own_matrix,
    row_relax,
    lane_weights,
    *rest,
):
    gy_count, gx_count = grid_sizes
    sides = (len(rest) - 5) // 5
    payloads, side_drive, after = rest[:sides], rest[sides : 2 * sides], rest[2 * sides]
    edges, far, edge_one = (
        rest[2 * sides + 1 + n * sides : 2 * sides + 1 + (n + 1) * sides] for n in range(3)
    )
    state, own_one, own_two, xdiv = rest[-4:]
    count_f, count_l, rows, cols = fields.shape
    wide_rows = relax.shape[0]
    gy = lax.axis_index("gy")
    pad_rows = jnp.zeros((PAD, LANES), jnp.float32)
    for f, l, slot in slots(count_f, count_l):
        north, south = halo_rows(gy_count, first_round, second_round, slot)
        if cols < LANES:
            state[f, l] = jnp.zeros(state.shape[2:], jnp.float32)
        else:
            state[f, l, 0:PAD, :] = pad_rows
            state[f, l, PAD + rows : 2 * PAD + rows, :] = pad_rows
        state[f, l, PAD - HALO : PAD, 0:cols] = north
        state[f, l, PAD : PAD + rows, 0:cols] = fields[f, l]
        state[f, l, PAD + rows : PAD + rows + HALO, 0:cols] = south
    lane = iota((wide_rows, LANES), 1)
    near, starts = edge_starts(gx_count, cols)
    short = iota((PAD, LANES), 1)
    for edge, payload, start in zip(edges, payloads, near):
        edge[PAD : PAD + rows, :] = payload[...]
        for at in (0, PAD + rows):
            packed = jnp.zeros((PAD, LANES), jnp.float32)
            for f, l, slot in slots(count_f, count_l):
                shift = lax.rem(slot + LANES - start, LANES)
                moved = pltpu.roll(state[f, l, at : at + PAD, :], shift, 1)
                packed = jnp.where((short >= slot) & (short < slot + HALO), moved, packed)
            edge[at : at + PAD, :] = packed

    def keep_far(src, section):
        for ref, start in zip(far, starts):
            packed = jnp.zeros((wide_rows, LANES), jnp.float32)
            here = (lane >= start) & (lane < start + REACH)
            for f, l, slot in slots(count_f, count_l):
                kept = jnp.where(here, src[f, l, FIRST : FIRST + wide_rows, :], 0.0)
                packed = packed + pltpu.roll(kept, lax.rem(slot + LANES - start, LANES), 1)
            ref[section] = packed

    keep_far(state, 0)
    for edge, forced, ref in zip(edges, side_drive, edge_one):
        for to in range(0, wide_rows, 8):
            rate = packed_rate(edge, FIRST + to, forced[1, to : to + 8, :], row_relax, lane_weights, count_f, count_l)
            ref[to : to + 8, :] = edge[FIRST + to : FIRST + to + 8, :] + THIRD * rate
    for section, (src, dst, fac) in enumerate(
        ((state, own_one, THIRD), (own_one, own_two, HALF), (own_two, after, 1.0))
    ):
        first, height = (PAD, rows) if dst is after else (FIRST, wide_rows)
        for l in range(count_l):
            x_divergence(src, l, first, height, own_matrix, xdiv)
            taps, mix, speed = loaded(weights, l, fac, count_f)
            for n in range(height // 8):
                at, row = first + n * 8, n * 8
                to = at - FIRST
                centers = [src[g, l, at : at + 8, :] for g in range(count_f)]
                weight = fac * relax[to : to + 8, :]
                for f in range(count_f):
                    base = centers[f] if src is state else state[f, l, at : at + 8, :]
                    total = base + fac * drive[f, l, to : to + 8, :]
                    total = total + speed * xdiv[f, row : row + 8, :]
                    total = cell_terms(src, l, f, at, centers, weight, taps, mix, total)
                    if dst is after:
                        after[f, l, row : row + 8, :] = total[:, 0:cols]
                    else:
                        dst[f, l, at : at + 8, :] = total
        if dst is not after:
            for row, here in ((FIRST, gy == 0), (PAD + rows, gy == gy_count - 1)):

                @pl.when(here)
                def _(dst=dst, row=row):
                    dst[:, :, row : row + 8, :] = jnp.zeros(
                        (count_f, count_l, 8, LANES), jnp.float32
                    )

            keep_far(dst, section + 1)


def finish_kernel(grid_sizes, sides, *refs):
    gy_count, gx_count = grid_sizes
    halos, edges, fars, edge_one, side_drive, side_matrix = (
        refs[n * sides : (n + 1) * sides] for n in range(6)
    )
    after, row_relax, inside, lane_weights, out, outer, one, two, ready, sent = refs[6 * sides :]
    count_f, count_l, rows, cols = out.shape
    wide_rows = row_relax.shape[0]
    gx = lax.axis_index("gx")
    starts = edge_starts(gx_count, cols)[0]
    exists = [None] if sides == 1 else [gx > 0, gx < gx_count - 1]
    speed = lane_weights[lane_weights.shape[0] - 1]

    def unpack(halo):
        count = count_f * count_l
        outer[0:8, :] = jnp.zeros((8, LANES), jnp.float32)
        outer[PAD + rows + 8 : 2 * PAD + rows, :] = jnp.zeros((8, LANES), jnp.float32)
        lane = iota((rows, LANES), 1)
        outer[PAD : PAD + rows, :] = jnp.where(lane < HALO * count, halo[...], 0.0)
        lane = iota((PAD, LANES), 1)
        corners = jnp.zeros((PAD, LANES), jnp.float32)
        for index in range(count):
            slot = HALO * index
            corner, row = corner_slot(index, count, rows)
            moved = pltpu.roll(halo[row : row + PAD, :], (slot - corner) % LANES, 1)
            corners = jnp.where((lane >= slot) & (lane < slot + HALO), moved, corners)
        outer[8:PAD, :] = corners[0:8]
        outer[PAD + rows : PAD + rows + 8, :] = corners[8:PAD]

    def section(parts, s, fac, number, first, height, wanted, store):
        columns = [part[first : first + height, :] for part in parts]
        columns.append(fars[s][number, first - FIRST : first - FIRST + height, :])
        both = jnp.concatenate(split(jnp.concatenate(columns, axis=1)), axis=1)
        matrix = side_matrix[s][:, wanted[0] * LANES :]
        moved = jnp.dot(
            both, jnp.concatenate([matrix, matrix], axis=0), preferred_element_type=jnp.float32
        )
        places = []
        for place, which in enumerate(wanted):
            short = number == 1 and which == 0
            for n in range(short, height // 8 - short):
                at = first + n * 8
                rate = None
                if number > 0 or which == 0:
                    forced = side_drive[s][which, at - FIRST : at - FIRST + 8, :]
                    rate = packed_rate(
                        parts[which], at, forced, row_relax, lane_weights, count_f, count_l
                    )
                places.append((place, which, n, at, rate))
        for place, which, n, at, rate in places:
            lanes, row = slice(place * LANES, (place + 1) * LANES), n * 8
            x_rate = moved[row : row + 8, lanes]
            if rate is None:
                value = edge_one[s][row : row + 8, :] + fac * (speed * x_rate)
            else:
                start = (outer, edges[s])[which]
                value = start[at : at + 8, :] + fac * (rate + speed * x_rate)
            store(which, at, at - FIRST, value)

    lane = iota((rows, LANES), 1)
    for s in range(sides):
        def keep(ref):
            def store(which, at, to, value):
                kept = inside[to : to + 8, :]
                if exists[s] is not None and which == 0:
                    kept = jnp.where(exists[s], kept, 0.0)
                ref[which, at : at + 8, :] = value * kept

            return store

        unpack(halos[s])
        section((outer, edges[s]), s, THIRD, 0, FIRST, wide_rows, (0, 1), keep(one))
        section((one.at[0], one.at[1]), s, HALF, 1, FIRST, wide_rows, (0, 1), keep(two))

        def last(which, at, to, value):
            one[0, at : at + 8, :] = value

        section((two.at[0], two.at[1]), s, 1.0, 2, PAD, rows, (1,), last)
        right = one[0, PAD : PAD + rows, :]
        near = (lane >= starts[s]) & (lane < starts[s] + HALO)
        if exists[s] is not None:
            near = near & exists[s]
        source = after if s == 0 else ready
        for f in range(count_f):
            for l in range(count_l):
                slot = HALO * (f * count_l + l)
                moved = pltpu.roll(right, lax.rem(starts[s] + LANES - slot, LANES), 1)
                ready[f, l] = jnp.where(near[:, 0:cols], moved[:, 0:cols], source[f, l])
            if s == sides - 1:
                pltpu.make_async_copy(ready.at[f], out.at[f], sent.at[f]).start()
    for f in range(count_f):
        pltpu.make_async_copy(ready.at[f], out.at[f], sent.at[f]).wait()


def pair_rounds(part_count, gy_count, gx_count):
    rounds = []
    for start in (0, 1):
        partner = {}
        for low in range(start, gy_count - 1, 2):
            partner[low], partner[low + 1] = low + 1, low
        pairs = []
        for place in np.ndindex(part_count, gy_count, gx_count):
            part, y, x = place
            if y in partner:
                to = part, partner[y], x
            elif part_count % 2 == 0:
                to = part ^ 1, y, x
            elif gx_count % 2 == 0:
                to = part, y, x ^ 1
            else:
                continue
            shape = (part_count, gy_count, gx_count)
            pairs.append(tuple(int(np.ravel_multi_index(at, shape)) for at in (place, to)))
        rounds.append(pairs)
    return rounds


def local(
    gy_count, gx_count, fields, wind_x, wind_y, coupling, north, south, west, east, strip_scale, widths
):
    count_f, count_l, rows, cols = fields.shape
    ext_rows = rows + 2 * PAD
    grid_sizes = (gy_count, gx_count)
    packed_rows = -(-HALO * count_f * count_l // 8) * 8
    vmem = pl.BlockSpec(memory_space=pltpu.VMEM)
    smem = pl.BlockSpec(memory_space=pltpu.SMEM)
    f32 = functools.partial(jax.ShapeDtypeStruct, dtype=jnp.float32)

    def call(body, name, out_shape, inputs, scratch=(), limit=4, out_space=vmem):
        several = isinstance(out_shape, tuple)
        return pl.pallas_call(
            body,
            out_shape=out_shape,
            in_specs=[space for _, space in inputs],
            out_specs=(out_space,) * len(out_shape) if several else out_space,
            scratch_shapes=list(scratch),
            compiler_params=pltpu.CompilerParams(vmem_limit_bytes=limit << 20),
            name=name,
        )(*[value for value, _ in inputs])

    def inputs(space, *values):
        return [(value, space) for value in values]

    strip_shape = f32((packed_rows, cols))
    sent_first, sent_second = call(
        pack_y_kernel, "pack_y", (strip_shape, strip_shape), inputs(vmem, fields)
    )
    axes = ("mem", "gy", "gx")
    first_pairs, second_pairs = pair_rounds(lax.axis_size("mem"), gy_count, gx_count)
    first_round = lax.ppermute(sent_first, axes, first_pairs)
    second_round = lax.ppermute(sent_second, axes, second_pairs)

    mixing = jnp.transpose(coupling, (1, 0, 2))
    scales = jnp.transpose(strip_scale, (0, 2, 1))
    sides = 1 if gx_count == 2 else 2
    wide_rows = rows + 16
    state_shape = (count_f, count_l, ext_rows, LANES)
    wide_shape = (count_f, count_l, wide_rows, LANES)
    plane = f32((wide_rows, LANES))
    matrix = functools.partial(jax.ShapeDtypeStruct, dtype=jnp.bfloat16)
    entries = 2 * REACH + count_f * count_f + 1
    lane_entries = 2 * REACH + 2 * count_f
    prepared = call(
        functools.partial(prepare_kernel, grid_sizes),
        "prepare",
        (f32(wide_shape), plane, plane, plane)
        + (f32((count_l, entries, 8, LANES)), f32((lane_entries, 8, LANES)))
        + (matrix((count_l, LANES, LANES)),)
        + (f32((rows, LANES)),) * sides
        + (f32((2, wide_rows, LANES)),) * sides
        + (matrix((3 * LANES, 2 * LANES)),) * sides,
        inputs(vmem, fields, north, south, jnp.swapaxes(west, 2, 3), jnp.swapaxes(east, 2, 3))
        + inputs(vmem, jnp.asarray(own_bands(cols), jnp.bfloat16))
        + inputs(smem, scales, widths, wind_x, wind_y, mixing),
        scratch=[pltpu.VMEM((rows, LANES), jnp.float32)],
    )
    drive, relax, row_relax, inside, weights, lane_weights, own_matrix = prepared[:7]
    payloads, side_drive, side_matrix = (
        prepared[7 + n * sides : 7 + (n + 1) * sides] for n in range(3)
    )

    sent = call(
        functools.partial(pack_x_kernel, grid_sizes),
        "pack_x",
        (f32((rows, LANES)),) * sides,
        inputs(vmem, first_round, second_round, *payloads),
        scratch=[pltpu.VMEM((count_f * count_l, 2 * PAD, LANES), jnp.float32)],
    )
    forward = [(i, i + 1) for i in range(gx_count - 1)]
    backward = [(b, a) for a, b in forward]
    if sides == 1:
        halos = [lax.ppermute(sent[0], "gx", forward + backward)]
    else:
        halos = [lax.ppermute(sent[0], "gx", forward), lax.ppermute(sent[1], "gx", backward)]

    state = pltpu.VMEM(state_shape, jnp.float32)
    after, *begun = call(
        functools.partial(begin_kernel, grid_sizes),
        "begin",
        (f32(fields.shape),)
        + (f32((ext_rows, LANES)),) * sides
        + (f32((3, wide_rows, LANES)),) * sides
        + (plane,) * sides,
        inputs(vmem, fields, first_round, second_round, drive, relax, weights, own_matrix)
        + inputs(vmem, row_relax, lane_weights, *payloads[::-1], *side_drive),
        scratch=[state] * 3 + [pltpu.VMEM((count_f, wide_rows, LANES), jnp.float32)],
        limit=8,
    )
    pair = pltpu.VMEM((2, ext_rows, LANES), jnp.float32)
    return call(
        functools.partial(finish_kernel, grid_sizes, sides),
        "finish",
        f32(fields.shape),
        inputs(vmem, *halos, *begun, *side_drive, *side_matrix)
        + inputs(vmem, after, row_relax, inside, lane_weights),
        scratch=[pltpu.VMEM((ext_rows, LANES), jnp.float32), pair, pair]
        + [pltpu.VMEM(fields.shape, jnp.float32), pltpu.SemaphoreType.DMA((count_f,))],
        out_space=pl.BlockSpec(memory_space=pl.ANY),
    )


def solution(mesh):
    return jax.shard_map(
        functools.partial(local, mesh.shape["gy"], mesh.shape["gx"]),
        mesh=mesh,
        in_specs=(
            P("mem", None, "gy", "gx"),
            P("mem"),
            P("mem"),
            P(),
            P("mem", None, None, None),
            P("mem", None, None, None),
            P("mem", None, None, None),
            P("mem", None, None, None),
            P("mem", None, None),
            P(),
        ),
        out_specs=P("mem", None, "gy", "gx"),
        check_vma=False,
    )
```
